256 devices in a mesh: gx: 16 (over z, core), gy: 16 (over x, y).
Axes of the slice: x: 4, y: 4, z: 8, core: 2. Of those that a mesh axis runs over, the one named last changes fastest.
Arguments:
- right_sides: float32 [16384, 8, 128], P(('gx', 'gy')), may hold values from -30 to 30
- diag_blocks: bfloat16 [16384, 128, 128], P(('gx', 'gy')), may hold values from -1 to 2
- face_blocks: bfloat16 [16384, 4, 128, 128], P(('gx', 'gy')), may hold values from -0.125 to 0.125
- neighbours: int32 [16384, 4], P(('gx', 'gy')), may hold values from -1 to 207, as said below
- send_slots: int32 [256, 9, 16], P(('gx', 'gy')), may hold values from -1 to 63, as said below
- counts: int32 [256], P(('gx', 'gy')), may hold values from 32 to 64, as said below
Outputs:
- solution: float32 [16384, 8, 128], P(('gx', 'gy'))
- residual: float32 [16384, 8, 128], P(('gx', 'gy'))
The draws below stay inside these ranges and needn't reach their ends.
Inputs may be any that keep to these rules, and one draw needn't show every extreme that they name: The first counts[g] slots of group g hold its elements; some group has exactly 64. send_slots[g, d, k] is a live slot of group g whose vector group g sends, as its k-th ghost of direction d = 3 (dx + 1) + (dy + 1), to the group at grid offset (dx, dy); -1 marks no block. A list's live entries come first and are distinct; direction 4 and directions leaving the grid hold only -1; some list holds 16 live entries. neighbours[e, f] is -1 (no coupling), a live slot of the same group, or 64 + d * 16 + k naming a live entry k of direction d of the sending group at offset -(dx, dy); slots at or beyond counts hold only -1.
All inputs are finite; a program needn't handle non-finite values.
Results may differ from the reference program's by a relative error of at most 0.0075.
The reference program's roundings to bfloat16 on the way (of `rounded`) count: a program that leaves them out, or rounds other values in their place, can miss the bound.
Values may be sent and summed in bfloat16 or wider, within the bound.
No kernel may reach another device: no remote copies, remote signals or barrier semaphores. Data moves between devices by JAX's collectives and lax.ppermute only.
A program may use at most 64 MiB of HBM per device.

```python
import math
import jax
import jax.numpy as jnp
from jax import lax

ELEM_ROWS = 128
NRHS = 8
POWERS = 4
FACES = 4
CAP = 64
SEND = 16
GRID_ROWS = 16
GRID_COLS = 16
GROUPS = 256
ELEMENTS = 16384
N_GY = 16


def mesh_tables(key):
    base = jax.random.fold_in(key, 7)
    key_count, key_pick, key_order, key_live, key_local, key_edge = jax.random.split(base, 6)
    groups = GRID_ROWS * GRID_COLS
    group_ids = jnp.arange(groups, dtype=jnp.int32)
    counts = jax.random.randint(key_count, (groups,), CAP // 2, CAP + 1)
    forced = jax.random.randint(key_pick, (), 0, groups)
    counts = jnp.where(group_ids == forced, CAP, counts).astype(jnp.int32)
    grid_row = group_ids // GRID_COLS
    grid_col = group_ids % GRID_COLS
    slot_ids = jnp.arange(CAP, dtype=jnp.int32)
    scores = jax.random.randint(key_order, (groups, 9, CAP), 0, 1 << 20) * CAP + slot_ids
    scores = jnp.where(slot_ids[None, None, :] < counts[:, None, None], scores, (1 << 20) * CAP + slot_ids)
    order = jnp.argsort(scores, axis=-1, stable=True)[:, :, :SEND].astype(jnp.int32)
    live_count = jax.random.randint(key_live, (groups, 9), SEND // 2, SEND + 1)
    full_group = GRID_COLS + 1
    direction_ids = jnp.arange(9, dtype=jnp.int32)
    live_count = jnp.where((group_ids[:, None] == full_group) & (direction_ids[None, :] == 8), SEND, live_count)
    target_row = grid_row[:, None] + direction_ids[None, :] // 3 - 1
    target_col = grid_col[:, None] + direction_ids[None, :] % 3 - 1
    target_ok = (target_row >= 0) & (target_row < GRID_ROWS) & (target_col >= 0) & (target_col < GRID_COLS) & (direction_ids[None, :] != 4)
    live_count = jnp.where(target_ok, live_count, 0).astype(jnp.int32)
    rank_ids = jnp.arange(SEND, dtype=jnp.int32)
    send_slots = jnp.where(rank_ids[None, None, :] < live_count[:, :, None], order, -1).astype(jnp.int32)
    half_cap = CAP // 2
    elem_ids = slot_ids[:, None]
    face_ids = jnp.arange(FACES, dtype=jnp.int32)[None, :]
    flat = face_ids * half_cap + elem_ids
    ghost_place = (elem_ids < half_cap) & (flat < 8 * SEND)
    flat_safe = jnp.minimum(flat, 8 * SEND - 1)
    eight_dir = flat_safe // SEND
    nine_dir = eight_dir + (eight_dir >= 4).astype(jnp.int32)
    rank_in = flat_safe % SEND
    sender_row = grid_row[:, None, None] - (nine_dir[None] // 3 - 1)
    sender_col = grid_col[:, None, None] - (nine_dir[None] % 3 - 1)
    sender_ok = (sender_row >= 0) & (sender_row < GRID_ROWS) & (sender_col >= 0) & (sender_col < GRID_COLS)
    sender = jnp.clip(sender_row * GRID_COLS + sender_col, 0, groups - 1)
    sender_live = live_count[sender, jnp.broadcast_to(nine_dir[None], sender.shape)]
    ghost_live = ghost_place[None] & sender_ok & (rank_in[None] < sender_live)
    ghost_value = CAP + nine_dir * SEND + rank_in
    offsets = jax.random.randint(key_local, (groups, CAP, FACES), 0, (counts - 1)[:, None, None])
    local_pick = (elem_ids[None] + 1 + offsets) % counts[:, None, None]
    edge_pick = jax.random.randint(key_edge, (groups, CAP, FACES), 0, 8) == 0
    neighbours = jnp.where(ghost_live, ghost_value[None], jnp.where(edge_pick, -1, local_pick))
    neighbours = jnp.where(elem_ids[None] < counts[:, None, None], neighbours, -1)
    return (counts, send_slots, neighbours.reshape(groups * CAP, FACES).astype(jnp.int32))


def draw_counts(key, part):
    return mesh_tables(key)[0]


def draw_send_slots(key, part):
    return mesh_tables(key)[1]


def draw_neighbours(key, part):
    return mesh_tables(key)[2]


def draw_right_sides(key, part):
    key_noise, key_scale = jax.random.split(jax.random.fold_in(key, 11), 2)
    groups = GRID_ROWS * GRID_COLS
    position = (jnp.arange(ELEMENTS) // CAP).astype(jnp.float32) / max(groups - 1, 1)
    ramp = jnp.exp(math.log(3.0) * position)
    scale = jnp.exp(jax.random.uniform(key_scale, (ELEMENTS, 1, 1), jnp.float32, math.log(0.25), math.log(2.5)))
    shape = (ELEMENTS, NRHS, ELEM_ROWS)
    noise = jnp.clip(jax.random.normal(key_noise, shape, jnp.float32), -4.0, 4.0)
    return noise * scale * ramp[:, None, None]


def draw_diag_blocks(key, part):
    key_noise = jax.random.fold_in(key, 23)
    sigma = 0.5 / math.sqrt(ELEM_ROWS)
    shape = (ELEMENTS, ELEM_ROWS, ELEM_ROWS)
    noise = jnp.clip(jax.random.normal(key_noise, shape, jnp.float32), -4.0, 4.0) * sigma
    return (0.7 * jnp.eye(ELEM_ROWS, dtype=jnp.float32)[None] + noise).astype(jnp.bfloat16)


def block_scale(stream_key, shape, cuts, low, top_value):
    loudness = 1.0
    for dim, parts in cuts:
        heights = jax.random.uniform(jax.random.fold_in(jax.random.fold_in(stream_key, 6), dim), (parts,), jnp.float32, low / len(cuts), top_value / len(cuts))
        loudness = loudness * jnp.repeat(jnp.exp(heights), shape[dim] // parts).reshape((-1,) + (1,) * (len(shape) - 1 - dim))
    return loudness


def gaussian(key, dims, scale, limit, cuts=(), kind=jnp.bfloat16):
    values = jax.random.normal(key, dims, jnp.float32) * scale
    if len(cuts) > 0:
        values = block_scale(key, dims, cuts, -0.22, 0.18) * values
    return jnp.clip(values, min=-limit, max=limit).astype(kind)


def setup_inputs(seed: int = 0) -> dict:
    arg_keys = jax.random.split(jax.random.key(seed), 7)
    return {
        "right_sides": draw_right_sides(jax.random.fold_in(arg_keys[6], 71), 0),
        "diag_blocks": draw_diag_blocks(jax.random.fold_in(arg_keys[6], 71), 0),
        "face_blocks": gaussian(arg_keys[2], (ELEMENTS, FACES, ELEM_ROWS, ELEM_ROWS), (4 * FACES * ELEM_ROWS) ** -0.5, 0.125, ((0, 256),)),
        "neighbours": draw_neighbours(jax.random.fold_in(arg_keys[6], 71), 0),
        "send_slots": draw_send_slots(jax.random.fold_in(arg_keys[6], 71), 0),
        "counts": draw_counts(jax.random.fold_in(arg_keys[6], 71), 0),
    }


HIGH = lax.Precision.HIGHEST

def forward_solve(factor, values):
    extent = factor.shape[-1]
    result = []
    for row_at in range(extent):
        running = values[:, row_at]
        for col_at in range(row_at):
            running = running - factor[:, row_at, col_at] * result[col_at]
        result.append(running / factor[:, row_at, row_at])
    return jnp.stack(result, axis=1)

def backward_solve(factor, values):
    extent = factor.shape[-1]
    result = [None] * extent
    for row_at in reversed(range(extent)):
        running = values[:, row_at]
        for col_at in range(row_at + 1, extent):
            running = running - factor[:, col_at, row_at] * result[col_at]
        result[row_at] = running / factor[:, row_at, row_at]
    return jnp.stack(result, axis=1)

def coefficients(gram):
    factor = jnp.linalg.cholesky(gram[:, 1:, 1:])
    return backward_solve(factor, forward_solve(factor, gram[:, 1:, 0]))

def apply_block(pieces):
    diag_piece, face_piece, own_piece, near_piece = pieces
    first = jnp.einsum('eij,erj->eri', diag_piece.astype(jnp.float32), own_piece.astype(jnp.float32), precision=HIGH)
    second = jnp.einsum('efij,efrj->eri', face_piece.astype(jnp.float32), near_piece.astype(jnp.float32), precision=HIGH)
    return first + second

def reference(right_sides, diag_blocks, face_blocks, neighbours, send_slots, counts):
    slot_ids = jnp.arange(ELEMENTS, dtype=jnp.int32)
    device = slot_ids // CAP
    live_mask = (slot_ids % CAP < counts[device]).astype(jnp.float32)[:, None, None]
    device_col = device[:, None]
    ghost = neighbours - CAP
    direction = jnp.clip(ghost // SEND, 0, 8).astype(jnp.int32)
    within = jnp.clip(ghost % SEND, 0, SEND - 1).astype(jnp.int32)
    sender_row = device_col // N_GY - (direction // 3 - 1)
    sender_col = device_col % N_GY - (direction % 3 - 1)
    sender = jnp.clip(sender_row * N_GY + sender_col, 0, GROUPS - 1).astype(jnp.int32)
    remote = sender * CAP + send_slots[sender, direction, within]
    source = jnp.where(neighbours < CAP, device_col * CAP + neighbours, remote)
    present = neighbours >= 0
    source = jnp.where(present, source, 0).astype(jnp.int32)

    def grouped(array):
        return array.reshape((GROUPS, CAP) + array.shape[1:])
    vectors = [right_sides * live_mask]
    for step_index in range(POWERS):
        rounded = vectors[-1].astype(jnp.bfloat16)
        gathered = jnp.where(present[:, :, None, None], rounded[source], jnp.zeros((), jnp.bfloat16))
        image = lax.map(apply_block, (grouped(diag_blocks), grouped(face_blocks), grouped(rounded), grouped(gathered)))
        vectors.append(image.reshape(right_sides.shape) * live_mask)
    basis = jnp.stack(vectors)
    gram = jnp.einsum('iern,jern->rij', basis, basis, precision=HIGH)
    weights = coefficients(gram)
    solution = jnp.einsum('rk,kern->ern', weights, basis[:POWERS], precision=HIGH)
    residual = basis[0] - jnp.einsum('rk,kern->ern', weights, basis[1:], precision=HIGH)
    return (solution, residual)
```

```python
import functools

import jax
import jax.numpy as jnp
from jax import lax
from jax.experimental import pallas as pl
from jax.experimental.pallas import tpu as pltpu
from jax.sharding import PartitionSpec as P

POWERS = 4
CAP = 64
SEND = 16
FACES = 4
SIDE = 16
LOOKUP = CAP + 9 * SEND
NOTHING = CAP + 4 * SEND
UNROLL = 16
META_SEND = FACES * CAP
META_COUNT = META_SEND + 9 * SEND
META_SIZE = 512

ROW_BY_ROW = (((1,), (1,)), ((), ()))
IN_VMEM = pl.BlockSpec(memory_space=pltpu.VMEM)
IN_SMEM = pl.BlockSpec(memory_space=pltpu.SMEM)
UP_DIRECTIONS = (2, 5, 8)
DOWN_DIRECTIONS = (0, 3, 6)


def pair_lane(first, second):
    return 5 * first + second


def vector_shape(count, dtype):
    return jax.ShapeDtypeStruct((count, 8, 128), dtype)


def params():
    return pltpu.CompilerParams(vmem_limit_bytes=16 << 20)


def pack(meta, rounded, up, down, next_row, last_row):
    for target, directions in (
        (up, UP_DIRECTIONS),
        (down, DOWN_DIRECTIONS),
        (next_row, (7,)),
        (last_row, (1,)),
    ):
        for at, direction in enumerate(directions):
            for k in range(SEND):
                slot = jnp.maximum(meta[META_SEND + direction * SEND + k], 0)
                target[at * SEND + k] = rounded[slot]


def start_kernel(meta, right_sides, basis, rounded, up, down, next_row, last_row):
    count = meta[META_COUNT]
    element = lax.broadcasted_iota(jnp.int32, basis.shape, 0)
    live = jnp.where(element < count, right_sides[...], 0.0)
    basis[...] = live
    rounded[...] = live.astype(jnp.bfloat16)
    pack(meta, rounded, up, down, next_row, last_row)


def relay_kernel(from_down, from_up, next_row, last_row, send_next, send_last):
    send_next[0:SEND] = from_up[2 * SEND : 3 * SEND]
    send_next[SEND : 2 * SEND] = next_row[...]
    send_next[2 * SEND : 3 * SEND] = from_down[2 * SEND : 3 * SEND]
    send_last[0:SEND] = from_up[0:SEND]
    send_last[SEND : 2 * SEND] = last_row[...]
    send_last[2 * SEND : 3 * SEND] = from_down[0:SEND]


def apply_kernel(power, *refs):
    meta, diag, face, rounded, from_down, from_up, from_last, from_next = refs[:8]
    basis = refs[8 : 9 + power]
    refs = refs[9 + power :]
    last = power == POWERS - 1
    gram_in = refs[0] if power else None
    refs = refs[1:] if power else refs
    if last:
        image, gram_out, lookup = refs
    else:
        image, image_rounded, up, down, next_row, last_row, gram_out, lookup = refs
    lookup[0:CAP] = rounded[...]
    lookup[CAP : CAP + 3 * SEND] = from_next[...]
    lookup[CAP + 3 * SEND : CAP + 4 * SEND] = from_up[SEND : 2 * SEND]
    lookup[NOTHING : NOTHING + SEND] = jnp.zeros((SEND, 8, 128), jnp.bfloat16)
    lookup[CAP + 5 * SEND : CAP + 6 * SEND] = from_down[SEND : 2 * SEND]
    lookup[CAP + 6 * SEND : CAP + 9 * SEND] = from_last[...]

    def element(e, sums):
        near = [rounded[e]]
        for f in range(FACES):
            at = meta[f * CAP + e]
            near.append(lookup[jnp.where(at < 0, NOTHING, at)])
        blocks = [diag[e]] + [face[e, f] for f in range(FACES)]
        out = lax.dot_general(
            jnp.concatenate(near, axis=1),
            jnp.concatenate(blocks, axis=1),
            ROW_BY_ROW,
            preferred_element_type=jnp.float32,
        )
        image[e] = out
        if not last:
            image_rounded[e] = out.astype(jnp.bfloat16)
        others = [ref[e] for ref in basis] + [out]
        return tuple(s + out * other for s, other in zip(sums, others))

    def several(step, sums):
        for u in range(UNROLL):
            sums = element(step * UNROLL + u, sums)
        return sums

    zero = jnp.zeros((8, 128), jnp.float32)
    sums = lax.fori_loop(0, CAP // UNROLL, several, (zero,) * (power + 2))
    if not last:
        pack(meta, image_rounded, up, down, next_row, last_row)
    lane = lax.broadcasted_iota(jnp.int32, (8, 128), 1)
    gram = gram_in[...] if power else zero
    for a, s in enumerate(sums):
        total = jnp.sum(s, axis=1, keepdims=True)
        gram = jnp.where(lane == pair_lane(a, power + 1), total, gram)
    gram_out[...] = gram


def finish_kernel(gram, b0, b1, b2, b3, b4, solution, residual):
    def entry(a, b):
        at = pair_lane(min(a, b), max(a, b))
        return jnp.broadcast_to(gram[:, at : at + 1], (8, 128))

    factor = {}
    for i in range(POWERS):
        for j in range(i + 1):
            value = entry(i + 1, j + 1)
            for k in range(j):
                value = value - factor[i, k] * factor[j, k]
            factor[i, j] = jnp.sqrt(value) if i == j else value / factor[j, j]
    forward = []
    for i in range(POWERS):
        value = entry(0, i + 1)
        for k in range(i):
            value = value - factor[i, k] * forward[k]
        forward.append(value / factor[i, i])
    weights = [None] * POWERS
    for i in reversed(range(POWERS)):
        value = forward[i]
        for k in range(i + 1, POWERS):
            value = value - factor[k, i] * weights[k]
        weights[i] = value / factor[i, i]
    basis = (b0, b1, b2, b3, b4)

    def several(step, carry):
        for u in range(8):
            e = step * 8 + u
            v = [ref[e] for ref in basis]
            total = weights[0] * v[0]
            moved = weights[0] * v[1]
            for k in range(1, POWERS):
                total = total + weights[k] * v[k]
                moved = moved + weights[k] * v[k + 1]
            solution[e] = total
            residual[e] = v[0] - moved
        return carry

    lax.fori_loop(0, CAP // 8, several, 0)


def shifted(block, axis, distance):
    return lax.ppermute(block, axis, [(i, (i + distance) % SIDE) for i in range(SIDE)])


def summed(block):
    for axis in ("gx", "gy"):
        for step in (1, 4):
            other = [
                lax.ppermute(block, axis, [(i, i ^ (k * step)) for i in range(SIDE)])
                for k in (1, 2, 3)
            ]
            block = (block + other[0]) + (other[1] + other[2])
    return block


def per_device(right_sides, diag_blocks, face_blocks, neighbours, send_slots, counts):
    meta = jnp.concatenate(
        [
            neighbours.T.reshape(-1),
            send_slots.reshape(-1),
            counts,
            jnp.zeros((META_SIZE - META_COUNT - 1,), jnp.int32),
        ]
    )
    diag_blocks = pltpu.with_memory_space_constraint(diag_blocks, pltpu.VMEM)
    face_blocks = pltpu.with_memory_space_constraint(face_blocks, pltpu.VMEM)
    half = jnp.bfloat16
    packets = [vector_shape(n * SEND, half) for n in (3, 3, 1, 1)]
    full = vector_shape(CAP, jnp.float32)
    gram_shape = jax.ShapeDtypeStruct((8, 128), jnp.float32)
    first, rounded, up, down, next_row, last_row = pl.pallas_call(
        start_kernel,
        name="start",
        in_specs=[IN_SMEM, IN_VMEM],
        out_specs=[IN_VMEM] * 6,
        out_shape=[full, vector_shape(CAP, half)] + packets,
        compiler_params=params(),
    )(meta, right_sides)
    basis = [first]
    gram = []
    for power in range(POWERS):
        last = power == POWERS - 1
        from_down = shifted(up, "gy", 1)
        from_up = shifted(down, "gy", -1)
        send_next, send_last = pl.pallas_call(
            relay_kernel,
            name="relay",
            in_specs=[IN_VMEM] * 4,
            out_specs=[IN_VMEM] * 2,
            out_shape=[vector_shape(3 * SEND, half)] * 2,
            compiler_params=params(),
        )(from_down, from_up, next_row, last_row)
        from_last = shifted(send_next, "gx", 1)
        from_next = shifted(send_last, "gx", -1)
        shapes = [full] if last else [full, vector_shape(CAP, half)] + packets
        shapes = shapes + [gram_shape]
        outs = pl.pallas_call(
            functools.partial(apply_kernel, power),
            name=f"apply{power}",
            in_specs=[IN_SMEM] + [IN_VMEM] * (8 + power + len(gram)),
            out_specs=[IN_VMEM] * len(shapes),
            out_shape=shapes,
            scratch_shapes=[pltpu.VMEM((LOOKUP, 8, 128), half)],
            compiler_params=params(),
        )(
            meta, diag_blocks, face_blocks, rounded, from_down, from_up, from_last,
            from_next, *basis, *gram,
        )
        basis.append(outs[0])
        gram = [outs[-1]]
        if not last:
            rounded, up, down, next_row, last_row = outs[1:-1]
    total = summed(gram[0])
    return pl.pallas_call(
        finish_kernel,
        name="finish",
        in_specs=[IN_VMEM] * 6,
        out_specs=[IN_VMEM] * 2,
        out_shape=[full] * 2,
        compiler_params=params(),
    )(total, *basis)


def solution(mesh):
    in_specs = (
        P(("gx", "gy"), None, None),
        P(("gx", "gy"), None, None),
        P(("gx", "gy"), None, None, None),
        P(("gx", "gy"), None),
        P(("gx", "gy"), None, None),
        P(("gx", "gy")),
    )
    out_specs = (P(("gx", "gy"), None, None), P(("gx", "gy"), None, None))
    return jax.shard_map(
        per_device, mesh=mesh, in_specs=in_specs, out_specs=out_specs, check_vma=False
    )
```

```python
import functools

import jax
import jax.numpy as jnp
from jax import lax
from jax.experimental import pallas as pl
from jax.experimental.pallas import tpu as pltpu
from jax.sharding import PartitionSpec as P

POWERS = 4
CAP = 64
SEND = 16
FACES = 4
SIDE = 16
GROUPS = SIDE * SIDE
ROWS = 128
LOOKUP = CAP + 9 * SEND
NOTHING = CAP + 4 * SEND
UNROLL = 16
BLOCKS = FACES + 1
CHUNK = 8
HALF_CAP = CAP // 2
CHUNKS = HALF_CAP // CHUNK

IN_VMEM = pl.BlockSpec(memory_space=pltpu.VMEM)
IN_SMEM = pl.BlockSpec(memory_space=pltpu.SMEM)
ANYWHERE = pl.BlockSpec(memory_space=pl.ANY)
IN_HBM = pl.BlockSpec(memory_space=pltpu.HBM)
UP_DIRECTIONS = (2, 5, 8)
DOWN_DIRECTIONS = (0, 3, 6)
PAIRS = [(a, b) for a in range(5) for b in range(a, 5) if b > 0]
PAIR_LANE = {pair: at for at, pair in enumerate(PAIRS)}
LANES_PER_SIDE = 16


def vector_shape(count, dtype):
    return jax.ShapeDtypeStruct((count, 8, ROWS), dtype)


def params(mebibytes=16):
    return pltpu.CompilerParams(vmem_limit_bytes=mebibytes << 20)


def pack(send_slots, rounded, up, down, next_row, last_row):
    for target, directions in (
        (up, UP_DIRECTIONS),
        (down, DOWN_DIRECTIONS),
        (next_row, (7,)),
        (last_row, (1,)),
    ):
        for at, direction in enumerate(directions):
            for k in range(SEND):
                slot = jnp.maximum(send_slots[direction, 0, k], 0)
                target[at * SEND + k] = rounded[slot]


def start_kernel(
    send_slots, counts, right_sides, basis, rounded, up, down, next_row, last_row
):
    element = lax.broadcasted_iota(jnp.int32, basis.shape, 0)
    live = jnp.where(element < counts[0], right_sides[...], 0.0)
    basis[...] = live
    rounded[...] = live.astype(jnp.bfloat16)
    pack(send_slots, rounded, up, down, next_row, last_row)


def make_plan(neighbours, order):
    local = jnp.int32(0)
    for e in range(CAP):
        farthest = neighbours[0, e]
        for f in range(1, FACES):
            farthest = jnp.maximum(farthest, neighbours[f, e])
        ghost = farthest >= CAP
        order[jnp.where(ghost, CAP - 1 - (e - local), local)] = e
        local = local + jnp.where(ghost, 0, 1)
    order[CAP] = local // UNROLL


def transpose_blocks(base, diag, face, turned, diag_here, face_here, arrived, extra):
    def fetch(c):
        here = pl.ds(c * CHUNK, CHUNK)
        there = pl.ds(base + c * CHUNK, CHUNK)
        return (
            pltpu.make_async_copy(diag.at[there], diag_here.at[here], arrived.at[c, 0]),
            pltpu.make_async_copy(face.at[there], face_here.at[here], arrived.at[c, 1]),
        )

    for c in range(CHUNKS):
        for copy in fetch(c):
            copy.start()
    extra()
    for c in range(CHUNKS):
        for copy in fetch(c):
            copy.wait()

        def element(at, carry, c=c):
            e = c * CHUNK + at
            turned[base + e, 0:ROWS] = diag_here[e].T
            for f in range(FACES):
                turned[base + e, (f + 1) * ROWS : (f + 2) * ROWS] = face_here[e, f].T
            return carry

        lax.fori_loop(0, CHUNK, element, 0, unroll=4)


def first_half_kernel(
    neighbours, diag, face, turned, order, diag_here, face_here, arrived
):
    transpose_blocks(
        0, diag, face, turned, diag_here, face_here, arrived,
        lambda: make_plan(neighbours, order),
    )


def second_half_kernel(diag, face, before, turned, diag_here, face_here, arrived):
    transpose_blocks(
        HALF_CAP, diag, face, turned, diag_here, face_here, arrived, lambda: None
    )


def relay_kernel(*refs):
    from_down, from_up, next_row, last_row = refs[:4]
    send_next, send_last = refs[-2:]
    send_next[0:SEND] = from_up[2 * SEND : 3 * SEND]
    send_next[SEND : 2 * SEND] = next_row[...]
    send_next[2 * SEND : 3 * SEND] = from_down[2 * SEND : 3 * SEND]
    send_last[0:SEND] = from_up[0:SEND]
    send_last[SEND : 2 * SEND] = last_row[...]
    send_last[2 * SEND : 3 * SEND] = from_down[0:SEND]


def fill_local(lookup, rounded):
    lookup[0:CAP] = rounded[...]
    lookup[NOTHING : NOTHING + SEND] = jnp.zeros((SEND, 8, ROWS), jnp.bfloat16)


def fill_ghosts(lookup, from_down, from_up, from_last, from_next):
    lookup[CAP : CAP + 3 * SEND] = from_next[...]
    lookup[CAP + 3 * SEND : CAP + 4 * SEND] = from_up[SEND : 2 * SEND]
    lookup[CAP + 5 * SEND : CAP + 6 * SEND] = from_down[SEND : 2 * SEND]
    lookup[CAP + 6 * SEND : CAP + 9 * SEND] = from_last[...]


def apply_runs(
    first, limit, order, neighbours, turned, lookup, basis, image, image_rounded
):
    def element(e, sums):
        near = [lookup[e]]
        for f in range(FACES):
            at = neighbours[f, e]
            near.append(lookup[jnp.where(at < 0, NOTHING, at)])
        out = jnp.dot(
            jnp.concatenate(near, axis=1),
            turned[e],
            preferred_element_type=jnp.float32,
        )
        image[e] = out
        if image_rounded is not None:
            image_rounded[e] = out.astype(jnp.bfloat16)
        others = [ref[e] for ref in basis] + [out]
        return tuple(s + out * other for s, other in zip(sums, others))

    def run(step, sums):
        for u in range(UNROLL):
            at = step * UNROLL + u
            sums = element(at if order is None else order[at], sums)
        return sums

    zero = jnp.zeros((8, ROWS), jnp.float32)
    return lax.fori_loop(first, limit, run, (zero,) * (len(basis) + 1))


def with_sums(gram, sums):
    lane = lax.broadcasted_iota(jnp.int32, (8, ROWS), 1)
    newest = len(sums) - 1
    for a, s in enumerate(sums):
        total = jnp.sum(s, axis=1, keepdims=True)
        gram = gram + jnp.where(lane == PAIR_LANE[a, newest], total, 0.0)
    return gram


def whole_kernel(
    neighbours, send_slots, turned, rounded, from_down, from_up, from_last, from_next,
    b0, image, image_rounded, up, down, next_row, last_row, gram_out, lookup,
):
    fill_local(lookup, rounded)
    fill_ghosts(lookup, from_down, from_up, from_last, from_next)
    sums = apply_runs(
        0, CAP // UNROLL, None, neighbours, turned, lookup, (b0,), image, image_rounded
    )
    pack(send_slots, image_rounded, up, down, next_row, last_row)
    gram_out[...] = with_sums(jnp.zeros((8, ROWS), jnp.float32), sums)


def local_kernel(power, *refs):
    neighbours, order, turned, rounded, gram_in = refs[:5]
    basis = refs[5 : 6 + power]
    image, image_rounded, gram_out, lookup = refs[6 + power :]
    fill_local(lookup, rounded)
    sums = apply_runs(
        0, order[CAP], order, neighbours, turned, lookup, basis, image, image_rounded
    )
    gram_out[...] = with_sums(gram_in[...], sums)


def ghost_kernel(power, *refs):
    neighbours, order, send_slots, turned, rounded = refs[:5]
    received = refs[5:9]
    gram_in = refs[9]
    basis = refs[10 : 11 + power]
    refs = refs[13 + power :]
    last = power == POWERS - 1
    if last:
        image, image_rounded, gram_out, lookup = refs
    else:
        image, image_rounded, up, down, next_row, last_row, gram_out, lookup = refs
    fill_local(lookup, rounded)
    fill_ghosts(lookup, *received)
    sums = apply_runs(
        order[CAP], CAP // UNROLL, order, neighbours, turned, lookup, basis, image,
        image_rounded,
    )
    if not last:
        pack(send_slots, image_rounded, up, down, next_row, last_row)
    gram = with_sums(gram_in[...], sums)
    if last:
        lane = lax.broadcasted_iota(jnp.int32, (8, ROWS), 1)
        side = lax.broadcasted_iota(jnp.int32, (8, ROWS), 0)
        spread = jnp.zeros((8, ROWS), jnp.float32)
        for at in range(len(PAIRS)):
            value = jnp.broadcast_to(gram[:, at : at + 1], (8, ROWS))
            spread = jnp.where(lane == side * LANES_PER_SIDE + at, value, spread)
        row = jnp.sum(spread, axis=0, keepdims=True)
        gram_out[...] = jnp.broadcast_to(row, gram_out.shape)
    else:
        gram_out[...] = gram


def finish_kernel(gram_rows, b0, b1, b2, b3, b4, solution, residual):
    lane = lax.broadcasted_iota(jnp.int32, (8, ROWS), 1)
    side = lax.broadcasted_iota(jnp.int32, (8, ROWS), 0)
    row = jnp.sum(gram_rows[...], axis=0, keepdims=True)
    spread = jnp.broadcast_to(row, (8, ROWS))

    def entry(a, b):
        at = PAIR_LANE[min(a, b), max(a, b)]
        mine = jnp.where(lane == side * LANES_PER_SIDE + at, spread, 0.0)
        total = jnp.sum(mine, axis=1, keepdims=True)
        return jnp.broadcast_to(total, (8, ROWS))

    factor = {}
    for i in range(POWERS):
        for j in range(i + 1):
            value = entry(i + 1, j + 1)
            for k in range(j):
                value = value - factor[i, k] * factor[j, k]
            factor[i, j] = jnp.sqrt(value) if i == j else value / factor[j, j]
    forward = []
    for i in range(POWERS):
        value = entry(0, i + 1)
        for k in range(i):
            value = value - factor[i, k] * forward[k]
        forward.append(value / factor[i, i])
    weights = [None] * POWERS
    for i in reversed(range(POWERS)):
        value = forward[i]
        for k in range(i + 1, POWERS):
            value = value - factor[k, i] * weights[k]
        weights[i] = value / factor[i, i]
    basis = (b0, b1, b2, b3, b4)

    def several(step, carry):
        for u in range(8):
            e = step * 8 + u
            v = [ref[e] for ref in basis]
            total = weights[0] * v[0]
            moved = weights[0] * v[1]
            for k in range(1, POWERS):
                total = total + weights[k] * v[k]
                moved = moved + weights[k] * v[k + 1]
            solution[e] = total
            residual[e] = v[0] - moved
        return carry

    lax.fori_loop(0, CAP // 8, several, 0)


def shifted(block, axis, distance):
    return lax.ppermute(block, axis, [(i, (i + distance) % SIDE) for i in range(SIDE)])


def per_device(right_sides, diag_blocks, face_blocks, neighbours, send_slots, counts):
    half = jnp.bfloat16
    neighbours = neighbours.T
    send_slots = send_slots.transpose(1, 0, 2)
    in_place = lambda array: pltpu.with_memory_space_constraint(array, pltpu.HBM)
    diag_blocks = in_place(diag_blocks)
    face_blocks = in_place(face_blocks)
    packets = [vector_shape(n * SEND, half) for n in (3, 3, 1, 1)]
    full = vector_shape(CAP, jnp.float32)
    narrow = vector_shape(CAP, half)
    gram_shape = jax.ShapeDtypeStruct((8, ROWS), jnp.float32)
    rows_shape = jax.ShapeDtypeStruct((GROUPS, ROWS), jnp.float32)
    turned_shape = pltpu.VMEM((CAP, BLOCKS * ROWS, ROWS), half)
    lookup = pltpu.VMEM((LOOKUP, 8, ROWS), half)
    landing = [
        pltpu.VMEM((HALF_CAP, ROWS, ROWS), half),
        pltpu.VMEM((HALF_CAP, FACES, ROWS, ROWS), half),
        pltpu.SemaphoreType.DMA((CHUNKS, 2)),
    ]
    first, rounded, up, down, next_row, last_row = pl.pallas_call(
        start_kernel,
        name="start",
        in_specs=[IN_SMEM, IN_SMEM, IN_VMEM],
        out_specs=[IN_VMEM] * 6,
        out_shape=[full, narrow] + packets,
        compiler_params=params(),
    )(in_place(send_slots), counts, in_place(right_sides))
    basis = [first]
    gram = None
    for power in range(POWERS):
        last = power == POWERS - 1
        from_down = shifted(up, "gy", 1)
        from_up = shifted(down, "gy", -1)
        if power == 0:
            turned, order = pl.pallas_call(
                first_half_kernel,
                name="first_half",
                in_specs=[IN_SMEM, IN_HBM, IN_HBM],
                out_specs=[IN_VMEM, IN_SMEM],
                out_shape=[turned_shape, jax.ShapeDtypeStruct((128,), jnp.int32)],
                scratch_shapes=landing,
                compiler_params=params(),
            )(neighbours, diag_blocks, face_blocks)
            after = (order,)
        else:
            after = ()
            image, image_rounded, gram = pl.pallas_call(
                functools.partial(local_kernel, power),
                name=f"local{power}",
                in_specs=[IN_SMEM] * 2 + [IN_VMEM] * (4 + power),
                out_specs=[IN_VMEM] * 3,
                out_shape=[full, narrow, gram_shape],
                scratch_shapes=[lookup],
                compiler_params=params(),
            )(neighbours, order, turned, rounded, gram, *basis)
        send_next, send_last = pl.pallas_call(
            relay_kernel,
            name="relay",
            in_specs=[IN_VMEM] * 4 + [ANYWHERE] * len(after),
            out_specs=[IN_VMEM] * 2,
            out_shape=[vector_shape(3 * SEND, half)] * 2,
            compiler_params=params(),
        )(from_down, from_up, next_row, last_row, *after)
        from_last = shifted(send_next, "gx", 1)
        from_next = shifted(send_last, "gx", -1)
        received = (from_down, from_up, from_last, from_next)
        if power == 0:
            turned = pl.pallas_call(
                second_half_kernel,
                name="second_half",
                in_specs=[IN_HBM, IN_HBM, IN_VMEM],
                out_specs=IN_VMEM,
                out_shape=turned_shape,
                scratch_shapes=landing,
                input_output_aliases={2: 0},
                compiler_params=params(),
            )(diag_blocks, face_blocks, turned)
            outs = pl.pallas_call(
                whole_kernel,
                name="whole",
                in_specs=[IN_SMEM] * 2 + [IN_VMEM] * 7,
                out_specs=[IN_VMEM] * 7,
                out_shape=[full, narrow] + packets + [gram_shape],
                scratch_shapes=[lookup],
                compiler_params=params(),
            )(neighbours, send_slots, turned, rounded, *received, first)
        else:
            shapes = [full, narrow] + ([rows_shape] if last else packets + [gram_shape])
            outs = pl.pallas_call(
                functools.partial(ghost_kernel, power),
                name=f"ghost{power}",
                in_specs=[IN_SMEM] * 3 + [IN_VMEM] * (10 + power),
                out_specs=[IN_VMEM] * len(shapes),
                out_shape=shapes,
                scratch_shapes=[lookup],
                input_output_aliases={11 + power: 0, 12 + power: 1},
                compiler_params=params(),
            )(
                neighbours, order, send_slots, turned, rounded, *received, gram, *basis,
                image, image_rounded,
            )
        basis.append(outs[0])
        rounded = outs[1]
        gram = outs[-1]
        if not last:
            up, down, next_row, last_row = outs[2:-1]
    gathered = lax.all_to_all(gram, ("gx", "gy"), 0, 0, tiled=True)
    return pl.pallas_call(
        finish_kernel,
        name="finish",
        in_specs=[IN_VMEM] * 6,
        out_specs=[IN_VMEM] * 2,
        out_shape=[full] * 2,
        compiler_params=params(),
    )(gathered, *basis)


def solution(mesh):
    in_specs = (
        P(("gx", "gy"), None, None),
        P(("gx", "gy"), None, None),
        P(("gx", "gy"), None, None, None),
        P(("gx", "gy"), None),
        P(("gx", "gy"), None, None),
        P(("gx", "gy")),
    )
    out_specs = (P(("gx", "gy"), None, None), P(("gx", "gy"), None, None))
    return jax.shard_map(
        per_device, mesh=mesh, in_specs=in_specs, out_specs=out_specs, check_vma=False
    )
```

```python
import functools

import jax
import jax.numpy as jnp
from jax import lax
from jax.experimental import pallas as pl
from jax.experimental.pallas import tpu as pltpu
from jax.sharding import PartitionSpec as P

POWERS = 4
CAP = 64
SEND = 16
FACES = 4
SIDE = 16
GROUPS = SIDE * SIDE
ROWS = 128
LOOKUP = CAP + 9 * SEND
NOTHING = CAP + 4 * SEND
UNROLL = 16
BLOCKS = FACES + 1
CHUNK = 8
HALF_CAP = CAP // 2
CHUNKS = HALF_CAP // CHUNK

IN_VMEM = pl.BlockSpec(memory_space=pltpu.VMEM)
IN_SMEM = pl.BlockSpec(memory_space=pltpu.SMEM)
ANYWHERE = pl.BlockSpec(memory_space=pl.ANY)
IN_HBM = pl.BlockSpec(memory_space=pltpu.HBM)
UP_DIRECTIONS = (2, 5, 8)
DOWN_DIRECTIONS = (0, 3, 6)
LOCAL_RUNS = CAP
PLACES = 2 * CAP
SLOTS = PLACES + FACES * CAP
TABLE = SLOTS + 2 * CAP + 2 * SEND
PAIRS = [(a, b) for a in range(5) for b in range(a, 5) if b > 0]
PAIR_LANE = {pair: at for at, pair in enumerate(PAIRS)}
LANES_PER_SIDE = 16


def vector_shape(count, dtype):
    return jax.ShapeDtypeStruct((count, 8, ROWS), dtype)


def params(mebibytes=16):
    return pltpu.CompilerParams(vmem_limit_bytes=mebibytes << 20)


def pack(slot_of, rounded, up, down, next_row, last_row):
    for target, directions in (
        (up, UP_DIRECTIONS),
        (down, DOWN_DIRECTIONS),
        (next_row, (7,)),
        (last_row, (1,)),
    ):
        for at, direction in enumerate(directions):
            for k in range(SEND):
                target[at * SEND + k] = rounded[slot_of(direction, k)]


def listed(send_slots):
    return lambda direction, k: jnp.maximum(send_slots[direction, 0, k], 0)


def planned(table):
    return lambda direction, k: table[SLOTS + direction * SEND + k]


def start_kernel(
    send_slots, counts, right_sides, basis, rounded, up, down, next_row, last_row
):
    element = lax.broadcasted_iota(jnp.int32, basis.shape, 0)
    live = jnp.where(element < counts[0], right_sides[...], 0.0)
    basis[...] = live
    rounded[...] = live.astype(jnp.bfloat16)
    pack(listed(send_slots), rounded, up, down, next_row, last_row)


def plan_kernel(neighbours, send_slots, table, done):
    local = jnp.int32(0)
    for e in range(CAP):
        at = [neighbours[f, e] for f in range(FACES)]
        farthest = jnp.maximum(jnp.maximum(at[0], at[1]), jnp.maximum(at[2], at[3]))
        ghost = farthest >= CAP
        place = jnp.where(ghost, CAP - 1 - (e - local), local)
        table[place] = e
        for f in range(FACES):
            table[PLACES + f * CAP + place] = jnp.where(at[f] < 0, NOTHING, at[f])
        local = local + jnp.where(ghost, 0, 1)
    table[LOCAL_RUNS] = local // UNROLL
    for direction in range(9):
        for k in range(SEND):
            slot = listed(send_slots)(direction, k)
            table[SLOTS + direction * SEND + k] = slot
    done[...] = jnp.zeros_like(done)


def transpose_blocks(base, diag, face, turned, diag_here, face_here, arrived):
    def fetch(c):
        here = pl.ds(c * CHUNK, CHUNK)
        there = pl.ds(base + c * CHUNK, CHUNK)
        return (
            pltpu.make_async_copy(diag.at[there], diag_here.at[here], arrived.at[c, 0]),
            pltpu.make_async_copy(face.at[there], face_here.at[here], arrived.at[c, 1]),
        )

    for c in range(CHUNKS):
        for copy in fetch(c):
            copy.start()
    for c in range(CHUNKS):
        for copy in fetch(c):
            copy.wait()

        def element(at, carry, c=c):
            e = c * CHUNK + at
            turned[base + e, 0:ROWS] = diag_here[e].T
            for f in range(FACES):
                turned[base + e, (f + 1) * ROWS : (f + 2) * ROWS] = face_here[e, f].T
            return carry

        lax.fori_loop(0, CHUNK, element, 0, unroll=4)


def first_half_kernel(diag, face, turned, done, diag_here, face_here, arrived):
    transpose_blocks(0, diag, face, turned, diag_here, face_here, arrived)
    done[...] = jnp.zeros_like(done)


def second_half_kernel(diag, face, before, turned, diag_here, face_here, arrived):
    transpose_blocks(HALF_CAP, diag, face, turned, diag_here, face_here, arrived)


def relay_kernel(*refs):
    from_down, from_up, next_row, last_row = refs[:4]
    send_next, send_last = refs[-2:]
    send_next[0:SEND] = from_up[2 * SEND : 3 * SEND]
    send_next[SEND : 2 * SEND] = next_row[...]
    send_next[2 * SEND : 3 * SEND] = from_down[2 * SEND : 3 * SEND]
    send_last[0:SEND] = from_up[0:SEND]
    send_last[SEND : 2 * SEND] = last_row[...]
    send_last[2 * SEND : 3 * SEND] = from_down[0:SEND]


def fill_local(lookup, rounded):
    lookup[0:CAP] = rounded[...]
    lookup[NOTHING : NOTHING + SEND] = jnp.zeros((SEND, 8, ROWS), jnp.bfloat16)


def fill_ghosts(lookup, from_down, from_up, from_last, from_next):
    lookup[CAP : CAP + 3 * SEND] = from_next[...]
    lookup[CAP + 3 * SEND : CAP + 4 * SEND] = from_up[SEND : 2 * SEND]
    lookup[CAP + 5 * SEND : CAP + 6 * SEND] = from_down[SEND : 2 * SEND]
    lookup[CAP + 6 * SEND : CAP + 9 * SEND] = from_last[...]


def apply_runs(first, limit, find, turned, lookup, basis, image, image_rounded):
    def near(found):
        vectors = jnp.concatenate([lookup[at] for at in found], axis=1)
        return vectors.astype(jnp.float32)

    def two(found, sums):
        elements = [places[0] for places in found]
        both = jnp.dot(
            jnp.concatenate([near(f) for f in found], axis=0).astype(jnp.bfloat16),
            jnp.concatenate([turned[e] for e in elements], axis=1),
            preferred_element_type=jnp.float32,
        )
        for at, e in enumerate(elements):
            out = both[8 * at : 8 * at + 8, ROWS * at : ROWS * at + ROWS]
            image[e] = out
            image_rounded[e] = out.astype(jnp.bfloat16)
            others = [ref[e] for ref in basis] + [out]
            sums = tuple(s + out * other for s, other in zip(sums, others))
        return sums

    def run(step, sums):
        for u in range(0, UNROLL, 2):
            at = step * UNROLL + u
            sums = two([find(at), find(at + 1)], sums)
        return sums

    zero = jnp.zeros((8, ROWS), jnp.float32)
    return lax.fori_loop(first, limit, run, (zero,) * (len(basis) + 1))


def with_sums(gram, sums):
    lane = lax.broadcasted_iota(jnp.int32, (8, ROWS), 1)
    newest = len(sums) - 1
    for a, s in enumerate(sums):
        total = jnp.sum(s, axis=1, keepdims=True)
        gram = gram + jnp.where(lane == PAIR_LANE[a, newest], total, 0.0)
    return gram


def whole_kernel(
    neighbours, send_slots, turned, rounded, from_down, from_up, from_last, from_next,
    b0, image, image_rounded, up, down, next_row, last_row, gram_out, lookup,
):
    fill_local(lookup, rounded)
    fill_ghosts(lookup, from_down, from_up, from_last, from_next)

    def find(e):
        at = [neighbours[f, e] for f in range(FACES)]
        return [e] + [jnp.where(a < 0, NOTHING, a) for a in at]

    sums = apply_runs(
        0, CAP // UNROLL, find, turned, lookup, (b0,), image, image_rounded
    )
    pack(listed(send_slots), image_rounded, up, down, next_row, last_row)
    gram_out[...] = with_sums(jnp.zeros((8, ROWS), jnp.float32), sums)


def find_in(table):
    return lambda at: [table[at]] + [table[PLACES + f * CAP + at] for f in range(FACES)]


def local_kernel(power, *refs):
    table, turned, rounded, gram_in = refs[:4]
    basis = refs[4 : 5 + power]
    image, image_rounded, gram_out, lookup = refs[5 + power :]
    fill_local(lookup, rounded)
    sums = apply_runs(
        0, table[LOCAL_RUNS], find_in(table), turned, lookup, basis, image, image_rounded
    )
    gram_out[...] = with_sums(gram_in[...], sums)


def ghost_kernel(power, *refs):
    table, turned, rounded = refs[:3]
    received = refs[3:7]
    gram_in = refs[7]
    basis = refs[8 : 9 + power]
    refs = refs[11 + power :]
    last = power == POWERS - 1
    if last:
        image, image_rounded, gram_out, lookup = refs
    else:
        image, image_rounded, up, down, next_row, last_row, gram_out, lookup = refs
    fill_local(lookup, rounded)
    fill_ghosts(lookup, *received)
    sums = apply_runs(
        table[LOCAL_RUNS], CAP // UNROLL, find_in(table), turned, lookup, basis, image,
        image_rounded,
    )
    if not last:
        pack(planned(table), image_rounded, up, down, next_row, last_row)
    gram = with_sums(gram_in[...], sums)
    if last:
        lane = lax.broadcasted_iota(jnp.int32, (8, ROWS), 1)
        side = lax.broadcasted_iota(jnp.int32, (8, ROWS), 0)
        spread = jnp.zeros((8, ROWS), jnp.float32)
        for at in range(len(PAIRS)):
            value = jnp.broadcast_to(gram[:, at : at + 1], (8, ROWS))
            spread = jnp.where(lane == side * LANES_PER_SIDE + at, value, spread)
        row = jnp.sum(spread, axis=0, keepdims=True)
        gram_out[...] = jnp.broadcast_to(row, gram_out.shape)
    else:
        gram_out[...] = gram


def finish_kernel(gram_rows, b0, b1, b2, b3, b4, solution, residual):
    lane = lax.broadcasted_iota(jnp.int32, (8, ROWS), 1)
    side = lax.broadcasted_iota(jnp.int32, (8, ROWS), 0)
    row = jnp.sum(gram_rows[...], axis=0, keepdims=True)
    spread = jnp.broadcast_to(row, (8, ROWS))

    def entry(a, b):
        at = PAIR_LANE[min(a, b), max(a, b)]
        mine = jnp.where(lane == side * LANES_PER_SIDE + at, spread, 0.0)
        total = jnp.sum(mine, axis=1, keepdims=True)
        return jnp.broadcast_to(total, (8, ROWS))

    factor = {}
    for i in range(POWERS):
        for j in range(i + 1):
            value = entry(i + 1, j + 1)
            for k in range(j):
                value = value - factor[i, k] * factor[j, k]
            factor[i, j] = jnp.sqrt(value) if i == j else value / factor[j, j]
    forward = []
    for i in range(POWERS):
        value = entry(0, i + 1)
        for k in range(i):
            value = value - factor[i, k] * forward[k]
        forward.append(value / factor[i, i])
    weights = [None] * POWERS
    for i in reversed(range(POWERS)):
        value = forward[i]
        for k in range(i + 1, POWERS):
            value = value - factor[k, i] * weights[k]
        weights[i] = value / factor[i, i]
    basis = (b0, b1, b2, b3, b4)

    def several(step, carry):
        for u in range(8):
            e = step * 8 + u
            v = [ref[e] for ref in basis]
            total = weights[0] * v[0]
            moved = weights[0] * v[1]
            for k in range(1, POWERS):
                total = total + weights[k] * v[k]
                moved = moved + weights[k] * v[k + 1]
            solution[e] = total
            residual[e] = v[0] - moved
        return carry

    lax.fori_loop(0, CAP // 8, several, 0)


def shifted(block, axis, distance):
    return lax.ppermute(block, axis, [(i, (i + distance) % SIDE) for i in range(SIDE)])


def per_device(right_sides, diag_blocks, face_blocks, neighbours, send_slots, counts):
    half = jnp.bfloat16
    neighbours = neighbours.T
    send_slots = send_slots.transpose(1, 0, 2)
    in_place = lambda array: pltpu.with_memory_space_constraint(array, pltpu.HBM)
    diag_blocks = in_place(diag_blocks)
    face_blocks = in_place(face_blocks)
    packets = [vector_shape(n * SEND, half) for n in (3, 3, 1, 1)]
    full = vector_shape(CAP, jnp.float32)
    narrow = vector_shape(CAP, half)
    gram_shape = jax.ShapeDtypeStruct((8, ROWS), jnp.float32)
    rows_shape = jax.ShapeDtypeStruct((GROUPS, ROWS), jnp.float32)
    turned_shape = pltpu.VMEM((CAP, BLOCKS * ROWS, ROWS), half)
    lookup = pltpu.VMEM((LOOKUP, 8, ROWS), half)
    landing = [
        pltpu.VMEM((HALF_CAP, ROWS, ROWS), half),
        pltpu.VMEM((HALF_CAP, FACES, ROWS, ROWS), half),
        pltpu.SemaphoreType.DMA((CHUNKS, 2)),
    ]
    first, rounded, up, down, next_row, last_row = pl.pallas_call(
        start_kernel,
        name="start",
        in_specs=[IN_SMEM, IN_SMEM, IN_VMEM],
        out_specs=[IN_VMEM] * 6,
        out_shape=[full, narrow] + packets,
        compiler_params=params(),
    )(in_place(send_slots), counts, in_place(right_sides))
    basis = [first]
    gram = None
    for power in range(POWERS):
        last = power == POWERS - 1
        from_down = shifted(up, "gy", 1)
        from_up = shifted(down, "gy", -1)
        after = ()
        if power == 0:
            turned, done = pl.pallas_call(
                first_half_kernel,
                name="first_half",
                in_specs=[IN_HBM] * 2,
                out_specs=[IN_VMEM] * 2,
                out_shape=[turned_shape, gram_shape],
                scratch_shapes=landing,
                compiler_params=params(),
            )(diag_blocks, face_blocks)
            after = (done,)
        elif power == 1:
            table, done = pl.pallas_call(
                plan_kernel,
                name="plan",
                in_specs=[IN_SMEM] * 2,
                out_specs=[IN_SMEM, IN_VMEM],
                out_shape=[pltpu.SMEM((TABLE,), jnp.int32), gram_shape],
                compiler_params=params(),
            )(neighbours, send_slots)
            after = (done,)
        if power > 0:
            image, image_rounded, gram = pl.pallas_call(
                functools.partial(local_kernel, power),
                name=f"local{power}",
                in_specs=[IN_SMEM] + [IN_VMEM] * (4 + power),
                out_specs=[IN_VMEM] * 3,
                out_shape=[full, narrow, gram_shape],
                scratch_shapes=[lookup],
                compiler_params=params(),
            )(table, turned, rounded, gram, *basis)
        send_next, send_last = pl.pallas_call(
            relay_kernel,
            name="relay",
            in_specs=[IN_VMEM] * 4 + [ANYWHERE] * len(after),
            out_specs=[IN_VMEM] * 2,
            out_shape=[vector_shape(3 * SEND, half)] * 2,
            compiler_params=params(),
        )(from_down, from_up, next_row, last_row, *after)
        from_last = shifted(send_next, "gx", 1)
        from_next = shifted(send_last, "gx", -1)
        received = (from_down, from_up, from_last, from_next)
        if power == 0:
            turned = pl.pallas_call(
                second_half_kernel,
                name="second_half",
                in_specs=[IN_HBM, IN_HBM, IN_VMEM],
                out_specs=IN_VMEM,
                out_shape=turned_shape,
                scratch_shapes=landing,
                input_output_aliases={2: 0},
                compiler_params=params(),
            )(diag_blocks, face_blocks, turned)
            outs = pl.pallas_call(
                whole_kernel,
                name="whole",
                in_specs=[IN_SMEM] * 2 + [IN_VMEM] * 7,
                out_specs=[IN_VMEM] * 7,
                out_shape=[full, narrow] + packets + [gram_shape],
                scratch_shapes=[lookup],
                compiler_params=params(),
            )(neighbours, send_slots, turned, rounded, *received, first)
        else:
            shapes = [full, narrow] + ([rows_shape] if last else packets + [gram_shape])
            outs = pl.pallas_call(
                functools.partial(ghost_kernel, power),
                name=f"ghost{power}",
                in_specs=[IN_SMEM] + [IN_VMEM] * (10 + power),
                out_specs=[IN_VMEM] * len(shapes),
                out_shape=shapes,
                scratch_shapes=[lookup],
                input_output_aliases={9 + power: 0, 10 + power: 1},
                compiler_params=params(),
            )(
                table, turned, rounded, *received, gram, *basis, image, image_rounded,
            )
        basis.append(outs[0])
        rounded = outs[1]
        gram = outs[-1]
        if not last:
            up, down, next_row, last_row = outs[2:-1]
    gathered = lax.all_to_all(gram, ("gx", "gy"), 0, 0, tiled=True)
    return pl.pallas_call(
        finish_kernel,
        name="finish",
        in_specs=[IN_VMEM] * 6,
        out_specs=[IN_VMEM] * 2,
        out_shape=[full] * 2,
        compiler_params=params(),
    )(gathered, *basis)


def solution(mesh):
    in_specs = (
        P(("gx", "gy"), None, None),
        P(("gx", "gy"), None, None),
        P(("gx", "gy"), None, None, None),
        P(("gx", "gy"), None),
        P(("gx", "gy"), None, None),
        P(("gx", "gy")),
    )
    out_specs = (P(("gx", "gy"), None, None), P(("gx", "gy"), None, None))
    return jax.shard_map(
        per_device, mesh=mesh, in_specs=in_specs, out_specs=out_specs, check_vma=False
    )
```

```python
import functools

import jax
import jax.numpy as jnp
from jax import lax
from jax.experimental import pallas as pl
from jax.experimental.pallas import tpu as pltpu
from jax.sharding import PartitionSpec as P

POWERS = 4
CAP = 64
SEND = 16
FACES = 4
SIDE = 16
GROUPS = SIDE * SIDE
ROWS = 128
LOOKUP = CAP + 9 * SEND
NOTHING = CAP + 4 * SEND
UNROLL = 16
BLOCKS = FACES + 1
QUARTER = CAP // 4

IN_VMEM = pl.BlockSpec(memory_space=pltpu.VMEM)
IN_SMEM = pl.BlockSpec(memory_space=pltpu.SMEM)
ANYWHERE = pl.BlockSpec(memory_space=pl.ANY)
IN_HBM = pl.BlockSpec(memory_space=pltpu.HBM)
UP_DIRECTIONS = (2, 5, 8)
DOWN_DIRECTIONS = (0, 3, 6)
LOCAL_RUNS = CAP
PLACES = 2 * CAP
SLOTS = PLACES + FACES * CAP
TABLE = SLOTS + 2 * CAP + 2 * SEND
PAIRS = [(a, b) for a in range(5) for b in range(a, 5) if b > 0]
PAIR_LANE = {pair: at for at, pair in enumerate(PAIRS)}
LANES_PER_SIDE = 16


def vector_shape(count, dtype):
    return jax.ShapeDtypeStruct((count, 8, ROWS), dtype)


def params(mebibytes=16):
    return pltpu.CompilerParams(vmem_limit_bytes=mebibytes << 20)


def pack(slot_of, rounded, up, down, next_row, last_row):
    for target, directions in (
        (up, UP_DIRECTIONS),
        (down, DOWN_DIRECTIONS),
        (next_row, (7,)),
        (last_row, (1,)),
    ):
        for at, direction in enumerate(directions):
            for k in range(SEND):
                target[at * SEND + k] = rounded[slot_of(direction, k)]


def listed(send_slots):
    return lambda direction, k: jnp.maximum(send_slots[direction, 0, k], 0)


def planned(table):
    return lambda direction, k: table[SLOTS + direction * SEND + k]


def start_kernel(
    send_slots, counts, right_sides, diag, face, basis, rounded, up, down, next_row,
    last_row, diag_first, face_first, arrived,
):
    first = fetching(0, diag, face, diag_first, face_first, arrived)
    for copy in first:
        copy.start()
    element = lax.broadcasted_iota(jnp.int32, basis.shape, 0)
    live = jnp.where(element < counts[0], right_sides[...], 0.0)
    basis[...] = live
    rounded[...] = live.astype(jnp.bfloat16)
    pack(listed(send_slots), rounded, up, down, next_row, last_row)
    for copy in first:
        copy.wait()


def plan_kernel(neighbours, send_slots, table, done):
    local = jnp.int32(0)
    for e in range(CAP):
        at = [neighbours[f, e] for f in range(FACES)]
        farthest = jnp.maximum(jnp.maximum(at[0], at[1]), jnp.maximum(at[2], at[3]))
        ghost = farthest >= CAP
        place = jnp.where(ghost, CAP - 1 - (e - local), local)
        table[place] = e
        for f in range(FACES):
            table[PLACES + f * CAP + place] = jnp.where(at[f] < 0, NOTHING, at[f])
        local = local + jnp.where(ghost, 0, 1)
    table[LOCAL_RUNS] = local // UNROLL
    for direction in range(9):
        for k in range(SEND):
            slot = listed(send_slots)(direction, k)
            table[SLOTS + direction * SEND + k] = slot
    done[...] = jnp.zeros_like(done)


def fetching(first, diag, face, diag_here, face_here, arrived):
    there = pl.ds(first, QUARTER)
    return (
        pltpu.make_async_copy(diag.at[there], diag_here, arrived.at[0]),
        pltpu.make_async_copy(face.at[there], face_here, arrived.at[1]),
    )


def transpose_quarter(first, diag_here, face_here, turned):
    def element(at, carry):
        e = first + at
        turned[e, 0:ROWS] = diag_here[at].T
        for f in range(FACES):
            turned[e, (f + 1) * ROWS : (f + 2) * ROWS] = face_here[at, f].T
        return carry

    lax.fori_loop(0, QUARTER, element, 0, unroll=8)


def first_half_kernel(
    diag, face, diag_first, face_first, turned, diag_third, face_third, done,
    diag_here, face_here, arrived, arrived_third,
):
    second = fetching(QUARTER, diag, face, diag_here, face_here, arrived)
    third = fetching(2 * QUARTER, diag, face, diag_third, face_third, arrived_third)
    for copy in second + third:
        copy.start()
    transpose_quarter(0, diag_first, face_first, turned)
    for copy in second:
        copy.wait()
    transpose_quarter(QUARTER, diag_here, face_here, turned)
    done[...] = jnp.zeros_like(done)
    for copy in third:
        copy.wait()


def second_half_kernel(
    diag, face, diag_third, face_third, before, turned, diag_here, face_here, arrived
):
    fourth = fetching(3 * QUARTER, diag, face, diag_here, face_here, arrived)
    for copy in fourth:
        copy.start()
    transpose_quarter(2 * QUARTER, diag_third, face_third, turned)
    for copy in fourth:
        copy.wait()
    transpose_quarter(3 * QUARTER, diag_here, face_here, turned)


def relay_kernel(*refs):
    from_down, from_up, next_row, last_row = refs[:4]
    send_next, send_last = refs[-2:]
    send_next[0:SEND] = from_up[2 * SEND : 3 * SEND]
    send_next[SEND : 2 * SEND] = next_row[...]
    send_next[2 * SEND : 3 * SEND] = from_down[2 * SEND : 3 * SEND]
    send_last[0:SEND] = from_up[0:SEND]
    send_last[SEND : 2 * SEND] = last_row[...]
    send_last[2 * SEND : 3 * SEND] = from_down[0:SEND]


def fill_local(lookup, rounded):
    lookup[0:CAP] = rounded[...]
    lookup[NOTHING : NOTHING + SEND] = jnp.zeros((SEND, 8, ROWS), jnp.bfloat16)


def fill_ghosts(lookup, from_down, from_up, from_last, from_next):
    lookup[CAP : CAP + 3 * SEND] = from_next[...]
    lookup[CAP + 3 * SEND : CAP + 4 * SEND] = from_up[SEND : 2 * SEND]
    lookup[CAP + 5 * SEND : CAP + 6 * SEND] = from_down[SEND : 2 * SEND]
    lookup[CAP + 6 * SEND : CAP + 9 * SEND] = from_last[...]


def apply_runs(first, limit, find, turned, lookup, basis, image, image_rounded):
    def near(found):
        vectors = jnp.concatenate([lookup[at] for at in found], axis=1)
        return vectors.astype(jnp.float32)

    def two(found, sums):
        elements = [places[0] for places in found]
        both = jnp.dot(
            jnp.concatenate([near(f) for f in found], axis=0).astype(jnp.bfloat16),
            jnp.concatenate([turned[e] for e in elements], axis=1),
            preferred_element_type=jnp.float32,
        )
        for at, e in enumerate(elements):
            out = both[8 * at : 8 * at + 8, ROWS * at : ROWS * at + ROWS]
            image[e] = out
            image_rounded[e] = out.astype(jnp.bfloat16)
            others = [ref[e] for ref in basis] + [out]
            sums = tuple(s + out * other for s, other in zip(sums, others))
        return sums

    def run(step, sums):
        for u in range(0, UNROLL, 2):
            at = step * UNROLL + u
            sums = two([find(at), find(at + 1)], sums)
        return sums

    zero = jnp.zeros((8, ROWS), jnp.float32)
    return lax.fori_loop(first, limit, run, (zero,) * (len(basis) + 1))


def with_sums(gram, sums):
    lane = lax.broadcasted_iota(jnp.int32, (8, ROWS), 1)
    newest = len(sums) - 1
    for a, s in enumerate(sums):
        total = jnp.sum(s, axis=1, keepdims=True)
        gram = gram + jnp.where(lane == PAIR_LANE[a, newest], total, 0.0)
    return gram


def whole_kernel(
    neighbours, send_slots, turned, rounded, from_down, from_up, from_last, from_next,
    b0, image, image_rounded, up, down, next_row, last_row, gram_out, lookup,
):
    fill_local(lookup, rounded)
    fill_ghosts(lookup, from_down, from_up, from_last, from_next)

    def find(e):
        at = [neighbours[f, e] for f in range(FACES)]
        return [e] + [jnp.where(a < 0, NOTHING, a) for a in at]

    sums = apply_runs(
        0, CAP // UNROLL, find, turned, lookup, (b0,), image, image_rounded
    )
    pack(listed(send_slots), image_rounded, up, down, next_row, last_row)
    gram_out[...] = with_sums(jnp.zeros((8, ROWS), jnp.float32), sums)


def find_in(table):
    return lambda at: [table[at]] + [table[PLACES + f * CAP + at] for f in range(FACES)]


def local_kernel(power, *refs):
    table, turned, rounded, gram_in = refs[:4]
    basis = refs[4 : 5 + power]
    image, image_rounded, gram_out, lookup = refs[5 + power :]
    fill_local(lookup, rounded)
    sums = apply_runs(
        0, table[LOCAL_RUNS], find_in(table), turned, lookup, basis, image, image_rounded
    )
    gram_out[...] = with_sums(gram_in[...], sums)


def ghost_kernel(power, *refs):
    table, turned, rounded = refs[:3]
    received = refs[3:7]
    gram_in = refs[7]
    basis = refs[8 : 9 + power]
    refs = refs[11 + power :]
    last = power == POWERS - 1
    if last:
        image, image_rounded, gram_out, lookup = refs
    else:
        image, image_rounded, up, down, next_row, last_row, gram_out, lookup = refs
    fill_local(lookup, rounded)
    fill_ghosts(lookup, *received)
    sums = apply_runs(
        table[LOCAL_RUNS], CAP // UNROLL, find_in(table), turned, lookup, basis, image,
        image_rounded,
    )
    if not last:
        pack(planned(table), image_rounded, up, down, next_row, last_row)
    gram = with_sums(gram_in[...], sums)
    if last:
        lane = lax.broadcasted_iota(jnp.int32, (8, ROWS), 1)
        side = lax.broadcasted_iota(jnp.int32, (8, ROWS), 0)
        spread = jnp.zeros((8, ROWS), jnp.float32)
        for at in range(len(PAIRS)):
            value = jnp.broadcast_to(gram[:, at : at + 1], (8, ROWS))
            spread = jnp.where(lane == side * LANES_PER_SIDE + at, value, spread)
        row = jnp.sum(spread, axis=0, keepdims=True)
        gram_out[...] = jnp.broadcast_to(row, gram_out.shape)
    else:
        gram_out[...] = gram


def finish_kernel(gram_rows, b0, b1, b2, b3, b4, solution, residual):
    lane = lax.broadcasted_iota(jnp.int32, (8, ROWS), 1)
    side = lax.broadcasted_iota(jnp.int32, (8, ROWS), 0)
    row = jnp.sum(gram_rows[...], axis=0, keepdims=True)
    spread = jnp.broadcast_to(row, (8, ROWS))

    def entry(a, b):
        at = PAIR_LANE[min(a, b), max(a, b)]
        mine = jnp.where(lane == side * LANES_PER_SIDE + at, spread, 0.0)
        total = jnp.sum(mine, axis=1, keepdims=True)
        return jnp.broadcast_to(total, (8, ROWS))

    factor = {}
    inverse = []
    for i in range(POWERS):
        for j in range(i + 1):
            value = entry(i + 1, j + 1)
            for k in range(j):
                value = value - factor[i, k] * factor[j, k]
            if i == j:
                inverse.append(1.0 / jnp.sqrt(value))
            else:
                factor[i, j] = value * inverse[j]
    forward = []
    for i in range(POWERS):
        value = entry(0, i + 1)
        for k in range(i):
            value = value - factor[i, k] * forward[k]
        forward.append(value * inverse[i])
    weights = [None] * POWERS
    for i in reversed(range(POWERS)):
        value = forward[i]
        for k in range(i + 1, POWERS):
            value = value - factor[k, i] * weights[k]
        weights[i] = value * inverse[i]
    basis = (b0, b1, b2, b3, b4)

    def several(step, carry):
        for u in range(8):
            e = step * 8 + u
            v = [ref[e] for ref in basis]
            total = weights[0] * v[0]
            moved = weights[0] * v[1]
            for k in range(1, POWERS):
                total = total + weights[k] * v[k]
                moved = moved + weights[k] * v[k + 1]
            solution[e] = total
            residual[e] = v[0] - moved
        return carry

    lax.fori_loop(0, CAP // 8, several, 0)


def shifted(block, axis, distance):
    return lax.ppermute(block, axis, [(i, (i + distance) % SIDE) for i in range(SIDE)])


def per_device(right_sides, diag_blocks, face_blocks, neighbours, send_slots, counts):
    half = jnp.bfloat16
    neighbours = neighbours.T
    send_slots = send_slots.transpose(1, 0, 2)
    in_place = lambda array: pltpu.with_memory_space_constraint(array, pltpu.HBM)
    diag_blocks = in_place(diag_blocks)
    face_blocks = in_place(face_blocks)
    packets = [vector_shape(n * SEND, half) for n in (3, 3, 1, 1)]
    full = vector_shape(CAP, jnp.float32)
    narrow = vector_shape(CAP, half)
    gram_shape = jax.ShapeDtypeStruct((8, ROWS), jnp.float32)
    rows_shape = jax.ShapeDtypeStruct((GROUPS, ROWS), jnp.float32)
    turned_shape = pltpu.VMEM((CAP, BLOCKS * ROWS, ROWS), half)
    lookup = pltpu.VMEM((LOOKUP, 8, ROWS), half)
    quarter = [
        pltpu.VMEM((QUARTER, ROWS, ROWS), half),
        pltpu.VMEM((QUARTER, FACES, ROWS, ROWS), half),
    ]
    arrived = pltpu.SemaphoreType.DMA((2,))
    first, rounded, up, down, next_row, last_row, *blocks = pl.pallas_call(
        start_kernel,
        name="start",
        in_specs=[IN_SMEM, IN_SMEM, IN_VMEM, IN_HBM, IN_HBM],
        out_specs=[IN_VMEM] * 8,
        out_shape=[full, narrow] + packets + quarter,
        scratch_shapes=[arrived],
        compiler_params=params(),
    )(in_place(send_slots), counts, in_place(right_sides), diag_blocks, face_blocks)
    basis = [first]
    gram = None
    for power in range(POWERS):
        last = power == POWERS - 1
        from_down = shifted(up, "gy", 1)
        from_up = shifted(down, "gy", -1)
        after = ()
        if power == 0:
            turned, *blocks, done = pl.pallas_call(
                first_half_kernel,
                name="first_half",
                in_specs=[IN_HBM] * 2 + [IN_VMEM] * 2,
                out_specs=[IN_VMEM] * 4,
                out_shape=[turned_shape] + quarter + [gram_shape],
                scratch_shapes=quarter + [arrived, arrived],
                compiler_params=params(),
            )(diag_blocks, face_blocks, *blocks)
            after = (done,)
        elif power == 1:
            table, done = pl.pallas_call(
                plan_kernel,
                name="plan",
                in_specs=[IN_SMEM] * 2,
                out_specs=[IN_SMEM, IN_VMEM],
                out_shape=[pltpu.SMEM((TABLE,), jnp.int32), gram_shape],
                compiler_params=params(),
            )(neighbours, send_slots)
            after = (done,)
        if power > 0:
            image, image_rounded, gram = pl.pallas_call(
                functools.partial(local_kernel, power),
                name=f"local{power}",
                in_specs=[IN_SMEM] + [IN_VMEM] * (4 + power),
                out_specs=[IN_VMEM] * 3,
                out_shape=[full, narrow, gram_shape],
                scratch_shapes=[lookup],
                compiler_params=params(),
            )(table, turned, rounded, gram, *basis)
        send_next, send_last = pl.pallas_call(
            relay_kernel,
            name="relay",
            in_specs=[IN_VMEM] * 4 + [ANYWHERE] * len(after),
            out_specs=[IN_VMEM] * 2,
            out_shape=[vector_shape(3 * SEND, half)] * 2,
            compiler_params=params(),
        )(from_down, from_up, next_row, last_row, *after)
        from_last = shifted(send_next, "gx", 1)
        from_next = shifted(send_last, "gx", -1)
        received = (from_down, from_up, from_last, from_next)
        if power == 0:
            turned = pl.pallas_call(
                second_half_kernel,
                name="second_half",
                in_specs=[IN_HBM] * 2 + [IN_VMEM] * 3,
                out_specs=IN_VMEM,
                out_shape=turned_shape,
                scratch_shapes=quarter + [arrived],
                input_output_aliases={4: 0},
                compiler_params=params(),
            )(diag_blocks, face_blocks, *blocks, turned)
            outs = pl.pallas_call(
                whole_kernel,
                name="whole",
                in_specs=[IN_SMEM] * 2 + [IN_VMEM] * 7,
                out_specs=[IN_VMEM] * 7,
                out_shape=[full, narrow] + packets + [gram_shape],
                scratch_shapes=[lookup],
                compiler_params=params(),
            )(neighbours, send_slots, turned, rounded, *received, first)
        else:
            shapes = [full, narrow] + ([rows_shape] if last else packets + [gram_shape])
            outs = pl.pallas_call(
                functools.partial(ghost_kernel, power),
                name=f"ghost{power}",
                in_specs=[IN_SMEM] + [IN_VMEM] * (10 + power),
                out_specs=[IN_VMEM] * len(shapes),
                out_shape=shapes,
                scratch_shapes=[lookup],
                input_output_aliases={9 + power: 0, 10 + power: 1},
                compiler_params=params(),
            )(
                table, turned, rounded, *received, gram, *basis, image, image_rounded,
            )
        basis.append(outs[0])
        rounded = outs[1]
        gram = outs[-1]
        if not last:
            up, down, next_row, last_row = outs[2:-1]
    gathered = lax.all_to_all(gram, ("gx", "gy"), 0, 0, tiled=True)
    return pl.pallas_call(
        finish_kernel,
        name="finish",
        in_specs=[IN_VMEM] * 6,
        out_specs=[IN_VMEM] * 2,
        out_shape=[full] * 2,
        compiler_params=params(),
    )(gathered, *basis)


def solution(mesh):
    in_specs = (
        P(("gx", "gy"), None, None),
        P(("gx", "gy"), None, None),
        P(("gx", "gy"), None, None, None),
        P(("gx", "gy"), None),
        P(("gx", "gy"), None, None),
        P(("gx", "gy")),
    )
    out_specs = (P(("gx", "gy"), None, None), P(("gx", "gy"), None, None))
    return jax.shard_map(
        per_device, mesh=mesh, in_specs=in_specs, out_specs=out_specs, check_vma=False
    )
```

```python
import functools

import jax
import jax.numpy as jnp
from jax import lax
from jax.experimental import pallas as pl
from jax.experimental.pallas import tpu as pltpu
from jax.sharding import PartitionSpec as P

POWERS = 4
CAP = 64
SEND = 16
FACES = 4
SIDE = 16
GROUPS = SIDE * SIDE
ROWS = 128
LOOKUP = CAP + 9 * SEND
NOTHING = CAP + 4 * SEND
UNROLL = 16
BLOCKS = FACES + 1
QUARTER = CAP // 4
EIGHTH = CAP // 8

IN_VMEM = pl.BlockSpec(memory_space=pltpu.VMEM)
IN_SMEM = pl.BlockSpec(memory_space=pltpu.SMEM)
ANYWHERE = pl.BlockSpec(memory_space=pl.ANY)
IN_HBM = pl.BlockSpec(memory_space=pltpu.HBM)
UP_DIRECTIONS = (2, 5, 8)
DOWN_DIRECTIONS = (0, 3, 6)
LOCAL_RUNS = CAP
PLACES = 2 * CAP
SLOTS = PLACES + FACES * CAP
TABLE = SLOTS + 2 * CAP + 2 * SEND
PAIRS = [(a, b) for a in range(5) for b in range(a, 5) if b > 0]
PAIR_LANE = {pair: at for at, pair in enumerate(PAIRS)}
LANES_PER_SIDE = 16


def vector_shape(count, dtype):
    return jax.ShapeDtypeStruct((count, 8, ROWS), dtype)


def params(mebibytes=16):
    return pltpu.CompilerParams(vmem_limit_bytes=mebibytes << 20)


def pack(slot_of, rounded, up, down, next_row, last_row):
    for target, directions in (
        (up, UP_DIRECTIONS),
        (down, DOWN_DIRECTIONS),
        (next_row, (7,)),
        (last_row, (1,)),
    ):
        for at, direction in enumerate(directions):
            for k in range(SEND):
                target[at * SEND + k] = rounded[slot_of(direction, k)]


def listed(send_slots):
    return lambda direction, k: jnp.maximum(send_slots[direction, 0, k], 0)


def planned(table):
    return lambda direction, k: table[SLOTS + direction * SEND + k]


def start_kernel(
    send_slots, counts, right_sides, basis, rounded, up, down, next_row, last_row
):
    element = lax.broadcasted_iota(jnp.int32, basis.shape, 0)
    live = jnp.where(element < counts[0], right_sides[...], 0.0)
    basis[...] = live
    rounded[...] = live.astype(jnp.bfloat16)
    pack(listed(send_slots), rounded, up, down, next_row, last_row)


def plan_kernel(neighbours, send_slots, table, done):
    local = jnp.int32(0)
    for e in range(CAP):
        at = [neighbours[f, e] for f in range(FACES)]
        farthest = jnp.maximum(jnp.maximum(at[0], at[1]), jnp.maximum(at[2], at[3]))
        ghost = farthest >= CAP
        place = jnp.where(ghost, CAP - 1 - (e - local), local)
        table[place] = e
        for f in range(FACES):
            table[PLACES + f * CAP + place] = jnp.where(at[f] < 0, NOTHING, at[f])
        local = local + jnp.where(ghost, 0, 1)
    table[LOCAL_RUNS] = local // UNROLL
    for direction in range(9):
        for k in range(SEND):
            slot = listed(send_slots)(direction, k)
            table[SLOTS + direction * SEND + k] = slot
    done[...] = jnp.zeros_like(done)


def fetching(first, diag, face, diag_here, face_here, arrived):
    there = pl.ds(first, diag_here.shape[0])
    return (
        pltpu.make_async_copy(diag.at[there], diag_here, arrived.at[0]),
        pltpu.make_async_copy(face.at[there], face_here, arrived.at[1]),
    )


def transpose_some(first, diag_here, face_here, turned, also=lambda at: None):
    def element(at, carry):
        e = first + at
        turned[e, 0:ROWS] = diag_here[at].T
        for f in range(FACES):
            turned[e, (f + 1) * ROWS : (f + 2) * ROWS] = face_here[at, f].T
        also(at)
        return carry

    lax.fori_loop(0, diag_here.shape[0], element, 0, unroll=8)


def first_half_kernel(
    diag, face, turned, diag_third, face_third, done, diag_here, face_here, arrived
):
    parts = []
    for at in range(0, 2 * QUARTER, EIGHTH):
        here = pl.ds(at, EIGHTH)
        place = diag_here.at[here], face_here.at[here]
        parts.append((at, place, fetching(at, diag, face, *place, arrived.at[at // EIGHTH])))
    third = fetching(2 * QUARTER, diag, face, diag_third, face_third, arrived.at[4])
    for _, _, copies in parts:
        for copy in copies:
            copy.start()
    for copy in third:
        copy.start()
    for at, place, copies in parts:
        for copy in copies:
            copy.wait()
        transpose_some(at, *place, turned)
    done[...] = jnp.zeros_like(done)
    for copy in third:
        copy.wait()


def second_half_kernel(
    neighbours, diag, face, diag_third, face_third, rounded, before, turned, image,
    image_rounded, ghostly, diag_here, face_here, arrived, lookup,
):
    fourth = fetching(3 * QUARTER, diag, face, diag_here, face_here, arrived)
    for copy in fourth:
        copy.start()
    fill_local(lookup, rounded)

    def apply_from(first, diag_of, face_of):
        def apply(at):
            e = first + at
            vectors = [lookup[e]]
            for f in range(FACES):
                near = neighbours[f, e]
                vectors.append(
                    lookup[jnp.where((near < 0) | (near >= CAP), NOTHING, near)]
                )
            blocks = [diag_of[at]] + [face_of[at, f] for f in range(FACES)]
            out = lax.dot_general(
                jnp.concatenate(vectors, axis=1),
                jnp.concatenate(blocks, axis=1),
                (((1,), (1,)), ((), ())),
                preferred_element_type=jnp.float32,
            )
            image[e] = out
            image_rounded[e] = out.astype(jnp.bfloat16)

        return apply

    transpose_some(
        2 * QUARTER, diag_third, face_third, turned,
        apply_from(2 * QUARTER, diag_third, face_third),
    )
    for run in (2, 3):
        farthest = jnp.int32(-1)
        for e in range(run * UNROLL, (run + 1) * UNROLL):
            for f in range(FACES):
                farthest = jnp.maximum(farthest, neighbours[f, e])
        ghostly[run] = farthest
    for copy in fourth:
        copy.wait()
    transpose_some(
        3 * QUARTER, diag_here, face_here, turned,
        apply_from(3 * QUARTER, diag_here, face_here),
    )


def relay_kernel(*refs):
    from_down, from_up, next_row, last_row = refs[:4]
    send_next, send_last = refs[-2:]
    send_next[0:SEND] = from_up[2 * SEND : 3 * SEND]
    send_next[SEND : 2 * SEND] = next_row[...]
    send_next[2 * SEND : 3 * SEND] = from_down[2 * SEND : 3 * SEND]
    send_last[0:SEND] = from_up[0:SEND]
    send_last[SEND : 2 * SEND] = last_row[...]
    send_last[2 * SEND : 3 * SEND] = from_down[0:SEND]


def fill_local(lookup, rounded):
    lookup[0:CAP] = rounded[...]
    lookup[NOTHING : NOTHING + SEND] = jnp.zeros((SEND, 8, ROWS), jnp.bfloat16)


def fill_ghosts(lookup, from_down, from_up, from_last, from_next):
    lookup[CAP : CAP + 3 * SEND] = from_next[...]
    lookup[CAP + 3 * SEND : CAP + 4 * SEND] = from_up[SEND : 2 * SEND]
    lookup[CAP + 5 * SEND : CAP + 6 * SEND] = from_down[SEND : 2 * SEND]
    lookup[CAP + 6 * SEND : CAP + 9 * SEND] = from_last[...]


def apply_runs(first, limit, find, turned, lookup, basis, image, image_rounded):
    def near(found):
        vectors = jnp.concatenate([lookup[at] for at in found], axis=1)
        return vectors.astype(jnp.float32)

    def two(found, sums):
        elements = [places[0] for places in found]
        both = jnp.dot(
            jnp.concatenate([near(f) for f in found], axis=0).astype(jnp.bfloat16),
            jnp.concatenate([turned[e] for e in elements], axis=1),
            preferred_element_type=jnp.float32,
        )
        for at, e in enumerate(elements):
            out = both[8 * at : 8 * at + 8, ROWS * at : ROWS * at + ROWS]
            image[e] = out
            image_rounded[e] = out.astype(jnp.bfloat16)
            others = [ref[e] for ref in basis] + [out]
            sums = tuple(s + out * other for s, other in zip(sums, others))
        return sums

    def run(step, sums):
        for u in range(0, UNROLL, 2):
            at = step * UNROLL + u
            sums = two([find(at), find(at + 1)], sums)
        return sums

    zero = jnp.zeros((8, ROWS), jnp.float32)
    return lax.fori_loop(first, limit, run, (zero,) * (len(basis) + 1))


def with_sums(gram, sums):
    lane = lax.broadcasted_iota(jnp.int32, (8, ROWS), 1)
    newest = len(sums) - 1
    for a, s in enumerate(sums):
        total = jnp.sum(s, axis=1, keepdims=True)
        gram = gram + jnp.where(lane == PAIR_LANE[a, newest], total, 0.0)
    return gram


def whole_kernel(
    neighbours, send_slots, ghostly, turned, rounded, from_down, from_up, from_last,
    from_next, b0, before, before_rounded, image, image_rounded, up, down, next_row,
    last_row, gram_out, lookup,
):
    fill_local(lookup, rounded)
    fill_ghosts(lookup, from_down, from_up, from_last, from_next)

    def find(e):
        at = [neighbours[f, e] for f in range(FACES)]
        return [e] + [jnp.where(a < 0, NOTHING, a) for a in at]

    def again(first, limit):
        apply_runs(first, limit, find, turned, lookup, (), image, image_rounded)

    again(0, 2)
    for run in (2, 3):
        pl.when(ghostly[run] >= CAP)(functools.partial(again, run, run + 1))
    pack(listed(send_slots), image_rounded, up, down, next_row, last_row)

    def products(step, sums):
        for u in range(UNROLL):
            out = image[step * UNROLL + u]
            sums = sums[0] + b0[step * UNROLL + u] * out, sums[1] + out * out
        return sums

    zero = jnp.zeros((8, ROWS), jnp.float32)
    sums = lax.fori_loop(0, CAP // UNROLL, products, (zero, zero))
    gram_out[...] = with_sums(zero, sums)


def find_in(table):
    return lambda at: [table[at]] + [table[PLACES + f * CAP + at] for f in range(FACES)]


def local_kernel(power, *refs):
    table, turned, rounded, gram_in = refs[:4]
    basis = refs[4 : 5 + power]
    image, image_rounded, gram_out, lookup = refs[5 + power :]
    fill_local(lookup, rounded)
    sums = apply_runs(
        0, table[LOCAL_RUNS], find_in(table), turned, lookup, basis, image, image_rounded
    )
    gram_out[...] = with_sums(gram_in[...], sums)


def ghost_kernel(power, *refs):
    table, turned, rounded = refs[:3]
    received = refs[3:7]
    gram_in = refs[7]
    basis = refs[8 : 9 + power]
    refs = refs[11 + power :]
    last = power == POWERS - 1
    if last:
        image, image_rounded, gram_out, lookup = refs
    else:
        image, image_rounded, up, down, next_row, last_row, gram_out, lookup = refs
    fill_local(lookup, rounded)
    fill_ghosts(lookup, *received)
    sums = apply_runs(
        table[LOCAL_RUNS], CAP // UNROLL, find_in(table), turned, lookup, basis, image,
        image_rounded,
    )
    if not last:
        pack(planned(table), image_rounded, up, down, next_row, last_row)
    gram = with_sums(gram_in[...], sums)
    if last:
        lane = lax.broadcasted_iota(jnp.int32, (8, ROWS), 1)
        side = lax.broadcasted_iota(jnp.int32, (8, ROWS), 0)
        spread = jnp.zeros((8, ROWS), jnp.float32)
        for at in range(len(PAIRS)):
            value = jnp.broadcast_to(gram[:, at : at + 1], (8, ROWS))
            spread = jnp.where(lane == side * LANES_PER_SIDE + at, value, spread)
        row = jnp.sum(spread, axis=0, keepdims=True)
        gram_out[...] = jnp.broadcast_to(row, gram_out.shape)
    else:
        gram_out[...] = gram


def finish_kernel(gram_rows, b0, b1, b2, b3, b4, solution, residual):
    lane = lax.broadcasted_iota(jnp.int32, (8, ROWS), 1)
    side = lax.broadcasted_iota(jnp.int32, (8, ROWS), 0)
    row = jnp.sum(gram_rows[...], axis=0, keepdims=True)
    spread = jnp.broadcast_to(row, (8, ROWS))

    def entry(a, b):
        at = PAIR_LANE[min(a, b), max(a, b)]
        mine = jnp.where(lane == side * LANES_PER_SIDE + at, spread, 0.0)
        total = jnp.sum(mine, axis=1, keepdims=True)
        return jnp.broadcast_to(total, (8, ROWS))

    factor = {}
    inverse = []
    for i in range(POWERS):
        for j in range(i + 1):
            value = entry(i + 1, j + 1)
            for k in range(j):
                value = value - factor[i, k] * factor[j, k]
            if i == j:
                inverse.append(1.0 / jnp.sqrt(value))
            else:
                factor[i, j] = value * inverse[j]
    forward = []
    for i in range(POWERS):
        value = entry(0, i + 1)
        for k in range(i):
            value = value - factor[i, k] * forward[k]
        forward.append(value * inverse[i])
    weights = [None] * POWERS
    for i in reversed(range(POWERS)):
        value = forward[i]
        for k in range(i + 1, POWERS):
            value = value - factor[k, i] * weights[k]
        weights[i] = value * inverse[i]
    basis = (b0, b1, b2, b3, b4)

    def several(step, carry):
        for u in range(8):
            e = step * 8 + u
            v = [ref[e] for ref in basis]
            total = weights[0] * v[0]
            moved = weights[0] * v[1]
            for k in range(1, POWERS):
                total = total + weights[k] * v[k]
                moved = moved + weights[k] * v[k + 1]
            solution[e] = total
            residual[e] = v[0] - moved
        return carry

    lax.fori_loop(0, CAP // 8, several, 0)


def shifted(block, axis, distance):
    return lax.ppermute(block, axis, [(i, (i + distance) % SIDE) for i in range(SIDE)])


def per_device(right_sides, diag_blocks, face_blocks, neighbours, send_slots, counts):
    half = jnp.bfloat16
    neighbours = neighbours.T
    send_slots = send_slots.transpose(1, 0, 2)
    in_place = lambda array: pltpu.with_memory_space_constraint(array, pltpu.HBM)
    diag_blocks = in_place(diag_blocks)
    face_blocks = in_place(face_blocks)
    packets = [vector_shape(n * SEND, half) for n in (3, 3, 1, 1)]
    full = vector_shape(CAP, jnp.float32)
    narrow = vector_shape(CAP, half)
    gram_shape = jax.ShapeDtypeStruct((8, ROWS), jnp.float32)
    rows_shape = jax.ShapeDtypeStruct((GROUPS, ROWS), jnp.float32)
    turned_shape = pltpu.VMEM((CAP, BLOCKS * ROWS, ROWS), half)
    lookup = pltpu.VMEM((LOOKUP, 8, ROWS), half)
    quarter = [
        pltpu.VMEM((QUARTER, ROWS, ROWS), half),
        pltpu.VMEM((QUARTER, FACES, ROWS, ROWS), half),
    ]
    arrived = pltpu.SemaphoreType.DMA((2,))
    first, rounded, up, down, next_row, last_row = pl.pallas_call(
        start_kernel,
        name="start",
        in_specs=[IN_SMEM, IN_SMEM, IN_VMEM],
        out_specs=[IN_VMEM] * 6,
        out_shape=[full, narrow] + packets,
        compiler_params=params(),
    )(in_place(send_slots), counts, in_place(right_sides))
    basis = [first]
    gram = None
    for power in range(POWERS):
        last = power == POWERS - 1
        from_down = shifted(up, "gy", 1)
        from_up = shifted(down, "gy", -1)
        after = ()
        if power == 0:
            turned, *blocks, done = pl.pallas_call(
                first_half_kernel,
                name="first_half",
                in_specs=[IN_HBM] * 2,
                out_specs=[IN_VMEM] * 4,
                out_shape=[turned_shape] + quarter + [gram_shape],
                scratch_shapes=[
                    pltpu.VMEM((2 * QUARTER, ROWS, ROWS), half),
                    pltpu.VMEM((2 * QUARTER, FACES, ROWS, ROWS), half),
                    pltpu.SemaphoreType.DMA((5, 2)),
                ],
                compiler_params=params(),
            )(diag_blocks, face_blocks)
            after = (done,)
        elif power == 1:
            table, done = pl.pallas_call(
                plan_kernel,
                name="plan",
                in_specs=[IN_SMEM] * 2,
                out_specs=[IN_SMEM, IN_VMEM],
                out_shape=[pltpu.SMEM((TABLE,), jnp.int32), gram_shape],
                compiler_params=params(),
            )(neighbours, send_slots)
            after = (done,)
        if power > 0:
            image, image_rounded, gram = pl.pallas_call(
                functools.partial(local_kernel, power),
                name=f"local{power}",
                in_specs=[IN_SMEM] + [IN_VMEM] * (4 + power),
                out_specs=[IN_VMEM] * 3,
                out_shape=[full, narrow, gram_shape],
                scratch_shapes=[lookup],
                compiler_params=params(),
            )(table, turned, rounded, gram, *basis)
        send_next, send_last = pl.pallas_call(
            relay_kernel,
            name="relay",
            in_specs=[IN_VMEM] * 4 + [ANYWHERE] * len(after),
            out_specs=[IN_VMEM] * 2,
            out_shape=[vector_shape(3 * SEND, half)] * 2,
            compiler_params=params(),
        )(from_down, from_up, next_row, last_row, *after)
        from_last = shifted(send_next, "gx", 1)
        from_next = shifted(send_last, "gx", -1)
        received = (from_down, from_up, from_last, from_next)
        if power == 0:
            turned, image, image_rounded, ghostly = pl.pallas_call(
                second_half_kernel,
                name="second_half",
                in_specs=[IN_SMEM] + [IN_HBM] * 2 + [IN_VMEM] * 4,
                out_specs=[IN_VMEM] * 3 + [IN_SMEM],
                out_shape=[turned_shape, full, narrow, pltpu.SMEM((8,), jnp.int32)],
                scratch_shapes=quarter + [arrived, lookup],
                input_output_aliases={6: 0},
                compiler_params=params(),
            )(neighbours, diag_blocks, face_blocks, *blocks, rounded, turned)
            outs = pl.pallas_call(
                whole_kernel,
                name="whole",
                in_specs=[IN_SMEM] * 3 + [IN_VMEM] * 9,
                out_specs=[IN_VMEM] * 7,
                out_shape=[full, narrow] + packets + [gram_shape],
                scratch_shapes=[lookup],
                input_output_aliases={10: 0, 11: 1},
                compiler_params=params(),
            )(
                neighbours, send_slots, ghostly, turned, rounded, *received, first,
                image, image_rounded,
            )
        else:
            shapes = [full, narrow] + ([rows_shape] if last else packets + [gram_shape])
            outs = pl.pallas_call(
                functools.partial(ghost_kernel, power),
                name=f"ghost{power}",
                in_specs=[IN_SMEM] + [IN_VMEM] * (10 + power),
                out_specs=[IN_VMEM] * len(shapes),
                out_shape=shapes,
                scratch_shapes=[lookup],
                input_output_aliases={9 + power: 0, 10 + power: 1},
                compiler_params=params(),
            )(
                table, turned, rounded, *received, gram, *basis, image, image_rounded,
            )
        basis.append(outs[0])
        rounded = outs[1]
        gram = outs[-1]
        if not last:
            up, down, next_row, last_row = outs[2:-1]
    gathered = lax.all_to_all(gram, ("gx", "gy"), 0, 0, tiled=True)
    return pl.pallas_call(
        finish_kernel,
        name="finish",
        in_specs=[IN_VMEM] * 6,
        out_specs=[IN_VMEM] * 2,
        out_shape=[full] * 2,
        compiler_params=params(),
    )(gathered, *basis)


def solution(mesh):
    in_specs = (
        P(("gx", "gy"), None, None),
        P(("gx", "gy"), None, None),
        P(("gx", "gy"), None, None, None),
        P(("gx", "gy"), None),
        P(("gx", "gy"), None, None),
        P(("gx", "gy")),
    )
    out_specs = (P(("gx", "gy"), None, None), P(("gx", "gy"), None, None))
    return jax.shard_map(
        per_device, mesh=mesh, in_specs=in_specs, out_specs=out_specs, check_vma=False
    )
```

```python
import functools

import jax
import jax.numpy as jnp
from jax import lax
from jax.experimental import pallas as pl
from jax.experimental.pallas import tpu as pltpu
from jax.sharding import PartitionSpec as P

POWERS = 4
CAP = 64
SEND = 16
FACES = 4
SIDE = 16
GROUPS = SIDE * SIDE
ROWS = 128
LOOKUP = CAP + 9 * SEND
NOTHING = CAP + 4 * SEND
UNROLL = 16
BLOCKS = FACES + 1
QUARTER = CAP // 4
EIGHTH = CAP // 8

IN_VMEM = pl.BlockSpec(memory_space=pltpu.VMEM)
IN_SMEM = pl.BlockSpec(memory_space=pltpu.SMEM)
ANYWHERE = pl.BlockSpec(memory_space=pl.ANY)
IN_HBM = pl.BlockSpec(memory_space=pltpu.HBM)
UP_DIRECTIONS = (2, 5, 8)
DOWN_DIRECTIONS = (0, 3, 6)
LOCAL_RUNS = CAP
PLACES = 2 * CAP
SLOTS = PLACES + FACES * CAP
TABLE = SLOTS + 2 * CAP + 2 * SEND
PAIRS = [(a, b) for a in range(5) for b in range(a, 5) if b > 0]
PAIR_LANE = {pair: at for at, pair in enumerate(PAIRS)}
LANES_PER_SIDE = 16


def vector_shape(count, dtype):
    return jax.ShapeDtypeStruct((count, 8, ROWS), dtype)


def params(mebibytes=16):
    return pltpu.CompilerParams(vmem_limit_bytes=mebibytes << 20)


def pack(slot_of, rounded, up, down, next_row, last_row):
    for target, directions in (
        (up, UP_DIRECTIONS),
        (down, DOWN_DIRECTIONS),
        (next_row, (7,)),
        (last_row, (1,)),
    ):
        for at, direction in enumerate(directions):
            for k in range(SEND):
                target[at * SEND + k] = rounded[slot_of(direction, k)]


def listed(send_slots):
    return lambda direction, k: jnp.maximum(send_slots[direction, 0, k], 0)


def planned(table):
    return lambda direction, k: table[SLOTS + direction * SEND + k]


def start_kernel(
    send_slots, counts, right_sides, basis, rounded, up, down, next_row, last_row
):
    element = lax.broadcasted_iota(jnp.int32, basis.shape, 0)
    live = jnp.where(element < counts[0], right_sides[...], 0.0)
    basis[...] = live
    rounded[...] = live.astype(jnp.bfloat16)
    pack(listed(send_slots), rounded, up, down, next_row, last_row)


def plan_kernel(neighbours, send_slots, table, done):
    local = jnp.int32(0)
    for e in range(CAP):
        at = [neighbours[f, e] for f in range(FACES)]
        farthest = jnp.maximum(jnp.maximum(at[0], at[1]), jnp.maximum(at[2], at[3]))
        ghost = farthest >= CAP
        place = jnp.where(ghost, CAP - 1 - (e - local), local)
        table[place] = e
        for f in range(FACES):
            table[PLACES + f * CAP + place] = jnp.where(at[f] < 0, NOTHING, at[f])
        local = local + jnp.where(ghost, 0, 1)
    table[LOCAL_RUNS] = local // UNROLL
    for direction in range(9):
        for k in range(SEND):
            slot = listed(send_slots)(direction, k)
            table[SLOTS + direction * SEND + k] = slot
    done[...] = jnp.zeros_like(done)


def fetching(first, diag, face, diag_here, face_here, arrived):
    there = pl.ds(first, diag_here.shape[0])
    return (
        pltpu.make_async_copy(diag.at[there], diag_here, arrived.at[0]),
        pltpu.make_async_copy(face.at[there], face_here, arrived.at[1]),
    )


def transpose_some(first, diag_here, face_here, turned, also=lambda at: None):
    def element(at, carry):
        e = first + at
        turned[e, 0:ROWS] = diag_here[at].T
        for f in range(FACES):
            turned[e, (f + 1) * ROWS : (f + 2) * ROWS] = face_here[at, f].T
        also(at)
        return carry

    lax.fori_loop(0, diag_here.shape[0], element, 0, unroll=8)


def first_half_kernel(
    diag, face, turned, diag_third, face_third, done, diag_here, face_here, arrived
):
    parts = []
    for at in range(0, 2 * QUARTER, EIGHTH):
        here = pl.ds(at, EIGHTH)
        place = diag_here.at[here], face_here.at[here]
        parts.append((at, place, fetching(at, diag, face, *place, arrived.at[at // EIGHTH])))
    third = fetching(2 * QUARTER, diag, face, diag_third, face_third, arrived.at[4])
    for _, _, copies in parts:
        for copy in copies:
            copy.start()
    for copy in third:
        copy.start()
    for at, place, copies in parts:
        for copy in copies:
            copy.wait()
        transpose_some(at, *place, turned)
    done[...] = jnp.zeros_like(done)
    for copy in third:
        copy.wait()


def second_half_kernel(
    neighbours, diag, face, diag_third, face_third, rounded, before, turned, image,
    image_rounded, ghostly, diag_here, face_here, arrived, lookup,
):
    fourth = fetching(3 * QUARTER, diag, face, diag_here, face_here, arrived)
    for copy in fourth:
        copy.start()
    fill_local(lookup, rounded)

    def apply_from(first, diag_of, face_of):
        def apply(at):
            e = first + at
            vectors = [lookup[e]]
            for f in range(FACES):
                near = neighbours[f, e]
                vectors.append(
                    lookup[jnp.where((near < 0) | (near >= CAP), NOTHING, near)]
                )
            blocks = [diag_of[at]] + [face_of[at, f] for f in range(FACES)]
            out = lax.dot_general(
                jnp.concatenate(vectors, axis=1),
                jnp.concatenate(blocks, axis=1),
                (((1,), (1,)), ((), ())),
                preferred_element_type=jnp.float32,
            )
            image[e] = out
            image_rounded[e] = out.astype(jnp.bfloat16)

        return apply

    transpose_some(
        2 * QUARTER, diag_third, face_third, turned,
        apply_from(2 * QUARTER, diag_third, face_third),
    )
    for run in (2, 3):
        farthest = jnp.int32(-1)
        for e in range(run * UNROLL, (run + 1) * UNROLL):
            for f in range(FACES):
                farthest = jnp.maximum(farthest, neighbours[f, e])
        ghostly[run] = farthest
    for copy in fourth:
        copy.wait()
    transpose_some(
        3 * QUARTER, diag_here, face_here, turned,
        apply_from(3 * QUARTER, diag_here, face_here),
    )


def relay_kernel(*refs):
    from_down, from_up, next_row, last_row = refs[:4]
    send_next, send_last = refs[-2:]
    send_next[0:SEND] = from_up[2 * SEND : 3 * SEND]
    send_next[SEND : 2 * SEND] = next_row[...]
    send_next[2 * SEND : 3 * SEND] = from_down[2 * SEND : 3 * SEND]
    send_last[0:SEND] = from_up[0:SEND]
    send_last[SEND : 2 * SEND] = last_row[...]
    send_last[2 * SEND : 3 * SEND] = from_down[0:SEND]


def fill_local(lookup, rounded):
    lookup[0:CAP] = rounded[...]
    lookup[NOTHING : NOTHING + SEND] = jnp.zeros((SEND, 8, ROWS), jnp.bfloat16)


def fill_ghosts(lookup, from_down, from_up, from_last, from_next):
    lookup[CAP : CAP + 3 * SEND] = from_next[...]
    lookup[CAP + 3 * SEND : CAP + 4 * SEND] = from_up[SEND : 2 * SEND]
    lookup[CAP + 5 * SEND : CAP + 6 * SEND] = from_down[SEND : 2 * SEND]
    lookup[CAP + 6 * SEND : CAP + 9 * SEND] = from_last[...]


def apply_runs(first, limit, find, turned, lookup, basis, image, image_rounded):
    def near(found):
        vectors = jnp.concatenate([lookup[at] for at in found], axis=1)
        return vectors.astype(jnp.float32)

    def two(found, sums):
        elements = [places[0] for places in found]
        both = jnp.dot(
            jnp.concatenate([near(f) for f in found], axis=0).astype(jnp.bfloat16),
            jnp.concatenate([turned[e] for e in elements], axis=1),
            preferred_element_type=jnp.float32,
        )
        for at, e in enumerate(elements):
            out = both[8 * at : 8 * at + 8, ROWS * at : ROWS * at + ROWS]
            image[e] = out
            image_rounded[e] = out.astype(jnp.bfloat16)
            others = [ref[e] for ref in basis] + [out]
            sums = tuple(s + out * other for s, other in zip(sums, others))
        return sums

    def run(step, sums):
        for u in range(0, UNROLL, 2):
            at = step * UNROLL + u
            sums = two([find(at), find(at + 1)], sums)
        return sums

    zero = jnp.zeros((8, ROWS), jnp.float32)
    return lax.fori_loop(first, limit, run, (zero,) * (len(basis) + 1))


def with_sums(gram, sums):
    lane = lax.broadcasted_iota(jnp.int32, (8, ROWS), 1)
    newest = len(sums) - 1
    for a, s in enumerate(sums):
        total = jnp.sum(s, axis=1, keepdims=True)
        gram = gram + jnp.where(lane == PAIR_LANE[a, newest], total, 0.0)
    return gram


def whole_kernel(
    neighbours, send_slots, ghostly, turned, rounded, from_down, from_up, from_last,
    from_next, b0, before, before_rounded, image, image_rounded, up, down, next_row,
    last_row, gram_out, lookup,
):
    fill_local(lookup, rounded)
    fill_ghosts(lookup, from_down, from_up, from_last, from_next)

    def find(e):
        at = [neighbours[f, e] for f in range(FACES)]
        return [e] + [jnp.where(a < 0, NOTHING, a) for a in at]

    def again(first, limit):
        apply_runs(first, limit, find, turned, lookup, (), image, image_rounded)

    again(0, 2)
    for run in (2, 3):
        pl.when(ghostly[run] >= CAP)(functools.partial(again, run, run + 1))
    pack(listed(send_slots), image_rounded, up, down, next_row, last_row)

    def products(step, sums):
        for u in range(UNROLL):
            out = image[step * UNROLL + u]
            sums = sums[0] + b0[step * UNROLL + u] * out, sums[1] + out * out
        return sums

    zero = jnp.zeros((8, ROWS), jnp.float32)
    sums = lax.fori_loop(0, CAP // UNROLL, products, (zero, zero))
    gram_out[...] = with_sums(zero, sums)


def find_in(table):
    return lambda at: [table[at]] + [table[PLACES + f * CAP + at] for f in range(FACES)]


def local_kernel(power, *refs):
    table, turned, rounded, gram_in = refs[:4]
    basis = refs[4 : 5 + power]
    image, image_rounded, gram_out, lookup = refs[5 + power :]
    fill_local(lookup, rounded)
    sums = apply_runs(
        0, table[LOCAL_RUNS], find_in(table), turned, lookup, basis, image, image_rounded
    )
    gram_out[...] = with_sums(gram_in[...], sums)


def ghost_kernel(power, *refs):
    table, turned, rounded = refs[:3]
    received = refs[3:7]
    gram_in = refs[7]
    basis = refs[8 : 9 + power]
    refs = refs[11 + power :]
    last = power == POWERS - 1
    if last:
        image, image_rounded, gram_out, lookup = refs
    else:
        image, image_rounded, up, down, next_row, last_row, gram_out, lookup = refs
    fill_local(lookup, rounded)
    fill_ghosts(lookup, *received)
    sums = apply_runs(
        table[LOCAL_RUNS], CAP // UNROLL, find_in(table), turned, lookup, basis, image,
        image_rounded,
    )
    if not last:
        pack(planned(table), image_rounded, up, down, next_row, last_row)
    gram = with_sums(gram_in[...], sums)
    if last:
        lane = lax.broadcasted_iota(jnp.int32, (8, ROWS), 1)
        side = lax.broadcasted_iota(jnp.int32, (8, ROWS), 0)
        spread = jnp.zeros((8, ROWS), jnp.float32)
        for at in range(len(PAIRS)):
            value = jnp.broadcast_to(gram[:, at : at + 1], (8, ROWS))
            spread = jnp.where(lane == side * LANES_PER_SIDE + at, value, spread)
        row = jnp.sum(spread, axis=0, keepdims=True)
        gram_out[...] = jnp.broadcast_to(row, gram_out.shape)
    else:
        gram_out[...] = gram


def finish_kernel(gram_rows, b0, b1, b2, b3, b4, solution, residual):
    lane = lax.broadcasted_iota(jnp.int32, (8, ROWS), 1)
    side = lax.broadcasted_iota(jnp.int32, (8, ROWS), 0)
    row = jnp.sum(gram_rows[...], axis=0, keepdims=True)
    spread = jnp.broadcast_to(row, (8, ROWS))

    def entry(a, b):
        at = PAIR_LANE[min(a, b), max(a, b)]
        mine = jnp.where(lane == side * LANES_PER_SIDE + at, spread, 0.0)
        total = jnp.sum(mine, axis=1, keepdims=True)
        return jnp.broadcast_to(total, (8, ROWS))

    factor = {}
    inverse = []
    for i in range(POWERS):
        for j in range(i + 1):
            value = entry(i + 1, j + 1)
            for k in range(j):
                value = value - factor[i, k] * factor[j, k]
            if i == j:
                inverse.append(1.0 / jnp.sqrt(value))
            else:
                factor[i, j] = value * inverse[j]
    forward = []
    for i in range(POWERS):
        value = entry(0, i + 1)
        for k in range(i):
            value = value - factor[i, k] * forward[k]
        forward.append(value * inverse[i])
    weights = [None] * POWERS
    for i in reversed(range(POWERS)):
        value = forward[i]
        for k in range(i + 1, POWERS):
            value = value - factor[k, i] * weights[k]
        weights[i] = value * inverse[i]
    basis = (b0, b1, b2, b3, b4)

    def several(step, carry):
        for u in range(8):
            e = step * 8 + u
            v = [ref[e] for ref in basis]
            total = weights[0] * v[0]
            moved = weights[0] * v[1]
            for k in range(1, POWERS):
                total = total + weights[k] * v[k]
                moved = moved + weights[k] * v[k + 1]
            solution[e] = total
            residual[e] = v[0] - moved
        return carry

    lax.fori_loop(0, CAP // 8, several, 0)


def shifted(block, axis, distance):
    return lax.ppermute(block, axis, [(i, (i + distance) % SIDE) for i in range(SIDE)])


def per_device(right_sides, diag_blocks, face_blocks, neighbours, send_slots, counts):
    half = jnp.bfloat16
    neighbours = neighbours.T
    send_slots = send_slots.transpose(1, 0, 2)
    in_place = lambda array: pltpu.with_memory_space_constraint(array, pltpu.HBM)
    diag_blocks = in_place(diag_blocks)
    face_blocks = in_place(face_blocks)
    packets = [vector_shape(n * SEND, half) for n in (3, 3, 1, 1)]
    full = vector_shape(CAP, jnp.float32)
    narrow = vector_shape(CAP, half)
    gram_shape = jax.ShapeDtypeStruct((8, ROWS), jnp.float32)
    rows_shape = jax.ShapeDtypeStruct((GROUPS, ROWS), jnp.float32)
    turned_shape = pltpu.VMEM((CAP, BLOCKS * ROWS, ROWS), half)
    lookup = pltpu.VMEM((LOOKUP, 8, ROWS), half)
    quarter = [
        pltpu.VMEM((QUARTER, ROWS, ROWS), half),
        pltpu.VMEM((QUARTER, FACES, ROWS, ROWS), half),
    ]
    arrived = pltpu.SemaphoreType.DMA((2,))
    first, rounded, up, down, next_row, last_row = pl.pallas_call(
        start_kernel,
        name="start",
        in_specs=[IN_SMEM, IN_SMEM, IN_VMEM],
        out_specs=[IN_VMEM] * 6,
        out_shape=[full, narrow] + packets,
        compiler_params=params(),
    )(in_place(send_slots), counts, in_place(right_sides))
    basis = [first]
    gram = None
    for power in range(POWERS):
        last = power == POWERS - 1
        from_down = shifted(up, "gy", 1)
        from_up = shifted(down, "gy", -1)
        after = ()
        if power == 0:
            turned, *blocks, done = pl.pallas_call(
                first_half_kernel,
                name="first_half",
                in_specs=[IN_HBM] * 2,
                out_specs=[IN_VMEM] * 4,
                out_shape=[turned_shape] + quarter + [gram_shape],
                scratch_shapes=[
                    pltpu.VMEM((2 * QUARTER, ROWS, ROWS), half),
                    pltpu.VMEM((2 * QUARTER, FACES, ROWS, ROWS), half),
                    pltpu.SemaphoreType.DMA((5, 2)),
                ],
                compiler_params=params(),
            )(diag_blocks, face_blocks)
            after = (done,)
        elif power == 1:
            table, done = pl.pallas_call(
                plan_kernel,
                name="plan",
                in_specs=[IN_SMEM] * 2,
                out_specs=[IN_SMEM, IN_VMEM],
                out_shape=[pltpu.SMEM((TABLE,), jnp.int32), gram_shape],
                compiler_params=params(),
            )(neighbours, send_slots)
            after = (done,)
        if power > 0:
            image, image_rounded, gram = pl.pallas_call(
                functools.partial(local_kernel, power),
                name=f"local{power}",
                in_specs=[IN_SMEM] + [IN_VMEM] * (4 + power),
                out_specs=[IN_VMEM] * 3,
                out_shape=[full, narrow, gram_shape],
                scratch_shapes=[lookup],
                compiler_params=params(),
            )(table, turned, rounded, gram, *basis)
            after = (gram,)
        send_next, send_last = pl.pallas_call(
            relay_kernel,
            name="relay",
            in_specs=[IN_VMEM] * 4 + [ANYWHERE] * len(after),
            out_specs=[IN_VMEM] * 2,
            out_shape=[vector_shape(3 * SEND, half)] * 2,
            compiler_params=params(),
        )(from_down, from_up, next_row, last_row, *after)
        from_last = shifted(send_next, "gx", 1)
        from_next = shifted(send_last, "gx", -1)
        received = (from_down, from_up, from_last, from_next)
        if power == 0:
            turned, image, image_rounded, ghostly = pl.pallas_call(
                second_half_kernel,
                name="second_half",
                in_specs=[IN_SMEM] + [IN_HBM] * 2 + [IN_VMEM] * 4,
                out_specs=[IN_VMEM] * 3 + [IN_SMEM],
                out_shape=[turned_shape, full, narrow, pltpu.SMEM((8,), jnp.int32)],
                scratch_shapes=quarter + [arrived, lookup],
                input_output_aliases={6: 0},
                compiler_params=params(),
            )(neighbours, diag_blocks, face_blocks, *blocks, rounded, turned)
            outs = pl.pallas_call(
                whole_kernel,
                name="whole",
                in_specs=[IN_SMEM] * 3 + [IN_VMEM] * 9,
                out_specs=[IN_VMEM] * 7,
                out_shape=[full, narrow] + packets + [gram_shape],
                scratch_shapes=[lookup],
                input_output_aliases={10: 0, 11: 1},
                compiler_params=params(),
            )(
                neighbours, send_slots, ghostly, turned, rounded, *received, first,
                image, image_rounded,
            )
        else:
            shapes = [full, narrow] + ([rows_shape] if last else packets + [gram_shape])
            outs = pl.pallas_call(
                functools.partial(ghost_kernel, power),
                name=f"ghost{power}",
                in_specs=[IN_SMEM] + [IN_VMEM] * (10 + power),
                out_specs=[IN_VMEM] * len(shapes),
                out_shape=shapes,
                scratch_shapes=[lookup],
                input_output_aliases={9 + power: 0, 10 + power: 1},
                compiler_params=params(),
            )(
                table, turned, rounded, *received, gram, *basis, image, image_rounded,
            )
        basis.append(outs[0])
        rounded = outs[1]
        gram = outs[-1]
        if not last:
            up, down, next_row, last_row = outs[2:-1]
    gathered = lax.all_to_all(gram, ("gx", "gy"), 0, 0, tiled=True)
    return pl.pallas_call(
        finish_kernel,
        name="finish",
        in_specs=[IN_VMEM] * 6,
        out_specs=[IN_VMEM] * 2,
        out_shape=[full] * 2,
        compiler_params=params(),
    )(gathered, *basis)


def solution(mesh):
    in_specs = (
        P(("gx", "gy"), None, None),
        P(("gx", "gy"), None, None),
        P(("gx", "gy"), None, None, None),
        P(("gx", "gy"), None),
        P(("gx", "gy"), None, None),
        P(("gx", "gy")),
    )
    out_specs = (P(("gx", "gy"), None, None), P(("gx", "gy"), None, None))
    return jax.shard_map(
        per_device, mesh=mesh, in_specs=in_specs, out_specs=out_specs, check_vma=False
    )
```

```python
import functools

import jax
import jax.numpy as jnp
from jax import lax
from jax.experimental import pallas as pl
from jax.experimental.pallas import tpu as pltpu
from jax.sharding import PartitionSpec as P

POWERS = 4
CAP = 64
SEND = 16
FACES = 4
SIDE = 16
GROUPS = SIDE * SIDE
ROWS = 128
LOOKUP = CAP + 9 * SEND
NOTHING = CAP + 4 * SEND
UNROLL = 16
BLOCKS = FACES + 1
QUARTER = CAP // 4
EIGHTH = CAP // 8

IN_VMEM = pl.BlockSpec(memory_space=pltpu.VMEM)
IN_SMEM = pl.BlockSpec(memory_space=pltpu.SMEM)
ANYWHERE = pl.BlockSpec(memory_space=pl.ANY)
IN_HBM = pl.BlockSpec(memory_space=pltpu.HBM)
UP_DIRECTIONS = (2, 5, 8)
DOWN_DIRECTIONS = (0, 3, 6)
LOCAL_RUNS = CAP
PLACES = 2 * CAP
SLOTS = PLACES + FACES * CAP
TABLE = SLOTS + 2 * CAP + 2 * SEND
PAIRS = [(a, b) for a in range(5) for b in range(a, 5) if b > 0]
PAIR_LANE = {pair: at for at, pair in enumerate(PAIRS)}
LANES_PER_SIDE = 16


def vector_shape(count, dtype):
    return jax.ShapeDtypeStruct((count, 8, ROWS), dtype)


def params(mebibytes=16):
    return pltpu.CompilerParams(vmem_limit_bytes=mebibytes << 20)


def pack(slot_of, rounded, up, down, next_row, last_row):
    for target, directions in (
        (up, UP_DIRECTIONS),
        (down, DOWN_DIRECTIONS),
        (next_row, (7,)),
        (last_row, (1,)),
    ):
        for at, direction in enumerate(directions):
            for k in range(SEND):
                target[at * SEND + k] = rounded[slot_of(direction, k)]


def listed(send_slots):
    return lambda direction, k: jnp.maximum(send_slots[direction, 0, k], 0)


def planned(table):
    return lambda direction, k: table[SLOTS + direction * SEND + k]


def start_kernel(
    neighbours_from, slots_from, counts, right_sides, basis, rounded, up, down,
    next_row, last_row, neighbours, send_slots, arrived,
):
    tables = (
        pltpu.make_async_copy(slots_from, send_slots, arrived.at[0]),
        pltpu.make_async_copy(neighbours_from, neighbours, arrived.at[1]),
    )
    for copy in tables:
        copy.start()
    element = lax.broadcasted_iota(jnp.int32, basis.shape, 0)
    live = jnp.where(element < counts[0], right_sides[...], 0.0)
    basis[...] = live
    rounded[...] = live.astype(jnp.bfloat16)
    for copy in tables:
        copy.wait()
    pack(listed(send_slots), rounded, up, down, next_row, last_row)


def plan_kernel(neighbours, send_slots, table, done):
    local = jnp.int32(0)
    for e in range(CAP):
        at = [neighbours[f, e] for f in range(FACES)]
        farthest = jnp.maximum(jnp.maximum(at[0], at[1]), jnp.maximum(at[2], at[3]))
        ghost = farthest >= CAP
        place = jnp.where(ghost, CAP - 1 - (e - local), local)
        table[place] = e
        for f in range(FACES):
            table[PLACES + f * CAP + place] = jnp.where(at[f] < 0, NOTHING, at[f])
        local = local + jnp.where(ghost, 0, 1)
    table[LOCAL_RUNS] = local // UNROLL
    for direction in range(9):
        for k in range(SEND):
            slot = listed(send_slots)(direction, k)
            table[SLOTS + direction * SEND + k] = slot
    done[...] = jnp.zeros_like(done)


def fetching(first, diag, face, diag_here, face_here, arrived):
    there = pl.ds(first, diag_here.shape[0])
    return (
        pltpu.make_async_copy(diag.at[there], diag_here, arrived.at[0]),
        pltpu.make_async_copy(face.at[there], face_here, arrived.at[1]),
    )


def transpose_some(first, diag_here, face_here, turned, also=lambda at: None):
    def element(at, carry):
        e = first + at
        turned[e, 0:ROWS] = diag_here[at].T
        for f in range(FACES):
            turned[e, (f + 1) * ROWS : (f + 2) * ROWS] = face_here[at, f].T
        also(at)
        return carry

    lax.fori_loop(0, diag_here.shape[0], element, 0, unroll=8)


def first_half_kernel(
    diag, face, turned, diag_third, face_third, done, diag_here, face_here, arrived
):
    parts = []
    for at in range(0, 2 * QUARTER, EIGHTH):
        here = pl.ds(at, EIGHTH)
        place = diag_here.at[here], face_here.at[here]
        parts.append((at, place, fetching(at, diag, face, *place, arrived.at[at // EIGHTH])))
    third = fetching(2 * QUARTER, diag, face, diag_third, face_third, arrived.at[4])
    for _, _, copies in parts:
        for copy in copies:
            copy.start()
    for copy in third:
        copy.start()
    for at, place, copies in parts:
        for copy in copies:
            copy.wait()
        transpose_some(at, *place, turned)
    done[...] = jnp.zeros_like(done)
    for copy in third:
        copy.wait()


def second_half_kernel(
    neighbours, diag, face, diag_third, face_third, rounded, before, turned, image,
    image_rounded, ghostly, diag_here, face_here, arrived, lookup,
):
    fourth = fetching(3 * QUARTER, diag, face, diag_here, face_here, arrived)
    for copy in fourth:
        copy.start()
    fill_local(lookup, rounded)

    def apply_from(first, diag_of, face_of):
        def apply(at):
            e = first + at
            vectors = [lookup[e]]
            for f in range(FACES):
                near = neighbours[f, e]
                vectors.append(
                    lookup[jnp.where((near < 0) | (near >= CAP), NOTHING, near)]
                )
            blocks = [diag_of[at]] + [face_of[at, f] for f in range(FACES)]
            out = lax.dot_general(
                jnp.concatenate(vectors, axis=1),
                jnp.concatenate(blocks, axis=1),
                (((1,), (1,)), ((), ())),
                preferred_element_type=jnp.float32,
            )
            image[e] = out
            image_rounded[e] = out.astype(jnp.bfloat16)

        return apply

    transpose_some(
        2 * QUARTER, diag_third, face_third, turned,
        apply_from(2 * QUARTER, diag_third, face_third),
    )
    for run in (2, 3):
        farthest = jnp.int32(-1)
        for e in range(run * UNROLL, (run + 1) * UNROLL):
            for f in range(FACES):
                farthest = jnp.maximum(farthest, neighbours[f, e])
        ghostly[run] = farthest
    for copy in fourth:
        copy.wait()
    transpose_some(
        3 * QUARTER, diag_here, face_here, turned,
        apply_from(3 * QUARTER, diag_here, face_here),
    )


def relay_kernel(*refs):
    from_down, from_up, next_row, last_row = refs[:4]
    send_next, send_last = refs[-2:]
    send_next[0:SEND] = from_up[2 * SEND : 3 * SEND]
    send_next[SEND : 2 * SEND] = next_row[...]
    send_next[2 * SEND : 3 * SEND] = from_down[2 * SEND : 3 * SEND]
    send_last[0:SEND] = from_up[0:SEND]
    send_last[SEND : 2 * SEND] = last_row[...]
    send_last[2 * SEND : 3 * SEND] = from_down[0:SEND]


def fill_local(lookup, rounded):
    lookup[0:CAP] = rounded[...]
    lookup[NOTHING : NOTHING + SEND] = jnp.zeros((SEND, 8, ROWS), jnp.bfloat16)


def fill_ghosts(lookup, from_down, from_up, from_last, from_next):
    lookup[CAP : CAP + 3 * SEND] = from_next[...]
    lookup[CAP + 3 * SEND : CAP + 4 * SEND] = from_up[SEND : 2 * SEND]
    lookup[CAP + 5 * SEND : CAP + 6 * SEND] = from_down[SEND : 2 * SEND]
    lookup[CAP + 6 * SEND : CAP + 9 * SEND] = from_last[...]


def apply_runs(first, limit, find, turned, lookup, basis, image, image_rounded):
    def near(found):
        vectors = jnp.concatenate([lookup[at] for at in found], axis=1)
        return vectors.astype(jnp.float32)

    def two(found, sums):
        elements = [places[0] for places in found]
        both = jnp.dot(
            jnp.concatenate([near(f) for f in found], axis=0).astype(jnp.bfloat16),
            jnp.concatenate([turned[e] for e in elements], axis=1),
            preferred_element_type=jnp.float32,
        )
        for at, e in enumerate(elements):
            out = both[8 * at : 8 * at + 8, ROWS * at : ROWS * at + ROWS]
            image[e] = out
            image_rounded[e] = out.astype(jnp.bfloat16)
            others = [ref[e] for ref in basis] + [out]
            sums = tuple(s + out * other for s, other in zip(sums, others))
        return sums

    def run(step, sums):
        for u in range(0, UNROLL, 2):
            at = step * UNROLL + u
            sums = two([find(at), find(at + 1)], sums)
        return sums

    zero = jnp.zeros((8, ROWS), jnp.float32)
    return lax.fori_loop(first, limit, run, (zero,) * (len(basis) + 1))


def with_sums(gram, sums):
    lane = lax.broadcasted_iota(jnp.int32, (8, ROWS), 1)
    newest = len(sums) - 1
    for a, s in enumerate(sums):
        total = jnp.sum(s, axis=1, keepdims=True)
        gram = gram + jnp.where(lane == PAIR_LANE[a, newest], total, 0.0)
    return gram


def whole_kernel(
    neighbours, send_slots, ghostly, turned, rounded, from_down, from_up, from_last,
    from_next, b0, before, before_rounded, image, image_rounded, up, down, next_row,
    last_row, gram_out, lookup,
):
    fill_local(lookup, rounded)
    fill_ghosts(lookup, from_down, from_up, from_last, from_next)

    def find(e):
        at = [neighbours[f, e] for f in range(FACES)]
        return [e] + [jnp.where(a < 0, NOTHING, a) for a in at]

    def again(first, limit):
        apply_runs(first, limit, find, turned, lookup, (), image, image_rounded)

    again(0, 2)
    for run in (2, 3):
        pl.when(ghostly[run] >= CAP)(functools.partial(again, run, run + 1))
    pack(listed(send_slots), image_rounded, up, down, next_row, last_row)

    def products(step, sums):
        for u in range(UNROLL):
            out = image[step * UNROLL + u]
            sums = sums[0] + b0[step * UNROLL + u] * out, sums[1] + out * out
        return sums

    zero = jnp.zeros((8, ROWS), jnp.float32)
    sums = lax.fori_loop(0, CAP // UNROLL, products, (zero, zero))
    gram_out[...] = with_sums(zero, sums)


def find_in(table):
    return lambda at: [table[at]] + [table[PLACES + f * CAP + at] for f in range(FACES)]


def local_kernel(power, *refs):
    table, turned, rounded, gram_in = refs[:4]
    basis = refs[4 : 5 + power]
    image, image_rounded, gram_out, lookup = refs[5 + power :]
    fill_local(lookup, rounded)
    sums = apply_runs(
        0, table[LOCAL_RUNS], find_in(table), turned, lookup, basis, image, image_rounded
    )
    gram_out[...] = with_sums(gram_in[...], sums)


def ghost_kernel(power, *refs):
    table, turned, rounded = refs[:3]
    received = refs[3:7]
    gram_in = refs[7]
    basis = refs[8 : 9 + power]
    refs = refs[11 + power :]
    last = power == POWERS - 1
    if last:
        image, image_rounded, gram_out, lookup = refs
    else:
        image, image_rounded, up, down, next_row, last_row, gram_out, lookup = refs
    fill_local(lookup, rounded)
    fill_ghosts(lookup, *received)
    sums = apply_runs(
        table[LOCAL_RUNS], CAP // UNROLL, find_in(table), turned, lookup, basis, image,
        image_rounded,
    )
    if not last:
        pack(planned(table), image_rounded, up, down, next_row, last_row)
    gram = with_sums(gram_in[...], sums)
    if last:
        lane = lax.broadcasted_iota(jnp.int32, (8, ROWS), 1)
        side = lax.broadcasted_iota(jnp.int32, (8, ROWS), 0)
        spread = jnp.zeros((8, ROWS), jnp.float32)
        for at in range(len(PAIRS)):
            value = jnp.broadcast_to(gram[:, at : at + 1], (8, ROWS))
            spread = jnp.where(lane == side * LANES_PER_SIDE + at, value, spread)
        row = jnp.sum(spread, axis=0, keepdims=True)
        gram_out[...] = jnp.broadcast_to(row, gram_out.shape)
    else:
        gram_out[...] = gram


def finish_kernel(
    gram_rows, b0, b1, b2, b3, b4, solution_out, residual_out, solution, residual, left
):
    lane = lax.broadcasted_iota(jnp.int32, (8, ROWS), 1)
    side = lax.broadcasted_iota(jnp.int32, (8, ROWS), 0)
    row = jnp.sum(gram_rows[...], axis=0, keepdims=True)
    spread = jnp.broadcast_to(row, (8, ROWS))

    def entry(a, b):
        at = PAIR_LANE[min(a, b), max(a, b)]
        mine = jnp.where(lane == side * LANES_PER_SIDE + at, spread, 0.0)
        total = jnp.sum(mine, axis=1, keepdims=True)
        return jnp.broadcast_to(total, (8, ROWS))

    factor = {}
    inverse = []
    for i in range(POWERS):
        for j in range(i + 1):
            value = entry(i + 1, j + 1)
            for k in range(j):
                value = value - factor[i, k] * factor[j, k]
            if i == j:
                inverse.append(1.0 / jnp.sqrt(value))
            else:
                factor[i, j] = value * inverse[j]
    forward = []
    for i in range(POWERS):
        value = entry(0, i + 1)
        for k in range(i):
            value = value - factor[i, k] * forward[k]
        forward.append(value * inverse[i])
    weights = [None] * POWERS
    for i in reversed(range(POWERS)):
        value = forward[i]
        for k in range(i + 1, POWERS):
            value = value - factor[k, i] * weights[k]
        weights[i] = value * inverse[i]
    basis = (b0, b1, b2, b3, b4)

    def several(step, carry):
        for u in range(8):
            e = step * 8 + u
            v = [ref[e] for ref in basis]
            total = weights[0] * v[0]
            moved = weights[0] * v[1]
            for k in range(1, POWERS):
                total = total + weights[k] * v[k]
                moved = moved + weights[k] * v[k + 1]
            solution[e] = total
            residual[e] = v[0] - moved
        return carry

    leaving = []
    for part in range(4):
        lax.fori_loop(part * QUARTER // 8, (part + 1) * QUARTER // 8, several, 0)
        rows = pl.ds(part * QUARTER, QUARTER)
        for at, (here, there) in enumerate(
            ((solution, solution_out), (residual, residual_out))
        ):
            copy = pltpu.make_async_copy(here.at[rows], there.at[rows], left.at[part, at])
            copy.start()
            leaving.append(copy)
    for copy in leaving:
        copy.wait()


def shifted(block, axis, distance):
    return lax.ppermute(block, axis, [(i, (i + distance) % SIDE) for i in range(SIDE)])


def per_device(right_sides, diag_blocks, face_blocks, neighbours, send_slots, counts):
    half = jnp.bfloat16
    neighbours = neighbours.T
    send_slots = send_slots.transpose(1, 0, 2)
    in_place = lambda array: pltpu.with_memory_space_constraint(array, pltpu.HBM)
    diag_blocks = in_place(diag_blocks)
    face_blocks = in_place(face_blocks)
    packets = [vector_shape(n * SEND, half) for n in (3, 3, 1, 1)]
    full = vector_shape(CAP, jnp.float32)
    narrow = vector_shape(CAP, half)
    gram_shape = jax.ShapeDtypeStruct((8, ROWS), jnp.float32)
    rows_shape = jax.ShapeDtypeStruct((GROUPS, ROWS), jnp.float32)
    turned_shape = pltpu.VMEM((CAP, BLOCKS * ROWS, ROWS), half)
    lookup = pltpu.VMEM((LOOKUP, 8, ROWS), half)
    quarter = [
        pltpu.VMEM((QUARTER, ROWS, ROWS), half),
        pltpu.VMEM((QUARTER, FACES, ROWS, ROWS), half),
    ]
    arrived = pltpu.SemaphoreType.DMA((2,))
    *outs, neighbours, send_slots = pl.pallas_call(
        start_kernel,
        name="start",
        in_specs=[IN_HBM, IN_HBM, IN_SMEM, IN_VMEM],
        out_specs=[IN_VMEM] * 6 + [IN_SMEM] * 2,
        out_shape=[full, narrow] + packets
        + [pltpu.SMEM(table.shape, jnp.int32) for table in (neighbours, send_slots)],
        scratch_shapes=[arrived],
        compiler_params=params(),
    )(in_place(neighbours), in_place(send_slots), counts, in_place(right_sides))
    first, rounded, up, down, next_row, last_row = outs
    basis = [first]
    gram = None
    for power in range(POWERS):
        last = power == POWERS - 1
        from_down = shifted(up, "gy", 1)
        from_up = shifted(down, "gy", -1)
        after = ()
        if power == 0:
            turned, *blocks, done = pl.pallas_call(
                first_half_kernel,
                name="first_half",
                in_specs=[IN_HBM] * 2,
                out_specs=[IN_VMEM] * 4,
                out_shape=[turned_shape] + quarter + [gram_shape],
                scratch_shapes=[
                    pltpu.VMEM((2 * QUARTER, ROWS, ROWS), half),
                    pltpu.VMEM((2 * QUARTER, FACES, ROWS, ROWS), half),
                    pltpu.SemaphoreType.DMA((5, 2)),
                ],
                compiler_params=params(),
            )(diag_blocks, face_blocks)
            after = (done,)
        elif power == 1:
            table, done = pl.pallas_call(
                plan_kernel,
                name="plan",
                in_specs=[IN_SMEM] * 2,
                out_specs=[IN_SMEM, IN_VMEM],
                out_shape=[pltpu.SMEM((TABLE,), jnp.int32), gram_shape],
                compiler_params=params(),
            )(neighbours, send_slots)
            after = (done,)
        if power > 0:
            image, image_rounded, gram = pl.pallas_call(
                functools.partial(local_kernel, power),
                name=f"local{power}",
                in_specs=[IN_SMEM] + [IN_VMEM] * (4 + power),
                out_specs=[IN_VMEM] * 3,
                out_shape=[full, narrow, gram_shape],
                scratch_shapes=[lookup],
                compiler_params=params(),
            )(table, turned, rounded, gram, *basis)
        send_next, send_last = pl.pallas_call(
            relay_kernel,
            name="relay",
            in_specs=[IN_VMEM] * 4 + [ANYWHERE] * len(after),
            out_specs=[IN_VMEM] * 2,
            out_shape=[vector_shape(3 * SEND, half)] * 2,
            compiler_params=params(),
        )(from_down, from_up, next_row, last_row, *after)
        from_last = shifted(send_next, "gx", 1)
        from_next = shifted(send_last, "gx", -1)
        received = (from_down, from_up, from_last, from_next)
        if power == 0:
            turned, image, image_rounded, ghostly = pl.pallas_call(
                second_half_kernel,
                name="second_half",
                in_specs=[IN_SMEM] + [IN_HBM] * 2 + [IN_VMEM] * 4,
                out_specs=[IN_VMEM] * 3 + [IN_SMEM],
                out_shape=[turned_shape, full, narrow, pltpu.SMEM((8,), jnp.int32)],
                scratch_shapes=quarter + [arrived, lookup],
                input_output_aliases={6: 0},
                compiler_params=params(),
            )(neighbours, diag_blocks, face_blocks, *blocks, rounded, turned)
            outs = pl.pallas_call(
                whole_kernel,
                name="whole",
                in_specs=[IN_SMEM] * 3 + [IN_VMEM] * 9,
                out_specs=[IN_VMEM] * 7,
                out_shape=[full, narrow] + packets + [gram_shape],
                scratch_shapes=[lookup],
                input_output_aliases={10: 0, 11: 1},
                compiler_params=params(),
            )(
                neighbours, send_slots, ghostly, turned, rounded, *received, first,
                image, image_rounded,
            )
        else:
            shapes = [full, narrow] + ([rows_shape] if last else packets + [gram_shape])
            outs = pl.pallas_call(
                functools.partial(ghost_kernel, power),
                name=f"ghost{power}",
                in_specs=[IN_SMEM] + [IN_VMEM] * (10 + power),
                out_specs=[IN_VMEM] * len(shapes),
                out_shape=shapes,
                scratch_shapes=[lookup],
                input_output_aliases={9 + power: 0, 10 + power: 1},
                compiler_params=params(),
            )(
                table, turned, rounded, *received, gram, *basis, image, image_rounded,
            )
        basis.append(outs[0])
        rounded = outs[1]
        gram = outs[-1]
        if not last:
            up, down, next_row, last_row = outs[2:-1]
    gathered = lax.all_to_all(gram, ("gx", "gy"), 0, 0, tiled=True)
    return pl.pallas_call(
        finish_kernel,
        name="finish",
        in_specs=[IN_VMEM] * 6,
        out_specs=[IN_HBM] * 2,
        out_shape=[full] * 2,
        scratch_shapes=[pltpu.VMEM((CAP, 8, ROWS), jnp.float32)] * 2
        + [pltpu.SemaphoreType.DMA((4, 2))],
        compiler_params=params(),
    )(gathered, *basis)


def solution(mesh):
    in_specs = (
        P(("gx", "gy"), None, None),
        P(("gx", "gy"), None, None),
        P(("gx", "gy"), None, None, None),
        P(("gx", "gy"), None),
        P(("gx", "gy"), None, None),
        P(("gx", "gy")),
    )
    out_specs = (P(("gx", "gy"), None, None), P(("gx", "gy"), None, None))
    return jax.shard_map(
        per_device, mesh=mesh, in_specs=in_specs, out_specs=out_specs, check_vma=False
    )
```

```python
import functools

import jax
import jax.numpy as jnp
from jax import lax
from jax.experimental import pallas as pl
from jax.experimental.pallas import tpu as pltpu
from jax.sharding import PartitionSpec as P

POWERS = 4
CAP = 64
SEND = 16
FACES = 4
SIDE = 16
GROUPS = SIDE * SIDE
ROWS = 128
LOOKUP = CAP + 9 * SEND
NOTHING = CAP + 4 * SEND
UNROLL = 16
BLOCKS = FACES + 1
QUARTER = CAP // 4
EIGHTH = CAP // 8

IN_VMEM = pl.BlockSpec(memory_space=pltpu.VMEM)
IN_SMEM = pl.BlockSpec(memory_space=pltpu.SMEM)
ANYWHERE = pl.BlockSpec(memory_space=pl.ANY)
IN_HBM = pl.BlockSpec(memory_space=pltpu.HBM)
UP_DIRECTIONS = (2, 5, 8)
DOWN_DIRECTIONS = (0, 3, 6)
LOCAL_RUNS = CAP
PLACES = 2 * CAP
SLOTS = PLACES + FACES * CAP
TABLE = SLOTS + 2 * CAP + 2 * SEND
PAIRS = [(a, b) for a in range(5) for b in range(a, 5) if b > 0]
PAIR_LANE = {pair: at for at, pair in enumerate(PAIRS)}
LANES_PER_SIDE = 16


def vector_shape(count, dtype):
    return jax.ShapeDtypeStruct((count, 8, ROWS), dtype)


def params(mebibytes=16):
    return pltpu.CompilerParams(vmem_limit_bytes=mebibytes << 20)


def pack(slot_of, rounded, up, down, next_row, last_row):
    for target, directions in (
        (up, UP_DIRECTIONS),
        (down, DOWN_DIRECTIONS),
        (next_row, (7,)),
        (last_row, (1,)),
    ):
        for at, direction in enumerate(directions):
            for k in range(SEND):
                target[at * SEND + k] = rounded[slot_of(direction, k)]


def listed(send_slots):
    return lambda direction, k: jnp.maximum(send_slots[direction, 0, k], 0)


def planned(table):
    return lambda direction, k: table[SLOTS + direction * SEND + k]


def start_kernel(
    neighbours_from, slots_from, counts, right_sides_from, basis, rounded, up, down,
    next_row, last_row, neighbours, send_slots, right_sides, arrived,
):
    vectors = pltpu.make_async_copy(right_sides_from, right_sides, arrived.at[2])
    tables = (
        pltpu.make_async_copy(slots_from, send_slots, arrived.at[0]),
        pltpu.make_async_copy(neighbours_from, neighbours, arrived.at[1]),
    )
    vectors.start()
    for copy in tables:
        copy.start()
    vectors.wait()
    element = lax.broadcasted_iota(jnp.int32, basis.shape, 0)
    live = jnp.where(element < counts[0], right_sides[...], 0.0)
    basis[...] = live
    rounded[...] = live.astype(jnp.bfloat16)
    for copy in tables:
        copy.wait()
    pack(listed(send_slots), rounded, up, down, next_row, last_row)


def plan_kernel(neighbours, send_slots, table, done):
    local = jnp.int32(0)
    for e in range(CAP):
        at = [neighbours[f, e] for f in range(FACES)]
        farthest = jnp.maximum(jnp.maximum(at[0], at[1]), jnp.maximum(at[2], at[3]))
        ghost = farthest >= CAP
        place = jnp.where(ghost, CAP - 1 - (e - local), local)
        table[place] = e
        for f in range(FACES):
            table[PLACES + f * CAP + place] = jnp.where(at[f] < 0, NOTHING, at[f])
        local = local + jnp.where(ghost, 0, 1)
    table[LOCAL_RUNS] = local // UNROLL
    for direction in range(9):
        for k in range(SEND):
            slot = listed(send_slots)(direction, k)
            table[SLOTS + direction * SEND + k] = slot
    done[...] = jnp.zeros_like(done)


def fetching(first, diag, face, diag_here, face_here, arrived):
    there = pl.ds(first, diag_here.shape[0])
    return (
        pltpu.make_async_copy(diag.at[there], diag_here, arrived.at[0]),
        pltpu.make_async_copy(face.at[there], face_here, arrived.at[1]),
    )


def transpose_some(first, diag_here, face_here, turned, also=lambda at: None):
    def element(at, carry):
        e = first + at
        turned[e, 0:ROWS] = diag_here[at].T
        for f in range(FACES):
            turned[e, (f + 1) * ROWS : (f + 2) * ROWS] = face_here[at, f].T
        also(at)
        return carry

    lax.fori_loop(0, diag_here.shape[0], element, 0, unroll=8)


def fetch_parts(first, count, diag, face, diag_here, face_here, arrived):
    parts = []
    for at in range(0, count, EIGHTH):
        here = pl.ds(at, EIGHTH)
        place = diag_here.at[here], face_here.at[here]
        copies = fetching(first + at, diag, face, *place, arrived.at[at // EIGHTH])
        parts.append((first + at, place, copies))
        for copy in copies:
            copy.start()
    return parts


def first_half_kernel(
    diag, face, turned, diag_next, face_next, done, diag_here, face_here, arrived
):
    parts = fetch_parts(0, CAP // 2, diag, face, diag_here, face_here, arrived)
    ahead = fetching(CAP // 2, diag, face, diag_next, face_next, arrived.at[4])
    for copy in ahead:
        copy.start()
    for at, place, copies in parts:
        for copy in copies:
            copy.wait()
        transpose_some(at, *place, turned)
    done[...] = jnp.zeros_like(done)
    for copy in ahead:
        copy.wait()


def second_half_kernel(
    neighbours, diag, face, diag_next, face_next, rounded, before, turned, image,
    image_rounded, ghostly, diag_here, face_here, arrived, lookup,
):
    parts = fetch_parts(
        CAP // 2 + EIGHTH, 3 * EIGHTH, diag, face, diag_here, face_here, arrived
    )
    fill_local(lookup, rounded)

    def apply_from(first, diag_of, face_of):
        def apply(at):
            e = first + at
            vectors = [lookup[e]]
            for f in range(FACES):
                near = neighbours[f, e]
                vectors.append(
                    lookup[jnp.where((near < 0) | (near >= CAP), NOTHING, near)]
                )
            blocks = [diag_of[at]] + [face_of[at, f] for f in range(FACES)]
            out = lax.dot_general(
                jnp.concatenate(vectors, axis=1),
                jnp.concatenate(blocks, axis=1),
                (((1,), (1,)), ((), ())),
                preferred_element_type=jnp.float32,
            )
            image[e] = out
            image_rounded[e] = out.astype(jnp.bfloat16)

        return apply

    place = diag_next, face_next
    transpose_some(CAP // 2, *place, turned, apply_from(CAP // 2, *place))
    for run in (2, 3):
        farthest = jnp.int32(-1)
        for e in range(run * UNROLL, (run + 1) * UNROLL):
            for f in range(FACES):
                farthest = jnp.maximum(farthest, neighbours[f, e])
        ghostly[run] = farthest
    for at, place, copies in parts:
        for copy in copies:
            copy.wait()
        transpose_some(at, *place, turned, apply_from(at, *place))


def relay_kernel(*refs):
    from_down, from_up, next_row, last_row = refs[:4]
    send_next, send_last = refs[-2:]
    send_next[0:SEND] = from_up[2 * SEND : 3 * SEND]
    send_next[SEND : 2 * SEND] = next_row[...]
    send_next[2 * SEND : 3 * SEND] = from_down[2 * SEND : 3 * SEND]
    send_last[0:SEND] = from_up[0:SEND]
    send_last[SEND : 2 * SEND] = last_row[...]
    send_last[2 * SEND : 3 * SEND] = from_down[0:SEND]


def fill_local(lookup, rounded):
    lookup[0:CAP] = rounded[...]
    lookup[NOTHING : NOTHING + SEND] = jnp.zeros((SEND, 8, ROWS), jnp.bfloat16)


def fill_ghosts(lookup, from_down, from_up, from_last, from_next):
    lookup[CAP : CAP + 3 * SEND] = from_next[...]
    lookup[CAP + 3 * SEND : CAP + 4 * SEND] = from_up[SEND : 2 * SEND]
    lookup[CAP + 5 * SEND : CAP + 6 * SEND] = from_down[SEND : 2 * SEND]
    lookup[CAP + 6 * SEND : CAP + 9 * SEND] = from_last[...]


def apply_runs(first, limit, find, turned, lookup, basis, image, image_rounded):
    def near(found):
        vectors = jnp.concatenate([lookup[at] for at in found], axis=1)
        return vectors.astype(jnp.float32)

    def two(found, sums):
        elements = [places[0] for places in found]
        both = jnp.dot(
            jnp.concatenate([near(f) for f in found], axis=0).astype(jnp.bfloat16),
            jnp.concatenate([turned[e] for e in elements], axis=1),
            preferred_element_type=jnp.float32,
        )
        for at, e in enumerate(elements):
            out = both[8 * at : 8 * at + 8, ROWS * at : ROWS * at + ROWS]
            image[e] = out
            image_rounded[e] = out.astype(jnp.bfloat16)
            others = [ref[e] for ref in basis] + [out]
            sums = tuple(s + out * other for s, other in zip(sums, others))
        return sums

    def run(step, sums):
        for u in range(0, UNROLL, 2):
            at = step * UNROLL + u
            sums = two([find(at), find(at + 1)], sums)
        return sums

    zero = jnp.zeros((8, ROWS), jnp.float32)
    return lax.fori_loop(first, limit, run, (zero,) * (len(basis) + 1))


def with_sums(gram, sums):
    lane = lax.broadcasted_iota(jnp.int32, (8, ROWS), 1)
    newest = len(sums) - 1
    for a, s in enumerate(sums):
        total = jnp.sum(s, axis=1, keepdims=True)
        gram = gram + jnp.where(lane == PAIR_LANE[a, newest], total, 0.0)
    return gram


def whole_kernel(
    neighbours, send_slots, ghostly, turned, rounded, from_down, from_up, from_last,
    from_next, b0, before, before_rounded, image, image_rounded, up, down, next_row,
    last_row, gram_out, lookup,
):
    fill_local(lookup, rounded)
    fill_ghosts(lookup, from_down, from_up, from_last, from_next)

    def find(e):
        at = [neighbours[f, e] for f in range(FACES)]
        return [e] + [jnp.where(a < 0, NOTHING, a) for a in at]

    def again(first, limit):
        apply_runs(first, limit, find, turned, lookup, (), image, image_rounded)

    again(0, 2)
    for run in (2, 3):
        pl.when(ghostly[run] >= CAP)(functools.partial(again, run, run + 1))
    pack(listed(send_slots), image_rounded, up, down, next_row, last_row)

    def products(step, sums):
        for u in range(UNROLL):
            out = image[step * UNROLL + u]
            sums = sums[0] + b0[step * UNROLL + u] * out, sums[1] + out * out
        return sums

    zero = jnp.zeros((8, ROWS), jnp.float32)
    sums = lax.fori_loop(0, CAP // UNROLL, products, (zero, zero))
    gram_out[...] = with_sums(zero, sums)


def find_in(table):
    return lambda at: [table[at]] + [table[PLACES + f * CAP + at] for f in range(FACES)]


def local_kernel(power, *refs):
    table, turned, rounded, gram_in = refs[:4]
    basis = refs[4 : 5 + power]
    image, image_rounded, gram_out, lookup = refs[5 + power :]
    fill_local(lookup, rounded)
    sums = apply_runs(
        0, table[LOCAL_RUNS], find_in(table), turned, lookup, basis, image, image_rounded
    )
    gram_out[...] = with_sums(gram_in[...], sums)


def ghost_kernel(power, *refs):
    table, turned, rounded = refs[:3]
    received = refs[3:7]
    gram_in = refs[7]
    basis = refs[8 : 9 + power]
    refs = refs[11 + power :]
    last = power == POWERS - 1
    if last:
        image, image_rounded, gram_out, lookup = refs
    else:
        image, image_rounded, up, down, next_row, last_row, gram_out, lookup = refs
    fill_local(lookup, rounded)
    fill_ghosts(lookup, *received)
    sums = apply_runs(
        table[LOCAL_RUNS], CAP // UNROLL, find_in(table), turned, lookup, basis, image,
        image_rounded,
    )
    if not last:
        pack(planned(table), image_rounded, up, down, next_row, last_row)
    gram = with_sums(gram_in[...], sums)
    if last:
        lane = lax.broadcasted_iota(jnp.int32, (8, ROWS), 1)
        side = lax.broadcasted_iota(jnp.int32, (8, ROWS), 0)
        spread = jnp.zeros((8, ROWS), jnp.float32)
        for at in range(len(PAIRS)):
            value = jnp.broadcast_to(gram[:, at : at + 1], (8, ROWS))
            spread = jnp.where(lane == side * LANES_PER_SIDE + at, value, spread)
        row = jnp.sum(spread, axis=0, keepdims=True)
        gram_out[...] = jnp.broadcast_to(row, gram_out.shape)
    else:
        gram_out[...] = gram


def finish_kernel(
    gram_rows, b0, b1, b2, b3, b4, solution_out, residual_out, solution, residual, left
):
    lane = lax.broadcasted_iota(jnp.int32, (8, ROWS), 1)
    side = lax.broadcasted_iota(jnp.int32, (8, ROWS), 0)
    row = jnp.sum(gram_rows[...], axis=0, keepdims=True)
    spread = jnp.broadcast_to(row, (8, ROWS))

    def entry(a, b):
        at = PAIR_LANE[min(a, b), max(a, b)]
        mine = jnp.where(lane == side * LANES_PER_SIDE + at, spread, 0.0)
        total = jnp.sum(mine, axis=1, keepdims=True)
        return jnp.broadcast_to(total, (8, ROWS))

    factor = {}
    inverse = []
    for i in range(POWERS):
        for j in range(i + 1):
            value = entry(i + 1, j + 1)
            for k in range(j):
                value = value - factor[i, k] * factor[j, k]
            if i == j:
                inverse.append(1.0 / jnp.sqrt(value))
            else:
                factor[i, j] = value * inverse[j]
    forward = []
    for i in range(POWERS):
        value = entry(0, i + 1)
        for k in range(i):
            value = value - factor[i, k] * forward[k]
        forward.append(value * inverse[i])
    weights = [None] * POWERS
    for i in reversed(range(POWERS)):
        value = forward[i]
        for k in range(i + 1, POWERS):
            value = value - factor[k, i] * weights[k]
        weights[i] = value * inverse[i]
    basis = (b0, b1, b2, b3, b4)

    def several(step, carry):
        for u in range(8):
            e = step * 8 + u
            v = [ref[e] for ref in basis]
            total = weights[0] * v[0]
            moved = weights[0] * v[1]
            for k in range(1, POWERS):
                total = total + weights[k] * v[k]
                moved = moved + weights[k] * v[k + 1]
            solution[e] = total
            residual[e] = v[0] - moved
        return carry

    leaving = []
    for part in range(4):
        lax.fori_loop(part * QUARTER // 8, (part + 1) * QUARTER // 8, several, 0)
        rows = pl.ds(part * QUARTER, QUARTER)
        for at, (here, there) in enumerate(
            ((solution, solution_out), (residual, residual_out))
        ):
            copy = pltpu.make_async_copy(here.at[rows], there.at[rows], left.at[part, at])
            copy.start()
            leaving.append(copy)
    for copy in leaving:
        copy.wait()


def shifted(block, axis, distance):
    return lax.ppermute(block, axis, [(i, (i + distance) % SIDE) for i in range(SIDE)])


def per_device(right_sides, diag_blocks, face_blocks, neighbours, send_slots, counts):
    half = jnp.bfloat16
    neighbours = neighbours.T
    send_slots = send_slots.transpose(1, 0, 2)
    in_place = lambda array: pltpu.with_memory_space_constraint(array, pltpu.HBM)
    diag_blocks = in_place(diag_blocks)
    face_blocks = in_place(face_blocks)
    packets = [vector_shape(n * SEND, half) for n in (3, 3, 1, 1)]
    full = vector_shape(CAP, jnp.float32)
    narrow = vector_shape(CAP, half)
    gram_shape = jax.ShapeDtypeStruct((8, ROWS), jnp.float32)
    rows_shape = jax.ShapeDtypeStruct((GROUPS, ROWS), jnp.float32)
    turned_shape = pltpu.VMEM((CAP, BLOCKS * ROWS, ROWS), half)
    lookup = pltpu.VMEM((LOOKUP, 8, ROWS), half)

    def room(count):
        return [
            pltpu.VMEM((count, ROWS, ROWS), half),
            pltpu.VMEM((count, FACES, ROWS, ROWS), half),
        ]

    *outs, neighbours, send_slots = pl.pallas_call(
        start_kernel,
        name="start",
        in_specs=[IN_HBM, IN_HBM, IN_SMEM, IN_HBM],
        out_specs=[IN_VMEM] * 6 + [IN_SMEM] * 2,
        out_shape=[full, narrow] + packets
        + [pltpu.SMEM(table.shape, jnp.int32) for table in (neighbours, send_slots)],
        scratch_shapes=[
            pltpu.VMEM(right_sides.shape, jnp.float32),
            pltpu.SemaphoreType.DMA((3,)),
        ],
        compiler_params=params(),
    )(in_place(neighbours), in_place(send_slots), counts, in_place(right_sides))
    first, rounded, up, down, next_row, last_row = outs
    basis = [first]
    gram = None
    for power in range(POWERS):
        last = power == POWERS - 1
        from_down = shifted(up, "gy", 1)
        from_up = shifted(down, "gy", -1)
        after = ()
        if power == 0:
            turned, *blocks, done = pl.pallas_call(
                first_half_kernel,
                name="first_half",
                in_specs=[IN_HBM] * 2,
                out_specs=[IN_VMEM] * 4,
                out_shape=[turned_shape] + room(EIGHTH) + [gram_shape],
                scratch_shapes=room(CAP // 2) + [pltpu.SemaphoreType.DMA((5, 2))],
                compiler_params=params(),
            )(diag_blocks, face_blocks)
            after = (done,)
        elif power == 1:
            table, done = pl.pallas_call(
                plan_kernel,
                name="plan",
                in_specs=[IN_SMEM] * 2,
                out_specs=[IN_SMEM, IN_VMEM],
                out_shape=[pltpu.SMEM((TABLE,), jnp.int32), gram_shape],
                compiler_params=params(),
            )(neighbours, send_slots)
            after = (done,)
        if power > 0:
            image, image_rounded, gram = pl.pallas_call(
                functools.partial(local_kernel, power),
                name=f"local{power}",
                in_specs=[IN_SMEM] + [IN_VMEM] * (4 + power),
                out_specs=[IN_VMEM] * 3,
                out_shape=[full, narrow, gram_shape],
                scratch_shapes=[lookup],
                compiler_params=params(),
            )(table, turned, rounded, gram, *basis)
        send_next, send_last = pl.pallas_call(
            relay_kernel,
            name="relay",
            in_specs=[IN_VMEM] * 4 + [ANYWHERE] * len(after),
            out_specs=[IN_VMEM] * 2,
            out_shape=[vector_shape(3 * SEND, half)] * 2,
            compiler_params=params(),
        )(from_down, from_up, next_row, last_row, *after)
        from_last = shifted(send_next, "gx", 1)
        from_next = shifted(send_last, "gx", -1)
        received = (from_down, from_up, from_last, from_next)
        if power == 0:
            turned, image, image_rounded, ghostly = pl.pallas_call(
                second_half_kernel,
                name="second_half",
                in_specs=[IN_SMEM] + [IN_HBM] * 2 + [IN_VMEM] * 4,
                out_specs=[IN_VMEM] * 3 + [IN_SMEM],
                out_shape=[turned_shape, full, narrow, pltpu.SMEM((8,), jnp.int32)],
                scratch_shapes=room(3 * EIGHTH)
                + [pltpu.SemaphoreType.DMA((3, 2)), lookup],
                input_output_aliases={6: 0},
                compiler_params=params(),
            )(neighbours, diag_blocks, face_blocks, *blocks, rounded, turned)
            outs = pl.pallas_call(
                whole_kernel,
                name="whole",
                in_specs=[IN_SMEM] * 3 + [IN_VMEM] * 9,
                out_specs=[IN_VMEM] * 7,
                out_shape=[full, narrow] + packets + [gram_shape],
                scratch_shapes=[lookup],
                input_output_aliases={10: 0, 11: 1},
                compiler_params=params(),
            )(
                neighbours, send_slots, ghostly, turned, rounded, *received, first,
                image, image_rounded,
            )
        else:
            shapes = [full, narrow] + ([rows_shape] if last else packets + [gram_shape])
            outs = pl.pallas_call(
                functools.partial(ghost_kernel, power),
                name=f"ghost{power}",
                in_specs=[IN_SMEM] + [IN_VMEM] * (10 + power),
                out_specs=[IN_VMEM] * len(shapes),
                out_shape=shapes,
                scratch_shapes=[lookup],
                input_output_aliases={9 + power: 0, 10 + power: 1},
                compiler_params=params(),
            )(
                table, turned, rounded, *received, gram, *basis, image, image_rounded,
            )
        basis.append(outs[0])
        rounded = outs[1]
        gram = outs[-1]
        if not last:
            up, down, next_row, last_row = outs[2:-1]
    gathered = lax.all_to_all(gram, ("gx", "gy"), 0, 0, tiled=True)
    return pl.pallas_call(
        finish_kernel,
        name="finish",
        in_specs=[IN_VMEM] * 6,
        out_specs=[IN_HBM] * 2,
        out_shape=[full] * 2,
        scratch_shapes=[pltpu.VMEM((CAP, 8, ROWS), jnp.float32)] * 2
        + [pltpu.SemaphoreType.DMA((4, 2))],
        compiler_params=params(),
    )(gathered, *basis)


def solution(mesh):
    in_specs = (
        P(("gx", "gy"), None, None),
        P(("gx", "gy"), None, None),
        P(("gx", "gy"), None, None, None),
        P(("gx", "gy"), None),
        P(("gx", "gy"), None, None),
        P(("gx", "gy")),
    )
    out_specs = (P(("gx", "gy"), None, None), P(("gx", "gy"), None, None))
    return jax.shard_map(
        per_device, mesh=mesh, in_specs=in_specs, out_specs=out_specs, check_vma=False
    )
```

```python
import functools

import jax
import jax.numpy as jnp
from jax import lax
from jax.experimental import pallas as pl
from jax.experimental.pallas import tpu as pltpu
from jax.sharding import PartitionSpec as P

POWERS = 4
CAP = 64
SEND = 16
FACES = 4
SIDE = 16
GROUPS = SIDE * SIDE
ROWS = 128
LOOKUP = CAP + 9 * SEND
NOTHING = CAP + 4 * SEND
UNROLL = 16
BLOCKS = FACES + 1
QUARTER = CAP // 4
EIGHTH = CAP // 8

IN_VMEM = pl.BlockSpec(memory_space=pltpu.VMEM)
IN_SMEM = pl.BlockSpec(memory_space=pltpu.SMEM)
ANYWHERE = pl.BlockSpec(memory_space=pl.ANY)
IN_HBM = pl.BlockSpec(memory_space=pltpu.HBM)
UP_DIRECTIONS = (2, 5, 8)
DOWN_DIRECTIONS = (0, 3, 6)
LOCAL_RUNS = CAP
PLACES = 2 * CAP
SLOTS = PLACES + FACES * CAP
TABLE = SLOTS + 2 * CAP + 2 * SEND
PAIRS = [(a, b) for a in range(5) for b in range(a, 5) if b > 0]
PAIR_LANE = {pair: at for at, pair in enumerate(PAIRS)}
LANES_PER_SIDE = 16


def vector_shape(count, dtype):
    return jax.ShapeDtypeStruct((count, 8, ROWS), dtype)


def params(mebibytes=16):
    return pltpu.CompilerParams(vmem_limit_bytes=mebibytes << 20)


def pack(slot_of, rounded, up, down, next_row, last_row):
    for target, directions in (
        (up, UP_DIRECTIONS),
        (down, DOWN_DIRECTIONS),
        (next_row, (7,)),
        (last_row, (1,)),
    ):
        for at, direction in enumerate(directions):
            for k in range(SEND):
                target[at * SEND + k] = rounded[slot_of(direction, k)]


def listed(send_slots):
    return lambda direction, k: jnp.maximum(send_slots[direction, 0, k], 0)


def planned(table):
    return lambda direction, k: table[SLOTS + direction * SEND + k]


def start_kernel(
    neighbours_from, slots_from, counts, right_sides_from, basis, rounded, up, down,
    next_row, last_row, neighbours, send_slots, right_sides, arrived,
):
    vectors = pltpu.make_async_copy(right_sides_from, right_sides, arrived.at[2])
    tables = (
        pltpu.make_async_copy(slots_from, send_slots, arrived.at[0]),
        pltpu.make_async_copy(neighbours_from, neighbours, arrived.at[1]),
    )
    vectors.start()
    for copy in tables:
        copy.start()
    vectors.wait()
    element = lax.broadcasted_iota(jnp.int32, basis.shape, 0)
    live = jnp.where(element < counts[0], right_sides[...], 0.0)
    basis[...] = live
    rounded[...] = live.astype(jnp.bfloat16)
    for copy in tables:
        copy.wait()
    pack(listed(send_slots), rounded, up, down, next_row, last_row)


def plan_kernel(neighbours, send_slots, table, done):
    local = jnp.int32(0)
    for e in range(CAP):
        at = [neighbours[f, e] for f in range(FACES)]
        farthest = jnp.maximum(jnp.maximum(at[0], at[1]), jnp.maximum(at[2], at[3]))
        ghost = farthest >= CAP
        place = jnp.where(ghost, CAP - 1 - (e - local), local)
        table[place] = e
        for f in range(FACES):
            table[PLACES + f * CAP + place] = jnp.where(at[f] < 0, NOTHING, at[f])
        local = local + jnp.where(ghost, 0, 1)
    table[LOCAL_RUNS] = local // UNROLL
    for direction in range(9):
        for k in range(SEND):
            slot = listed(send_slots)(direction, k)
            table[SLOTS + direction * SEND + k] = slot
    done[...] = jnp.zeros_like(done)


def fetching(first, diag, face, diag_here, face_here, arrived):
    there = pl.ds(first, diag_here.shape[0])
    return (
        pltpu.make_async_copy(diag.at[there], diag_here, arrived.at[0]),
        pltpu.make_async_copy(face.at[there], face_here, arrived.at[1]),
    )


def transpose_some(first, diag_here, face_here, turned):
    def element(at, carry):
        e = first + at
        turned[e, 0:ROWS] = diag_here[at].T
        for f in range(FACES):
            turned[e, (f + 1) * ROWS : (f + 2) * ROWS] = face_here[at, f].T
        return carry

    lax.fori_loop(0, diag_here.shape[0], element, 0, unroll=8)


def fetch_parts(first, count, diag, face, diag_here, face_here, arrived):
    parts = []
    for at in range(0, count, EIGHTH):
        here = pl.ds(at, EIGHTH)
        place = diag_here.at[here], face_here.at[here]
        copies = fetching(first + at, diag, face, *place, arrived.at[at // EIGHTH])
        parts.append((first + at, place, copies))
        for copy in copies:
            copy.start()
    return parts


def first_half_kernel(
    diag, face, turned, diag_next, face_next, done, diag_here, face_here, arrived
):
    parts = fetch_parts(0, CAP // 2, diag, face, diag_here, face_here, arrived)
    ahead = fetching(CAP // 2, diag, face, diag_next, face_next, arrived.at[4])
    for copy in ahead:
        copy.start()
    for at, place, copies in parts:
        for copy in copies:
            copy.wait()
        transpose_some(at, *place, turned)
    done[...] = jnp.zeros_like(done)
    for copy in ahead:
        copy.wait()


def apply_as_is(e, vectors, diag_block, face_rows, image, image_rounded):
    out = lax.dot_general(
        jnp.concatenate(vectors, axis=1),
        jnp.concatenate([diag_block] + face_rows, axis=1),
        (((1,), (1,)), ((), ())),
        preferred_element_type=jnp.float32,
    )
    image[e] = out
    image_rounded[e] = out.astype(jnp.bfloat16)


def second_half_kernel(
    neighbours, diag, face, diag_next, face_next, rounded, image, image_rounded,
    diag_rest, face_rest, ghostly, arrived, lookup,
):
    first = CAP // 2
    parts = fetch_parts(
        first + EIGHTH, 3 * EIGHTH, diag, face, diag_rest, face_rest, arrived
    )
    fill_local(lookup, rounded)

    def apply_some(begin, diag_of, face_of):
        for at in range(EIGHTH):
            e = begin + at
            vectors = [lookup[e]]
            for f in range(FACES):
                near = neighbours[f, e]
                vectors.append(
                    lookup[jnp.where((near < 0) | (near >= CAP), NOTHING, near)]
                )
            rows = [face_of[at, f] for f in range(FACES)]
            apply_as_is(e, vectors, diag_of[at], rows, image, image_rounded)

    apply_some(first, diag_next, face_next)
    for run in (2, 3):
        farthest = jnp.int32(-1)
        for e in range(run * UNROLL, (run + 1) * UNROLL):
            for f in range(FACES):
                farthest = jnp.maximum(farthest, neighbours[f, e])
        ghostly[run] = farthest
    for begin, place, copies in parts:
        for copy in copies:
            copy.wait()
        apply_some(begin, *place)


def late_kernel(diag_next, face_next, diag_rest, face_rest, before, turned, done):
    transpose_some(CAP // 2, diag_next, face_next, turned)
    transpose_some(CAP // 2 + EIGHTH, diag_rest, face_rest, turned)
    done[...] = jnp.zeros_like(done)


def relay_kernel(*refs):
    from_down, from_up, next_row, last_row = refs[:4]
    send_next, send_last = refs[-2:]
    send_next[0:SEND] = from_up[2 * SEND : 3 * SEND]
    send_next[SEND : 2 * SEND] = next_row[...]
    send_next[2 * SEND : 3 * SEND] = from_down[2 * SEND : 3 * SEND]
    send_last[0:SEND] = from_up[0:SEND]
    send_last[SEND : 2 * SEND] = last_row[...]
    send_last[2 * SEND : 3 * SEND] = from_down[0:SEND]


def fill_local(lookup, rounded):
    lookup[0:CAP] = rounded[...]
    lookup[NOTHING : NOTHING + SEND] = jnp.zeros((SEND, 8, ROWS), jnp.bfloat16)


def fill_ghosts(lookup, from_down, from_up, from_last, from_next):
    lookup[CAP : CAP + 3 * SEND] = from_next[...]
    lookup[CAP + 3 * SEND : CAP + 4 * SEND] = from_up[SEND : 2 * SEND]
    lookup[CAP + 5 * SEND : CAP + 6 * SEND] = from_down[SEND : 2 * SEND]
    lookup[CAP + 6 * SEND : CAP + 9 * SEND] = from_last[...]


def apply_runs(first, limit, find, turned, lookup, basis, image, image_rounded):
    def near(found):
        vectors = jnp.concatenate([lookup[at] for at in found], axis=1)
        return vectors.astype(jnp.float32)

    def two(found, sums):
        elements = [places[0] for places in found]
        both = jnp.dot(
            jnp.concatenate([near(f) for f in found], axis=0).astype(jnp.bfloat16),
            jnp.concatenate([turned[e] for e in elements], axis=1),
            preferred_element_type=jnp.float32,
        )
        for at, e in enumerate(elements):
            out = both[8 * at : 8 * at + 8, ROWS * at : ROWS * at + ROWS]
            image[e] = out
            image_rounded[e] = out.astype(jnp.bfloat16)
            others = [ref[e] for ref in basis] + [out]
            sums = tuple(s + out * other for s, other in zip(sums, others))
        return sums

    def run(step, sums):
        for u in range(0, UNROLL, 2):
            at = step * UNROLL + u
            sums = two([find(at), find(at + 1)], sums)
        return sums

    zero = jnp.zeros((8, ROWS), jnp.float32)
    return lax.fori_loop(first, limit, run, (zero,) * (len(basis) + 1))


def with_sums(gram, sums):
    lane = lax.broadcasted_iota(jnp.int32, (8, ROWS), 1)
    newest = len(sums) - 1
    for a, s in enumerate(sums):
        total = jnp.sum(s, axis=1, keepdims=True)
        gram = gram + jnp.where(lane == PAIR_LANE[a, newest], total, 0.0)
    return gram


def whole_kernel(
    neighbours, send_slots, ghostly, turned, diag_next, face_next, diag_rest, face_rest,
    rounded, from_down, from_up, from_last, from_next, b0, before, before_rounded,
    image, image_rounded, up, down, next_row, last_row, gram_out, lookup,
):
    fill_local(lookup, rounded)
    fill_ghosts(lookup, from_down, from_up, from_last, from_next)

    def find(e):
        at = [neighbours[f, e] for f in range(FACES)]
        return [e] + [jnp.where(a < 0, NOTHING, a) for a in at]

    def again(run):
        for e in range(run * UNROLL, (run + 1) * UNROLL):
            at = e - CAP // 2
            diag_of, face_of = diag_next, face_next
            if at >= EIGHTH:
                at, diag_of, face_of = at - EIGHTH, diag_rest, face_rest
            vectors = [lookup[place] for place in find(e)]
            rows = [face_of[at, f] for f in range(FACES)]
            apply_as_is(e, vectors, diag_of[at], rows, image, image_rounded)

    apply_runs(0, 2, find, turned, lookup, (), image, image_rounded)
    for run in (2, 3):
        pl.when(ghostly[run] >= CAP)(functools.partial(again, run))
    pack(listed(send_slots), image_rounded, up, down, next_row, last_row)

    def products(step, sums):
        for u in range(UNROLL):
            out = image[step * UNROLL + u]
            sums = sums[0] + b0[step * UNROLL + u] * out, sums[1] + out * out
        return sums

    zero = jnp.zeros((8, ROWS), jnp.float32)
    sums = lax.fori_loop(0, CAP // UNROLL, products, (zero, zero))
    gram_out[...] = with_sums(zero, sums)


def find_in(table):
    return lambda at: [table[at]] + [table[PLACES + f * CAP + at] for f in range(FACES)]


def local_kernel(power, *refs):
    table, turned, rounded, gram_in = refs[:4]
    basis = refs[4 : 5 + power]
    image, image_rounded, gram_out, lookup = refs[5 + power :]
    fill_local(lookup, rounded)
    sums = apply_runs(
        0, table[LOCAL_RUNS], find_in(table), turned, lookup, basis, image, image_rounded
    )
    gram_out[...] = with_sums(gram_in[...], sums)


def ghost_kernel(power, *refs):
    table, turned, rounded = refs[:3]
    received = refs[3:7]
    gram_in = refs[7]
    basis = refs[8 : 9 + power]
    refs = refs[11 + power :]
    last = power == POWERS - 1
    if last:
        image, image_rounded, gram_out, lookup = refs
    else:
        image, image_rounded, up, down, next_row, last_row, gram_out, lookup = refs
    fill_local(lookup, rounded)
    fill_ghosts(lookup, *received)
    sums = apply_runs(
        table[LOCAL_RUNS], CAP // UNROLL, find_in(table), turned, lookup, basis, image,
        image_rounded,
    )
    if not last:
        pack(planned(table), image_rounded, up, down, next_row, last_row)
    gram = with_sums(gram_in[...], sums)
    if last:
        lane = lax.broadcasted_iota(jnp.int32, (8, ROWS), 1)
        side = lax.broadcasted_iota(jnp.int32, (8, ROWS), 0)
        spread = jnp.zeros((8, ROWS), jnp.float32)
        for at in range(len(PAIRS)):
            value = jnp.broadcast_to(gram[:, at : at + 1], (8, ROWS))
            spread = jnp.where(lane == side * LANES_PER_SIDE + at, value, spread)
        row = jnp.sum(spread, axis=0, keepdims=True)
        gram_out[...] = jnp.broadcast_to(row, gram_out.shape)
    else:
        gram_out[...] = gram


def finish_kernel(
    gram_rows, b0, b1, b2, b3, b4, solution_out, residual_out, solution, residual, left
):
    lane = lax.broadcasted_iota(jnp.int32, (8, ROWS), 1)
    side = lax.broadcasted_iota(jnp.int32, (8, ROWS), 0)
    row = jnp.sum(gram_rows[...], axis=0, keepdims=True)
    spread = jnp.broadcast_to(row, (8, ROWS))

    def entry(a, b):
        at = PAIR_LANE[min(a, b), max(a, b)]
        mine = jnp.where(lane == side * LANES_PER_SIDE + at, spread, 0.0)
        total = jnp.sum(mine, axis=1, keepdims=True)
        return jnp.broadcast_to(total, (8, ROWS))

    factor = {}
    inverse = []
    for i in range(POWERS):
        for j in range(i + 1):
            value = entry(i + 1, j + 1)
            for k in range(j):
                value = value - factor[i, k] * factor[j, k]
            if i == j:
                inverse.append(1.0 / jnp.sqrt(value))
            else:
                factor[i, j] = value * inverse[j]
    forward = []
    for i in range(POWERS):
        value = entry(0, i + 1)
        for k in range(i):
            value = value - factor[i, k] * forward[k]
        forward.append(value * inverse[i])
    weights = [None] * POWERS
    for i in reversed(range(POWERS)):
        value = forward[i]
        for k in range(i + 1, POWERS):
            value = value - factor[k, i] * weights[k]
        weights[i] = value * inverse[i]
    basis = (b0, b1, b2, b3, b4)

    def several(step, carry):
        for u in range(8):
            e = step * 8 + u
            v = [ref[e] for ref in basis]
            total = weights[0] * v[0]
            moved = weights[0] * v[1]
            for k in range(1, POWERS):
                total = total + weights[k] * v[k]
                moved = moved + weights[k] * v[k + 1]
            solution[e] = total
            residual[e] = v[0] - moved
        return carry

    leaving = []
    for part in range(4):
        lax.fori_loop(part * QUARTER // 8, (part + 1) * QUARTER // 8, several, 0)
        rows = pl.ds(part * QUARTER, QUARTER)
        for at, (here, there) in enumerate(
            ((solution, solution_out), (residual, residual_out))
        ):
            copy = pltpu.make_async_copy(here.at[rows], there.at[rows], left.at[part, at])
            copy.start()
            leaving.append(copy)
    for copy in leaving:
        copy.wait()


def shifted(block, axis, distance):
    return lax.ppermute(block, axis, [(i, (i + distance) % SIDE) for i in range(SIDE)])


def per_device(right_sides, diag_blocks, face_blocks, neighbours, send_slots, counts):
    half = jnp.bfloat16
    neighbours = neighbours.T
    send_slots = send_slots.transpose(1, 0, 2)
    in_place = lambda array: pltpu.with_memory_space_constraint(array, pltpu.HBM)
    diag_blocks = in_place(diag_blocks)
    face_blocks = in_place(face_blocks)
    packets = [vector_shape(n * SEND, half) for n in (3, 3, 1, 1)]
    full = vector_shape(CAP, jnp.float32)
    narrow = vector_shape(CAP, half)
    gram_shape = jax.ShapeDtypeStruct((8, ROWS), jnp.float32)
    rows_shape = jax.ShapeDtypeStruct((GROUPS, ROWS), jnp.float32)
    turned_shape = pltpu.VMEM((CAP, BLOCKS * ROWS, ROWS), half)
    lookup = pltpu.VMEM((LOOKUP, 8, ROWS), half)

    def room(count):
        return [
            pltpu.VMEM((count, ROWS, ROWS), half),
            pltpu.VMEM((count, FACES, ROWS, ROWS), half),
        ]

    *outs, neighbours, send_slots = pl.pallas_call(
        start_kernel,
        name="start",
        in_specs=[IN_HBM, IN_HBM, IN_SMEM, IN_HBM],
        out_specs=[IN_VMEM] * 6 + [IN_SMEM] * 2,
        out_shape=[full, narrow] + packets
        + [pltpu.SMEM(table.shape, jnp.int32) for table in (neighbours, send_slots)],
        scratch_shapes=[
            pltpu.VMEM(right_sides.shape, jnp.float32),
            pltpu.SemaphoreType.DMA((3,)),
        ],
        compiler_params=params(),
    )(in_place(neighbours), in_place(send_slots), counts, in_place(right_sides))
    first, rounded, up, down, next_row, last_row = outs
    basis = [first]
    gram = None
    for power in range(POWERS):
        last = power == POWERS - 1
        from_down = shifted(up, "gy", 1)
        from_up = shifted(down, "gy", -1)
        after = ()
        if power == 0:
            turned, *blocks, done = pl.pallas_call(
                first_half_kernel,
                name="first_half",
                in_specs=[IN_HBM] * 2,
                out_specs=[IN_VMEM] * 4,
                out_shape=[turned_shape] + room(EIGHTH) + [gram_shape],
                scratch_shapes=room(CAP // 2) + [pltpu.SemaphoreType.DMA((5, 2))],
                compiler_params=params(),
            )(diag_blocks, face_blocks)
            after = (done,)
        elif power == 1:
            table, done = pl.pallas_call(
                plan_kernel,
                name="plan",
                in_specs=[IN_SMEM] * 2,
                out_specs=[IN_SMEM, IN_VMEM],
                out_shape=[pltpu.SMEM((TABLE,), jnp.int32), gram_shape],
                compiler_params=params(),
            )(neighbours, send_slots)
            turned, turned_done = pl.pallas_call(
                late_kernel,
                name="late",
                in_specs=[IN_VMEM] * 5,
                out_specs=[IN_VMEM] * 2,
                out_shape=[turned_shape, gram_shape],
                input_output_aliases={4: 0},
                compiler_params=params(),
            )(*blocks, turned)
            after = (done, turned_done)
        if power > 0:
            image, image_rounded, gram = pl.pallas_call(
                functools.partial(local_kernel, power),
                name=f"local{power}",
                in_specs=[IN_SMEM] + [IN_VMEM] * (4 + power),
                out_specs=[IN_VMEM] * 3,
                out_shape=[full, narrow, gram_shape],
                scratch_shapes=[lookup],
                compiler_params=params(),
            )(table, turned, rounded, gram, *basis)
        send_next, send_last = pl.pallas_call(
            relay_kernel,
            name="relay",
            in_specs=[IN_VMEM] * 4 + [ANYWHERE] * len(after),
            out_specs=[IN_VMEM] * 2,
            out_shape=[vector_shape(3 * SEND, half)] * 2,
            compiler_params=params(),
        )(from_down, from_up, next_row, last_row, *after)
        from_last = shifted(send_next, "gx", 1)
        from_next = shifted(send_last, "gx", -1)
        received = (from_down, from_up, from_last, from_next)
        if power == 0:
            image, image_rounded, *rest, ghostly = pl.pallas_call(
                second_half_kernel,
                name="second_half",
                in_specs=[IN_SMEM] + [IN_HBM] * 2 + [IN_VMEM] * 3,
                out_specs=[IN_VMEM] * 4 + [IN_SMEM],
                out_shape=[full, narrow] + room(3 * EIGHTH)
                + [pltpu.SMEM((8,), jnp.int32)],
                scratch_shapes=[pltpu.SemaphoreType.DMA((3, 2)), lookup],
                compiler_params=params(),
            )(neighbours, diag_blocks, face_blocks, *blocks, rounded)
            blocks = blocks + rest
            outs = pl.pallas_call(
                whole_kernel,
                name="whole",
                in_specs=[IN_SMEM] * 3 + [IN_VMEM] * 13,
                out_specs=[IN_VMEM] * 7,
                out_shape=[full, narrow] + packets + [gram_shape],
                scratch_shapes=[lookup],
                input_output_aliases={14: 0, 15: 1},
                compiler_params=params(),
            )(
                neighbours, send_slots, ghostly, turned, *blocks, rounded, *received,
                first, image, image_rounded,
            )
        else:
            shapes = [full, narrow] + ([rows_shape] if last else packets + [gram_shape])
            outs = pl.pallas_call(
                functools.partial(ghost_kernel, power),
                name=f"ghost{power}",
                in_specs=[IN_SMEM] + [IN_VMEM] * (10 + power),
                out_specs=[IN_VMEM] * len(shapes),
                out_shape=shapes,
                scratch_shapes=[lookup],
                input_output_aliases={9 + power: 0, 10 + power: 1},
                compiler_params=params(),
            )(
                table, turned, rounded, *received, gram, *basis, image, image_rounded,
            )
        basis.append(outs[0])
        rounded = outs[1]
        gram = outs[-1]
        if not last:
            up, down, next_row, last_row = outs[2:-1]
    gathered = lax.all_to_all(gram, ("gx", "gy"), 0, 0, tiled=True)
    return pl.pallas_call(
        finish_kernel,
        name="finish",
        in_specs=[IN_VMEM] * 6,
        out_specs=[IN_HBM] * 2,
        out_shape=[full] * 2,
        scratch_shapes=[pltpu.VMEM((CAP, 8, ROWS), jnp.float32)] * 2
        + [pltpu.SemaphoreType.DMA((4, 2))],
        compiler_params=params(),
    )(gathered, *basis)


def solution(mesh):
    in_specs = (
        P(("gx", "gy"), None, None),
        P(("gx", "gy"), None, None),
        P(("gx", "gy"), None, None, None),
        P(("gx", "gy"), None),
        P(("gx", "gy"), None, None),
        P(("gx", "gy")),
    )
    out_specs = (P(("gx", "gy"), None, None), P(("gx", "gy"), None, None))
    return jax.shard_map(
        per_device, mesh=mesh, in_specs=in_specs, out_specs=out_specs, check_vma=False
    )
```

```python
import functools

import jax
import jax.numpy as jnp
from jax import lax
from jax.experimental import pallas as pl
from jax.experimental.pallas import tpu as pltpu
from jax.sharding import PartitionSpec as P

POWERS = 4
CAP = 64
SEND = 16
FACES = 4
SIDE = 16
GROUPS = SIDE * SIDE
ROWS = 128
LOOKUP = CAP + 9 * SEND
NOTHING = CAP + 4 * SEND
UNROLL = 16
BLOCKS = FACES + 1
QUARTER = CAP // 4
EIGHTH = CAP // 8

IN_VMEM = pl.BlockSpec(memory_space=pltpu.VMEM)
IN_SMEM = pl.BlockSpec(memory_space=pltpu.SMEM)
ANYWHERE = pl.BlockSpec(memory_space=pl.ANY)
IN_HBM = pl.BlockSpec(memory_space=pltpu.HBM)
UP_DIRECTIONS = (2, 5, 8)
DOWN_DIRECTIONS = (0, 3, 6)
LOCAL_RUNS = CAP
PLACES = 2 * CAP
SLOTS = PLACES + FACES * CAP
TABLE = SLOTS + 2 * CAP + 2 * SEND
PAIRS = [(a, b) for a in range(5) for b in range(a, 5) if b > 0]
PAIR_LANE = {pair: at for at, pair in enumerate(PAIRS)}
LANES_PER_SIDE = 16


def vector_shape(count, dtype):
    return jax.ShapeDtypeStruct((count, 8, ROWS), dtype)


def params(mebibytes=16):
    return pltpu.CompilerParams(vmem_limit_bytes=mebibytes << 20)


def pack(slot_of, rounded, up, down, next_row, last_row):
    for target, directions in (
        (up, UP_DIRECTIONS),
        (down, DOWN_DIRECTIONS),
        (next_row, (7,)),
        (last_row, (1,)),
    ):
        for at, direction in enumerate(directions):
            for k in range(SEND):
                target[at * SEND + k] = rounded[slot_of(direction, k)]


def listed(send_slots):
    return lambda direction, k: jnp.maximum(send_slots[direction, 0, k], 0)


def planned(table):
    return lambda direction, k: table[SLOTS + direction * SEND + k]


def start_kernel(
    neighbours_from, slots_from, counts, right_sides_from, basis, rounded, up, down,
    next_row, last_row, neighbours, send_slots, right_sides, arrived,
):
    vectors = pltpu.make_async_copy(right_sides_from, right_sides, arrived.at[2])
    tables = (
        pltpu.make_async_copy(slots_from, send_slots, arrived.at[0]),
        pltpu.make_async_copy(neighbours_from, neighbours, arrived.at[1]),
    )
    vectors.start()
    for copy in tables:
        copy.start()
    vectors.wait()
    element = lax.broadcasted_iota(jnp.int32, basis.shape, 0)
    live = jnp.where(element < counts[0], right_sides[...], 0.0)
    basis[...] = live
    rounded[...] = live.astype(jnp.bfloat16)
    for copy in tables:
        copy.wait()
    pack(listed(send_slots), rounded, up, down, next_row, last_row)


def plan_kernel(neighbours, send_slots, table, done):
    local = jnp.int32(0)
    for e in range(CAP):
        at = [neighbours[f, e] for f in range(FACES)]
        farthest = jnp.maximum(jnp.maximum(at[0], at[1]), jnp.maximum(at[2], at[3]))
        ghost = farthest >= CAP
        place = jnp.where(ghost, CAP - 1 - (e - local), local)
        table[place] = e
        for f in range(FACES):
            table[PLACES + f * CAP + place] = jnp.where(at[f] < 0, NOTHING, at[f])
        local = local + jnp.where(ghost, 0, 1)
    table[LOCAL_RUNS] = local // UNROLL
    for direction in range(9):
        for k in range(SEND):
            slot = listed(send_slots)(direction, k)
            table[SLOTS + direction * SEND + k] = slot
    done[...] = jnp.zeros_like(done)


def fetching(first, diag, face, diag_here, face_here, arrived):
    there = pl.ds(first, diag_here.shape[0])
    return (
        pltpu.make_async_copy(diag.at[there], diag_here, arrived.at[0]),
        pltpu.make_async_copy(face.at[there], face_here, arrived.at[1]),
    )


def transpose_some(first, diag_here, face_here, turned):
    def element(at, carry):
        e = first + at
        turned[e, 0:ROWS] = diag_here[at].T
        for f in range(FACES):
            turned[e, (f + 1) * ROWS : (f + 2) * ROWS] = face_here[at, f].T
        return carry

    lax.fori_loop(0, diag_here.shape[0], element, 0, unroll=8)


def fetch_parts(first, count, diag, face, diag_here, face_here, arrived):
    parts = []
    for at in range(0, count, EIGHTH):
        here = pl.ds(at, EIGHTH)
        place = diag_here.at[here], face_here.at[here]
        copies = fetching(first + at, diag, face, *place, arrived.at[at // EIGHTH])
        parts.append((first + at, place, copies))
        for copy in copies:
            copy.start()
    return parts


def first_half_kernel(diag, face, turned, done, diag_here, face_here, arrived):
    parts = fetch_parts(0, CAP // 2, diag, face, diag_here, face_here, arrived)
    for at, place, copies in parts:
        for copy in copies:
            copy.wait()
        transpose_some(at, *place, turned)
    done[...] = jnp.zeros_like(done)


def apply_as_is(e, vectors, diag_block, face_rows, image, image_rounded):
    out = lax.dot_general(
        jnp.concatenate(vectors, axis=1),
        jnp.concatenate([diag_block] + face_rows, axis=1),
        (((1,), (1,)), ((), ())),
        preferred_element_type=jnp.float32,
    )
    image[e] = out
    image_rounded[e] = out.astype(jnp.bfloat16)


def second_half_kernel(
    neighbours, diag, face, rounded, image, image_rounded, ghostly, lookup
):
    fill_local(lookup, rounded)
    for e in range(CAP // 2, CAP):
        vectors = [lookup[e]]
        for f in range(FACES):
            near = neighbours[f, e]
            vectors.append(
                lookup[jnp.where((near < 0) | (near >= CAP), NOTHING, near)]
            )
        rows = [face[e, f] for f in range(FACES)]
        apply_as_is(e, vectors, diag[e], rows, image, image_rounded)
    for run in (2, 3):
        farthest = jnp.int32(-1)
        for e in range(run * UNROLL, (run + 1) * UNROLL):
            for f in range(FACES):
                farthest = jnp.maximum(farthest, neighbours[f, e])
        ghostly[run] = farthest


def late_kernel(diag, face, before, turned, done):
    half = pl.ds(CAP // 2, CAP // 2)
    transpose_some(CAP // 2, diag.at[half], face.at[half], turned)
    done[...] = jnp.zeros_like(done)


def relay_kernel(*refs):
    from_down, from_up, next_row, last_row = refs[:4]
    send_next, send_last = refs[-2:]
    send_next[0:SEND] = from_up[2 * SEND : 3 * SEND]
    send_next[SEND : 2 * SEND] = next_row[...]
    send_next[2 * SEND : 3 * SEND] = from_down[2 * SEND : 3 * SEND]
    send_last[0:SEND] = from_up[0:SEND]
    send_last[SEND : 2 * SEND] = last_row[...]
    send_last[2 * SEND : 3 * SEND] = from_down[0:SEND]


def fill_local(lookup, rounded):
    lookup[0:CAP] = rounded[...]
    lookup[NOTHING : NOTHING + SEND] = jnp.zeros((SEND, 8, ROWS), jnp.bfloat16)


def fill_ghosts(lookup, from_down, from_up, from_last, from_next):
    lookup[CAP : CAP + 3 * SEND] = from_next[...]
    lookup[CAP + 3 * SEND : CAP + 4 * SEND] = from_up[SEND : 2 * SEND]
    lookup[CAP + 5 * SEND : CAP + 6 * SEND] = from_down[SEND : 2 * SEND]
    lookup[CAP + 6 * SEND : CAP + 9 * SEND] = from_last[...]


def apply_runs(first, limit, find, turned, lookup, basis, image, image_rounded):
    def near(found):
        vectors = jnp.concatenate([lookup[at] for at in found], axis=1)
        return vectors.astype(jnp.float32)

    def two(found, sums):
        elements = [places[0] for places in found]
        both = jnp.dot(
            jnp.concatenate([near(f) for f in found], axis=0).astype(jnp.bfloat16),
            jnp.concatenate([turned[e] for e in elements], axis=1),
            preferred_element_type=jnp.float32,
        )
        for at, e in enumerate(elements):
            out = both[8 * at : 8 * at + 8, ROWS * at : ROWS * at + ROWS]
            image[e] = out
            image_rounded[e] = out.astype(jnp.bfloat16)
            others = [ref[e] for ref in basis] + [out]
            sums = tuple(s + out * other for s, other in zip(sums, others))
        return sums

    def run(step, sums):
        for u in range(0, UNROLL, 2):
            at = step * UNROLL + u
            sums = two([find(at), find(at + 1)], sums)
        return sums

    zero = jnp.zeros((8, ROWS), jnp.float32)
    return lax.fori_loop(first, limit, run, (zero,) * (len(basis) + 1))


def with_sums(gram, sums):
    lane = lax.broadcasted_iota(jnp.int32, (8, ROWS), 1)
    newest = len(sums) - 1
    for a, s in enumerate(sums):
        total = jnp.sum(s, axis=1, keepdims=True)
        gram = gram + jnp.where(lane == PAIR_LANE[a, newest], total, 0.0)
    return gram


def whole_kernel(
    neighbours, send_slots, ghostly, turned, diag, face, rounded, from_down, from_up, from_last, from_next, b0, before, before_rounded,
    image, image_rounded, up, down, next_row, last_row, gram_out, lookup,
):
    fill_local(lookup, rounded)
    fill_ghosts(lookup, from_down, from_up, from_last, from_next)

    def find(e):
        at = [neighbours[f, e] for f in range(FACES)]
        return [e] + [jnp.where(a < 0, NOTHING, a) for a in at]

    def again(run):
        for e in range(run * UNROLL, (run + 1) * UNROLL):
            vectors = [lookup[place] for place in find(e)]
            rows = [face[e, f] for f in range(FACES)]
            apply_as_is(e, vectors, diag[e], rows, image, image_rounded)

    apply_runs(0, 2, find, turned, lookup, (), image, image_rounded)
    for run in (2, 3):
        pl.when(ghostly[run] >= CAP)(functools.partial(again, run))
    pack(listed(send_slots), image_rounded, up, down, next_row, last_row)

    def products(step, sums):
        for u in range(UNROLL):
            out = image[step * UNROLL + u]
            sums = sums[0] + b0[step * UNROLL + u] * out, sums[1] + out * out
        return sums

    zero = jnp.zeros((8, ROWS), jnp.float32)
    sums = lax.fori_loop(0, CAP // UNROLL, products, (zero, zero))
    gram_out[...] = with_sums(zero, sums)


def find_in(table):
    return lambda at: [table[at]] + [table[PLACES + f * CAP + at] for f in range(FACES)]


def local_kernel(power, *refs):
    table, turned, rounded, gram_in = refs[:4]
    basis = refs[4 : 5 + power]
    image, image_rounded, gram_out, lookup = refs[5 + power :]
    fill_local(lookup, rounded)
    sums = apply_runs(
        0, table[LOCAL_RUNS], find_in(table), turned, lookup, basis, image, image_rounded
    )
    gram_out[...] = with_sums(gram_in[...], sums)


def ghost_kernel(power, *refs):
    table, turned, rounded = refs[:3]
    received = refs[3:7]
    gram_in = refs[7]
    basis = refs[8 : 9 + power]
    refs = refs[11 + power :]
    last = power == POWERS - 1
    if last:
        image, image_rounded, gram_out, lookup = refs
    else:
        image, image_rounded, up, down, next_row, last_row, gram_out, lookup = refs
    fill_local(lookup, rounded)
    fill_ghosts(lookup, *received)
    sums = apply_runs(
        table[LOCAL_RUNS], CAP // UNROLL, find_in(table), turned, lookup, basis, image,
        image_rounded,
    )
    if not last:
        pack(planned(table), image_rounded, up, down, next_row, last_row)
    gram = with_sums(gram_in[...], sums)
    if last:
        lane = lax.broadcasted_iota(jnp.int32, (8, ROWS), 1)
        side = lax.broadcasted_iota(jnp.int32, (8, ROWS), 0)
        spread = jnp.zeros((8, ROWS), jnp.float32)
        for at in range(len(PAIRS)):
            value = jnp.broadcast_to(gram[:, at : at + 1], (8, ROWS))
            spread = jnp.where(lane == side * LANES_PER_SIDE + at, value, spread)
        row = jnp.sum(spread, axis=0, keepdims=True)
        gram_out[...] = jnp.broadcast_to(row, gram_out.shape)
    else:
        gram_out[...] = gram


def finish_kernel(
    gram_rows, b0, b1, b2, b3, b4, solution_out, residual_out, solution, residual, left
):
    lane = lax.broadcasted_iota(jnp.int32, (8, ROWS), 1)
    side = lax.broadcasted_iota(jnp.int32, (8, ROWS), 0)
    row = jnp.sum(gram_rows[...], axis=0, keepdims=True)
    spread = jnp.broadcast_to(row, (8, ROWS))

    def entry(a, b):
        at = PAIR_LANE[min(a, b), max(a, b)]
        mine = jnp.where(lane == side * LANES_PER_SIDE + at, spread, 0.0)
        total = jnp.sum(mine, axis=1, keepdims=True)
        return jnp.broadcast_to(total, (8, ROWS))

    factor = {}
    inverse = []
    for i in range(POWERS):
        for j in range(i + 1):
            value = entry(i + 1, j + 1)
            for k in range(j):
                value = value - factor[i, k] * factor[j, k]
            if i == j:
                inverse.append(1.0 / jnp.sqrt(value))
            else:
                factor[i, j] = value * inverse[j]
    forward = []
    for i in range(POWERS):
        value = entry(0, i + 1)
        for k in range(i):
            value = value - factor[i, k] * forward[k]
        forward.append(value * inverse[i])
    weights = [None] * POWERS
    for i in reversed(range(POWERS)):
        value = forward[i]
        for k in range(i + 1, POWERS):
            value = value - factor[k, i] * weights[k]
        weights[i] = value * inverse[i]
    basis = (b0, b1, b2, b3, b4)

    def several(step, carry):
        for u in range(8):
            e = step * 8 + u
            v = [ref[e] for ref in basis]
            total = weights[0] * v[0]
            moved = weights[0] * v[1]
            for k in range(1, POWERS):
                total = total + weights[k] * v[k]
                moved = moved + weights[k] * v[k + 1]
            solution[e] = total
            residual[e] = v[0] - moved
        return carry

    leaving = []
    for part in range(4):
        lax.fori_loop(part * QUARTER // 8, (part + 1) * QUARTER // 8, several, 0)
        rows = pl.ds(part * QUARTER, QUARTER)
        for at, (here, there) in enumerate(
            ((solution, solution_out), (residual, residual_out))
        ):
            copy = pltpu.make_async_copy(here.at[rows], there.at[rows], left.at[part, at])
            copy.start()
            leaving.append(copy)
    for copy in leaving:
        copy.wait()


def shifted(block, axis, distance):
    return lax.ppermute(block, axis, [(i, (i + distance) % SIDE) for i in range(SIDE)])


def per_device(right_sides, diag_blocks, face_blocks, neighbours, send_slots, counts):
    half = jnp.bfloat16
    neighbours = neighbours.T
    send_slots = send_slots.transpose(1, 0, 2)
    in_place = lambda array: pltpu.with_memory_space_constraint(array, pltpu.HBM)
    blocks = diag_blocks, face_blocks
    diag_blocks = in_place(diag_blocks)
    face_blocks = in_place(face_blocks)
    packets = [vector_shape(n * SEND, half) for n in (3, 3, 1, 1)]
    full = vector_shape(CAP, jnp.float32)
    narrow = vector_shape(CAP, half)
    gram_shape = jax.ShapeDtypeStruct((8, ROWS), jnp.float32)
    rows_shape = jax.ShapeDtypeStruct((GROUPS, ROWS), jnp.float32)
    turned_shape = pltpu.VMEM((CAP, BLOCKS * ROWS, ROWS), half)
    lookup = pltpu.VMEM((LOOKUP, 8, ROWS), half)

    def room(count):
        return [
            pltpu.VMEM((count, ROWS, ROWS), half),
            pltpu.VMEM((count, FACES, ROWS, ROWS), half),
        ]

    *outs, neighbours, send_slots = pl.pallas_call(
        start_kernel,
        name="start",
        in_specs=[IN_HBM, IN_HBM, IN_SMEM, IN_HBM],
        out_specs=[IN_VMEM] * 6 + [IN_SMEM] * 2,
        out_shape=[full, narrow] + packets
        + [pltpu.SMEM(table.shape, jnp.int32) for table in (neighbours, send_slots)],
        scratch_shapes=[
            pltpu.VMEM(right_sides.shape, jnp.float32),
            pltpu.SemaphoreType.DMA((3,)),
        ],
        compiler_params=params(),
    )(in_place(neighbours), in_place(send_slots), counts, in_place(right_sides))
    first, rounded, up, down, next_row, last_row = outs
    basis = [first]
    gram = None
    for power in range(POWERS):
        last = power == POWERS - 1
        from_down = shifted(up, "gy", 1)
        from_up = shifted(down, "gy", -1)
        after = ()
        if power == 0:
            turned, done = pl.pallas_call(
                first_half_kernel,
                name="first_half",
                in_specs=[IN_HBM] * 2,
                out_specs=[IN_VMEM] * 2,
                out_shape=[turned_shape, gram_shape],
                scratch_shapes=room(CAP // 2) + [pltpu.SemaphoreType.DMA((4, 2))],
                compiler_params=params(),
            )(diag_blocks, face_blocks)
            after = (done,)
        elif power == 1:
            table, done = pl.pallas_call(
                plan_kernel,
                name="plan",
                in_specs=[IN_SMEM] * 2,
                out_specs=[IN_SMEM, IN_VMEM],
                out_shape=[pltpu.SMEM((TABLE,), jnp.int32), gram_shape],
                compiler_params=params(),
            )(neighbours, send_slots)
            turned, turned_done = pl.pallas_call(
                late_kernel,
                name="late",
                in_specs=[IN_VMEM] * 3,
                out_specs=[IN_VMEM] * 2,
                out_shape=[turned_shape, gram_shape],
                input_output_aliases={2: 0},
                compiler_params=params(),
            )(*blocks, turned)
            after = (done, turned_done)
        if power > 0:
            image, image_rounded, gram = pl.pallas_call(
                functools.partial(local_kernel, power),
                name=f"local{power}",
                in_specs=[IN_SMEM] + [IN_VMEM] * (4 + power),
                out_specs=[IN_VMEM] * 3,
                out_shape=[full, narrow, gram_shape],
                scratch_shapes=[lookup],
                compiler_params=params(),
            )(table, turned, rounded, gram, *basis)
        send_next, send_last = pl.pallas_call(
            relay_kernel,
            name="relay",
            in_specs=[IN_VMEM] * 4 + [ANYWHERE] * len(after),
            out_specs=[IN_VMEM] * 2,
            out_shape=[vector_shape(3 * SEND, half)] * 2,
            compiler_params=params(),
        )(from_down, from_up, next_row, last_row, *after)
        from_last = shifted(send_next, "gx", 1)
        from_next = shifted(send_last, "gx", -1)
        received = (from_down, from_up, from_last, from_next)
        if power == 0:
            image, image_rounded, ghostly = pl.pallas_call(
                second_half_kernel,
                name="second_half",
                in_specs=[IN_SMEM] + [IN_VMEM] * 3,
                out_specs=[IN_VMEM] * 2 + [IN_SMEM],
                out_shape=[full, narrow, pltpu.SMEM((8,), jnp.int32)],
                scratch_shapes=[lookup],
                compiler_params=params(),
            )(neighbours, *blocks, rounded)
            outs = pl.pallas_call(
                whole_kernel,
                name="whole",
                in_specs=[IN_SMEM] * 3 + [IN_VMEM] * 11,
                out_specs=[IN_VMEM] * 7,
                out_shape=[full, narrow] + packets + [gram_shape],
                scratch_shapes=[lookup],
                input_output_aliases={12: 0, 13: 1},
                compiler_params=params(),
            )(
                neighbours, send_slots, ghostly, turned, *blocks, rounded, *received,
                first, image, image_rounded,
            )
        else:
            shapes = [full, narrow] + ([rows_shape] if last else packets + [gram_shape])
            outs = pl.pallas_call(
                functools.partial(ghost_kernel, power),
                name=f"ghost{power}",
                in_specs=[IN_SMEM] + [IN_VMEM] * (10 + power),
                out_specs=[IN_VMEM] * len(shapes),
                out_shape=shapes,
                scratch_shapes=[lookup],
                input_output_aliases={9 + power: 0, 10 + power: 1},
                compiler_params=params(),
            )(
                table, turned, rounded, *received, gram, *basis, image, image_rounded,
            )
        basis.append(outs[0])
        rounded = outs[1]
        gram = outs[-1]
        if not last:
            up, down, next_row, last_row = outs[2:-1]
    gathered = lax.all_to_all(gram, ("gx", "gy"), 0, 0, tiled=True)
    return pl.pallas_call(
        finish_kernel,
        name="finish",
        in_specs=[IN_VMEM] * 6,
        out_specs=[IN_HBM] * 2,
        out_shape=[full] * 2,
        scratch_shapes=[pltpu.VMEM((CAP, 8, ROWS), jnp.float32)] * 2
        + [pltpu.SemaphoreType.DMA((4, 2))],
        compiler_params=params(),
    )(gathered, *basis)


def solution(mesh):
    in_specs = (
        P(("gx", "gy"), None, None),
        P(("gx", "gy"), None, None),
        P(("gx", "gy"), None, None, None),
        P(("gx", "gy"), None),
        P(("gx", "gy"), None, None),
        P(("gx", "gy")),
    )
    out_specs = (P(("gx", "gy"), None, None), P(("gx", "gy"), None, None))
    return jax.shard_map(
        per_device, mesh=mesh, in_specs=in_specs, out_specs=out_specs, check_vma=False
    )
```

```python
import functools

import jax
import jax.numpy as jnp
from jax import lax
from jax.experimental import pallas as pl
from jax.experimental.pallas import tpu as pltpu
from jax.sharding import PartitionSpec as P

POWERS = 4
CAP = 64
SEND = 16
FACES = 4
SIDE = 16
GROUPS = SIDE * SIDE
ROWS = 128
LOOKUP = CAP + 9 * SEND
NOTHING = CAP + 4 * SEND
UNROLL = 32
RUN = 16
BLOCKS = FACES + 1
QUARTER = CAP // 4
EIGHTH = CAP // 8

IN_VMEM = pl.BlockSpec(memory_space=pltpu.VMEM)
IN_SMEM = pl.BlockSpec(memory_space=pltpu.SMEM)
ANYWHERE = pl.BlockSpec(memory_space=pl.ANY)
IN_HBM = pl.BlockSpec(memory_space=pltpu.HBM)
UP_DIRECTIONS = (2, 5, 8)
DOWN_DIRECTIONS = (0, 3, 6)
LOCAL_RUNS = CAP
PLACES = 2 * CAP
SLOTS = PLACES + FACES * CAP
TABLE = SLOTS + 2 * CAP + 2 * SEND
PAIRS = [(a, b) for a in range(5) for b in range(a, 5) if b > 0]
PAIR_LANE = {pair: at for at, pair in enumerate(PAIRS)}
LANES_PER_SIDE = 16


def vector_shape(count, dtype):
    return jax.ShapeDtypeStruct((count, 8, ROWS), dtype)


def params(mebibytes=16):
    return pltpu.CompilerParams(vmem_limit_bytes=mebibytes << 20)


def pack(slot_of, rounded, up, down, next_row, last_row):
    for target, directions in (
        (up, UP_DIRECTIONS),
        (down, DOWN_DIRECTIONS),
        (next_row, (7,)),
        (last_row, (1,)),
    ):
        for at, direction in enumerate(directions):
            for k in range(SEND):
                target[at * SEND + k] = rounded[slot_of(direction, k)]


def listed(send_slots):
    return lambda direction, k: jnp.maximum(send_slots[direction, 0, k], 0)


def planned(table):
    return lambda direction, k: table[SLOTS + direction * SEND + k]


def start_kernel(
    neighbours_from, slots_from, counts, right_sides_from, basis, rounded, up, down,
    next_row, last_row, neighbours, send_slots, right_sides, arrived,
):
    vectors = pltpu.make_async_copy(right_sides_from, right_sides, arrived.at[2])
    tables = (
        pltpu.make_async_copy(slots_from, send_slots, arrived.at[0]),
        pltpu.make_async_copy(neighbours_from, neighbours, arrived.at[1]),
    )
    vectors.start()
    for copy in tables:
        copy.start()
    vectors.wait()
    element = lax.broadcasted_iota(jnp.int32, basis.shape, 0)
    live = jnp.where(element < counts[0], right_sides[...], 0.0)
    basis[...] = live
    rounded[...] = live.astype(jnp.bfloat16)
    for copy in tables:
        copy.wait()
    pack(listed(send_slots), rounded, up, down, next_row, last_row)


def plan_kernel(neighbours, send_slots, table, done):
    local = jnp.int32(0)
    for e in range(CAP):
        at = [neighbours[f, e] for f in range(FACES)]
        farthest = jnp.maximum(jnp.maximum(at[0], at[1]), jnp.maximum(at[2], at[3]))
        ghost = farthest >= CAP
        place = jnp.where(ghost, CAP - 1 - (e - local), local)
        table[place] = e
        for f in range(FACES):
            table[PLACES + f * CAP + place] = jnp.where(at[f] < 0, NOTHING, at[f])
        local = local + jnp.where(ghost, 0, 1)
    table[LOCAL_RUNS] = local // UNROLL
    for direction in range(9):
        for k in range(SEND):
            slot = listed(send_slots)(direction, k)
            table[SLOTS + direction * SEND + k] = slot
    done[...] = jnp.zeros_like(done)


def fetching(first, diag, face, diag_here, face_here, arrived):
    there = pl.ds(first, diag_here.shape[0])
    return (
        pltpu.make_async_copy(diag.at[there], diag_here, arrived.at[0]),
        pltpu.make_async_copy(face.at[there], face_here, arrived.at[1]),
    )


def transpose_some(first, diag_here, face_here, turned):
    def element(at, carry):
        e = first + at
        turned[e, 0:ROWS] = diag_here[at].T
        for f in range(FACES):
            turned[e, (f + 1) * ROWS : (f + 2) * ROWS] = face_here[at, f].T
        return carry

    lax.fori_loop(0, diag_here.shape[0], element, 0, unroll=8)


def fetch_parts(first, count, diag, face, diag_here, face_here, arrived):
    parts = []
    for at in range(0, count, EIGHTH):
        here = pl.ds(at, EIGHTH)
        place = diag_here.at[here], face_here.at[here]
        copies = fetching(first + at, diag, face, *place, arrived.at[at // EIGHTH])
        parts.append((first + at, place, copies))
        for copy in copies:
            copy.start()
    return parts


def first_half_kernel(diag, face, turned, done, diag_here, face_here, arrived):
    parts = fetch_parts(0, CAP // 2, diag, face, diag_here, face_here, arrived)
    for at, place, copies in parts:
        for copy in copies:
            copy.wait()
        transpose_some(at, *place, turned)
    done[...] = jnp.zeros_like(done)


def apply_as_is(e, vectors, diag_block, face_rows, image, image_rounded):
    out = lax.dot_general(
        jnp.concatenate(vectors, axis=1),
        jnp.concatenate([diag_block] + face_rows, axis=1),
        (((1,), (1,)), ((), ())),
        preferred_element_type=jnp.float32,
    )
    image[e] = out
    image_rounded[e] = out.astype(jnp.bfloat16)


def second_half_kernel(
    neighbours, diag, face, rounded, image, image_rounded, ghostly, lookup
):
    fill_local(lookup, rounded)
    for e in range(CAP // 2, CAP):
        vectors = [lookup[e]]
        for f in range(FACES):
            near = neighbours[f, e]
            vectors.append(
                lookup[jnp.where((near < 0) | (near >= CAP), NOTHING, near)]
            )
        rows = [face[e, f] for f in range(FACES)]
        apply_as_is(e, vectors, diag[e], rows, image, image_rounded)
    for run in (2, 3):
        farthest = jnp.int32(-1)
        for e in range(run * RUN, (run + 1) * RUN):
            for f in range(FACES):
                farthest = jnp.maximum(farthest, neighbours[f, e])
        ghostly[run] = farthest


def late_kernel(diag, face, before, turned, done):
    half = pl.ds(CAP // 2, CAP // 2)
    transpose_some(CAP // 2, diag.at[half], face.at[half], turned)
    done[...] = jnp.zeros_like(done)


def relay_kernel(*refs):
    from_down, from_up, next_row, last_row = refs[:4]
    send_next, send_last = refs[-2:]
    send_next[0:SEND] = from_up[2 * SEND : 3 * SEND]
    send_next[SEND : 2 * SEND] = next_row[...]
    send_next[2 * SEND : 3 * SEND] = from_down[2 * SEND : 3 * SEND]
    send_last[0:SEND] = from_up[0:SEND]
    send_last[SEND : 2 * SEND] = last_row[...]
    send_last[2 * SEND : 3 * SEND] = from_down[0:SEND]


def fill_local(lookup, rounded):
    lookup[0:CAP] = rounded[...]
    lookup[NOTHING : NOTHING + SEND] = jnp.zeros((SEND, 8, ROWS), jnp.bfloat16)


def fill_ghosts(lookup, from_down, from_up, from_last, from_next):
    lookup[CAP : CAP + 3 * SEND] = from_next[...]
    lookup[CAP + 3 * SEND : CAP + 4 * SEND] = from_up[SEND : 2 * SEND]
    lookup[CAP + 5 * SEND : CAP + 6 * SEND] = from_down[SEND : 2 * SEND]
    lookup[CAP + 6 * SEND : CAP + 9 * SEND] = from_last[...]


def apply_runs(first, limit, find, turned, lookup, basis, image, image_rounded):
    def near(found):
        vectors = jnp.concatenate([lookup[at] for at in found], axis=1)
        return vectors.astype(jnp.float32)

    def two(found, sums):
        elements = [places[0] for places in found]
        both = jnp.dot(
            jnp.concatenate([near(f) for f in found], axis=0).astype(jnp.bfloat16),
            jnp.concatenate([turned[e] for e in elements], axis=1),
            preferred_element_type=jnp.float32,
        )
        for at, e in enumerate(elements):
            out = both[8 * at : 8 * at + 8, ROWS * at : ROWS * at + ROWS]
            image[e] = out
            image_rounded[e] = out.astype(jnp.bfloat16)
            others = [ref[e] for ref in basis] + [out]
            sums = tuple(s + out * other for s, other in zip(sums, others))
        return sums

    def run(step, sums):
        for u in range(0, UNROLL, 2):
            at = step * UNROLL + u
            sums = two([find(at), find(at + 1)], sums)
        return sums

    zero = jnp.zeros((8, ROWS), jnp.float32)
    return lax.fori_loop(first, limit, run, (zero,) * (len(basis) + 1))


def with_sums(gram, sums):
    lane = lax.broadcasted_iota(jnp.int32, (8, ROWS), 1)
    newest = len(sums) - 1
    for a, s in enumerate(sums):
        total = jnp.sum(s, axis=1, keepdims=True)
        gram = gram + jnp.where(lane == PAIR_LANE[a, newest], total, 0.0)
    return gram


def whole_kernel(
    neighbours, send_slots, ghostly, turned, diag, face, rounded, from_down, from_up, from_last, from_next, b0, before, before_rounded,
    image, image_rounded, up, down, next_row, last_row, gram_out, lookup,
):
    fill_local(lookup, rounded)
    fill_ghosts(lookup, from_down, from_up, from_last, from_next)

    def find(e):
        at = [neighbours[f, e] for f in range(FACES)]
        return [e] + [jnp.where(a < 0, NOTHING, a) for a in at]

    def again(run):
        for e in range(run * RUN, (run + 1) * RUN):
            vectors = [lookup[place] for place in find(e)]
            rows = [face[e, f] for f in range(FACES)]
            apply_as_is(e, vectors, diag[e], rows, image, image_rounded)

    apply_runs(0, CAP // 2 // UNROLL, find, turned, lookup, (), image, image_rounded)
    for run in (2, 3):
        pl.when(ghostly[run] >= CAP)(functools.partial(again, run))
    pack(listed(send_slots), image_rounded, up, down, next_row, last_row)

    def products(step, sums):
        for u in range(UNROLL):
            out = image[step * UNROLL + u]
            sums = sums[0] + b0[step * UNROLL + u] * out, sums[1] + out * out
        return sums

    zero = jnp.zeros((8, ROWS), jnp.float32)
    sums = lax.fori_loop(0, CAP // UNROLL, products, (zero, zero))
    gram_out[...] = with_sums(zero, sums)


def find_in(table):
    return lambda at: [table[at]] + [table[PLACES + f * CAP + at] for f in range(FACES)]


def local_kernel(power, *refs):
    table, turned, rounded, gram_in = refs[:4]
    basis = refs[4 : 5 + power]
    image, image_rounded, gram_out, lookup = refs[5 + power :]
    fill_local(lookup, rounded)
    sums = apply_runs(
        0, table[LOCAL_RUNS], find_in(table), turned, lookup, basis, image, image_rounded
    )
    gram_out[...] = with_sums(gram_in[...], sums)


def ghost_kernel(power, *refs):
    table, turned, rounded = refs[:3]
    received = refs[3:7]
    gram_in = refs[7]
    basis = refs[8 : 9 + power]
    refs = refs[11 + power :]
    last = power == POWERS - 1
    if last:
        image, image_rounded, gram_out, lookup = refs
    else:
        image, image_rounded, up, down, next_row, last_row, gram_out, lookup = refs
    fill_local(lookup, rounded)
    fill_ghosts(lookup, *received)
    sums = apply_runs(
        table[LOCAL_RUNS], CAP // UNROLL, find_in(table), turned, lookup, basis, image,
        image_rounded,
    )
    if not last:
        pack(planned(table), image_rounded, up, down, next_row, last_row)
    gram = with_sums(gram_in[...], sums)
    if last:
        lane = lax.broadcasted_iota(jnp.int32, (8, ROWS), 1)
        side = lax.broadcasted_iota(jnp.int32, (8, ROWS), 0)
        spread = jnp.zeros((8, ROWS), jnp.float32)
        for at in range(len(PAIRS)):
            value = jnp.broadcast_to(gram[:, at : at + 1], (8, ROWS))
            spread = jnp.where(lane == side * LANES_PER_SIDE + at, value, spread)
        row = jnp.sum(spread, axis=0, keepdims=True)
        gram_out[...] = jnp.broadcast_to(row, gram_out.shape)
    else:
        gram_out[...] = gram


def finish_kernel(
    gram_rows, b0, b1, b2, b3, b4, solution_out, residual_out, solution, residual, left
):
    lane = lax.broadcasted_iota(jnp.int32, (8, ROWS), 1)
    side = lax.broadcasted_iota(jnp.int32, (8, ROWS), 0)
    row = jnp.sum(gram_rows[...], axis=0, keepdims=True)
    spread = jnp.broadcast_to(row, (8, ROWS))

    def entry(a, b):
        at = PAIR_LANE[min(a, b), max(a, b)]
        mine = jnp.where(lane == side * LANES_PER_SIDE + at, spread, 0.0)
        total = jnp.sum(mine, axis=1, keepdims=True)
        return jnp.broadcast_to(total, (8, ROWS))

    factor = {}
    inverse = []
    for i in range(POWERS):
        for j in range(i + 1):
            value = entry(i + 1, j + 1)
            for k in range(j):
                value = value - factor[i, k] * factor[j, k]
            if i == j:
                inverse.append(1.0 / jnp.sqrt(value))
            else:
                factor[i, j] = value * inverse[j]
    forward = []
    for i in range(POWERS):
        value = entry(0, i + 1)
        for k in range(i):
            value = value - factor[i, k] * forward[k]
        forward.append(value * inverse[i])
    weights = [None] * POWERS
    for i in reversed(range(POWERS)):
        value = forward[i]
        for k in range(i + 1, POWERS):
            value = value - factor[k, i] * weights[k]
        weights[i] = value * inverse[i]
    basis = (b0, b1, b2, b3, b4)

    def several(step, carry):
        for u in range(8):
            e = step * 8 + u
            v = [ref[e] for ref in basis]
            total = weights[0] * v[0]
            moved = weights[0] * v[1]
            for k in range(1, POWERS):
                total = total + weights[k] * v[k]
                moved = moved + weights[k] * v[k + 1]
            solution[e] = total
            residual[e] = v[0] - moved
        return carry

    leaving = []
    for part in range(4):
        lax.fori_loop(part * QUARTER // 8, (part + 1) * QUARTER // 8, several, 0)
        rows = pl.ds(part * QUARTER, QUARTER)
        for at, (here, there) in enumerate(
            ((solution, solution_out), (residual, residual_out))
        ):
            copy = pltpu.make_async_copy(here.at[rows], there.at[rows], left.at[part, at])
            copy.start()
            leaving.append(copy)
    for copy in leaving:
        copy.wait()


def shifted(block, axis, distance):
    return lax.ppermute(block, axis, [(i, (i + distance) % SIDE) for i in range(SIDE)])


def per_device(right_sides, diag_blocks, face_blocks, neighbours, send_slots, counts):
    half = jnp.bfloat16
    neighbours = neighbours.T
    send_slots = send_slots.transpose(1, 0, 2)
    in_place = lambda array: pltpu.with_memory_space_constraint(array, pltpu.HBM)
    blocks = diag_blocks, face_blocks
    diag_blocks = in_place(diag_blocks)
    face_blocks = in_place(face_blocks)
    packets = [vector_shape(n * SEND, half) for n in (3, 3, 1, 1)]
    full = vector_shape(CAP, jnp.float32)
    narrow = vector_shape(CAP, half)
    gram_shape = jax.ShapeDtypeStruct((8, ROWS), jnp.float32)
    rows_shape = jax.ShapeDtypeStruct((GROUPS, ROWS), jnp.float32)
    turned_shape = pltpu.VMEM((CAP, BLOCKS * ROWS, ROWS), half)
    lookup = pltpu.VMEM((LOOKUP, 8, ROWS), half)

    def room(count):
        return [
            pltpu.VMEM((count, ROWS, ROWS), half),
            pltpu.VMEM((count, FACES, ROWS, ROWS), half),
        ]

    *outs, neighbours, send_slots = pl.pallas_call(
        start_kernel,
        name="start",
        in_specs=[IN_HBM, IN_HBM, IN_SMEM, IN_HBM],
        out_specs=[IN_VMEM] * 6 + [IN_SMEM] * 2,
        out_shape=[full, narrow] + packets
        + [pltpu.SMEM(table.shape, jnp.int32) for table in (neighbours, send_slots)],
        scratch_shapes=[
            pltpu.VMEM(right_sides.shape, jnp.float32),
            pltpu.SemaphoreType.DMA((3,)),
        ],
        compiler_params=params(),
    )(in_place(neighbours), in_place(send_slots), counts, in_place(right_sides))
    first, rounded, up, down, next_row, last_row = outs
    basis = [first]
    gram = None
    for power in range(POWERS):
        last = power == POWERS - 1
        from_down = shifted(up, "gy", 1)
        from_up = shifted(down, "gy", -1)
        after = ()
        if power == 0:
            turned, done = pl.pallas_call(
                first_half_kernel,
                name="first_half",
                in_specs=[IN_HBM] * 2,
                out_specs=[IN_VMEM] * 2,
                out_shape=[turned_shape, gram_shape],
                scratch_shapes=room(CAP // 2) + [pltpu.SemaphoreType.DMA((4, 2))],
                compiler_params=params(),
            )(diag_blocks, face_blocks)
            after = (done,)
        elif power == 1:
            table, done = pl.pallas_call(
                plan_kernel,
                name="plan",
                in_specs=[IN_SMEM] * 2,
                out_specs=[IN_SMEM, IN_VMEM],
                out_shape=[pltpu.SMEM((TABLE,), jnp.int32), gram_shape],
                compiler_params=params(),
            )(neighbours, send_slots)
            turned, turned_done = pl.pallas_call(
                late_kernel,
                name="late",
                in_specs=[IN_VMEM] * 3,
                out_specs=[IN_VMEM] * 2,
                out_shape=[turned_shape, gram_shape],
                input_output_aliases={2: 0},
                compiler_params=params(),
            )(*blocks, turned)
            after = (done, turned_done)
        if power > 0:
            image, image_rounded, gram = pl.pallas_call(
                functools.partial(local_kernel, power),
                name=f"local{power}",
                in_specs=[IN_SMEM] + [IN_VMEM] * (4 + power),
                out_specs=[IN_VMEM] * 3,
                out_shape=[full, narrow, gram_shape],
                scratch_shapes=[lookup],
                compiler_params=params(),
            )(table, turned, rounded, gram, *basis)
        send_next, send_last = pl.pallas_call(
            relay_kernel,
            name="relay",
            in_specs=[IN_VMEM] * 4 + [ANYWHERE] * len(after),
            out_specs=[IN_VMEM] * 2,
            out_shape=[vector_shape(3 * SEND, half)] * 2,
            compiler_params=params(),
        )(from_down, from_up, next_row, last_row, *after)
        from_last = shifted(send_next, "gx", 1)
        from_next = shifted(send_last, "gx", -1)
        received = (from_down, from_up, from_last, from_next)
        if power == 0:
            image, image_rounded, ghostly = pl.pallas_call(
                second_half_kernel,
                name="second_half",
                in_specs=[IN_SMEM] + [IN_VMEM] * 3,
                out_specs=[IN_VMEM] * 2 + [IN_SMEM],
                out_shape=[full, narrow, pltpu.SMEM((8,), jnp.int32)],
                scratch_shapes=[lookup],
                compiler_params=params(),
            )(neighbours, *blocks, rounded)
            outs = pl.pallas_call(
                whole_kernel,
                name="whole",
                in_specs=[IN_SMEM] * 3 + [IN_VMEM] * 11,
                out_specs=[IN_VMEM] * 7,
                out_shape=[full, narrow] + packets + [gram_shape],
                scratch_shapes=[lookup],
                input_output_aliases={12: 0, 13: 1},
                compiler_params=params(),
            )(
                neighbours, send_slots, ghostly, turned, *blocks, rounded, *received,
                first, image, image_rounded,
            )
        else:
            shapes = [full, narrow] + ([rows_shape] if last else packets + [gram_shape])
            outs = pl.pallas_call(
                functools.partial(ghost_kernel, power),
                name=f"ghost{power}",
                in_specs=[IN_SMEM] + [IN_VMEM] * (10 + power),
                out_specs=[IN_VMEM] * len(shapes),
                out_shape=shapes,
                scratch_shapes=[lookup],
                input_output_aliases={9 + power: 0, 10 + power: 1},
                compiler_params=params(),
            )(
                table, turned, rounded, *received, gram, *basis, image, image_rounded,
            )
        basis.append(outs[0])
        rounded = outs[1]
        gram = outs[-1]
        if not last:
            up, down, next_row, last_row = outs[2:-1]
    gathered = lax.all_to_all(gram, ("gx", "gy"), 0, 0, tiled=True)
    return pl.pallas_call(
        finish_kernel,
        name="finish",
        in_specs=[IN_VMEM] * 6,
        out_specs=[IN_HBM] * 2,
        out_shape=[full] * 2,
        scratch_shapes=[pltpu.VMEM((CAP, 8, ROWS), jnp.float32)] * 2
        + [pltpu.SemaphoreType.DMA((4, 2))],
        compiler_params=params(),
    )(gathered, *basis)


def solution(mesh):
    in_specs = (
        P(("gx", "gy"), None, None),
        P(("gx", "gy"), None, None),
        P(("gx", "gy"), None, None, None),
        P(("gx", "gy"), None),
        P(("gx", "gy"), None, None),
        P(("gx", "gy")),
    )
    out_specs = (P(("gx", "gy"), None, None), P(("gx", "gy"), None, None))
    return jax.shard_map(
        per_device, mesh=mesh, in_specs=in_specs, out_specs=out_specs, check_vma=False
    )
```
